128 devices in a mesh: db: 16 (over z, y), rack: 8 (over x, core).
Axes of the slice: x: 4, y: 4, z: 4, core: 2. Of those that a mesh axis runs over, the one named last changes fastest.
Arguments:
- queries: bfloat16 [8192, 8192], P('db', 'rack'), may hold values from -10 to 10
- cotangent: bfloat16 [8192, 8192], P('db', 'rack'), may hold values from -6 to 6
- database: bfloat16 [512, 128, 896], P('db'), may hold values from -6 to 6
- w_key: bfloat16 [896, 8192], P(None, 'rack'), may hold values from -0.20044593 to 0.20044593
- w_value: bfloat16 [896, 8192], P(None, 'rack'), may hold values from -0.1875 to 0.1875
- neighbour_owner: int32 [128, 2], P('db'), may hold values from 0 to 15, all different within a row; in each aligned block of 8 rows (0 to 7, 8 to 15, ...) at most 3 rows name the same one
- neighbour_slot: int32 [128, 2], P('db'), may hold values from 0 to 31
Outputs:
- attended: bfloat16 [8192, 8192], P('db', 'rack')
- grad_queries: bfloat16 [8192, 8192], P('db', 'rack')
- grad_w_key: float32 [896, 8192], P(None, 'rack')
- grad_w_value: float32 [896, 8192], P(None, 'rack')
- grad_database: bfloat16 [512, 128, 896], P('db', 'rack')
The draws below stay inside these ranges and needn't reach their ends.
Inputs may be any that keep to these rules, and one draw needn't show every extreme that they name: `neighbour_owner`: the 2 owners of one span differ. Among the spans of one db index, no owner is named by more than 3 spans, a bound that some block reaches.
All inputs are finite; a program needn't handle non-finite values.
Results may differ from the reference program's by a relative error of at most 0.02.
The reference program's roundings to bfloat16 on the way count: a program that leaves them out, or rounds other values in their place, can miss the bound.
Values may be sent and summed in bfloat16 or wider, within the bound.
A program may use at most 192 MiB of HBM per device.

```python
import math
import jax
import jax.numpy as jnp
import numpy as np
from jax import lax

D = 8192
H = 64
HD = 128
DE = 896
SPAN = 64
NBR_LEN = 128
NBRS = 2
CAP = 3
TOK_DEV = 512
NDB_DEV = 32
CH_DEV = 8
TOKENS = 8192
NCH = 128
NDB = 512
N_DB = 16


def draw_w_key(key, part):
    result = jax.random.truncated_normal(jax.random.fold_in(key, 5), -4.0, 4.0, (DE, D), jnp.float32) * DE ** (-0.5)
    return result.astype(jnp.bfloat16)


def draw_database(key, part):
    result = jax.random.truncated_normal(jax.random.fold_in(key, 6), -4.0, 4.0, (NDB, NBR_LEN, DE), jnp.float32)
    return result.astype(jnp.bfloat16)


def draw_queries(key, part):
    result = jax.random.truncated_normal(jax.random.fold_in(key, 8), -4.0, 4.0, (TOKENS, D), jnp.float32) * 2.0
    return result.astype(jnp.bfloat16)


def plant(array, stream_key, smallest, high):
    spot = [jax.random.randint(jax.random.fold_in(stream_key, axis), (), 0, length) for axis, length in enumerate(array.shape)]
    widest = array.shape.index(max(array.shape))
    beside = spot[:widest] + [(spot[widest] + 1) % array.shape[widest]] + spot[widest + 1:]
    return array.at[tuple(spot)].set(smallest).at[tuple(beside)].set(high)


def steps_of(own_key, extent, shards, low, largest):
    level, own = 1.0, jax.random.fold_in(own_key, 6)
    for dim, blocks in shards:
        heights = jnp.exp(jax.random.uniform(jax.random.fold_in(own, dim), (blocks,), jnp.float32, low / len(shards), largest / len(shards)))
        level = level * jnp.repeat(heights, extent[dim] // blocks).reshape([-1 if axis == dim else 1 for axis in range(len(extent))])
    return level


def assign_block(stream_key, own, number, rows, count, top, reach, skew):
    ranking = jax.random.permutation(stream_key, count)
    packed, ordinary = portions_of(count, rows * top, reach, skew, True), portions_of(count, rows * top, reach, skew, False)
    places = jnp.arange(count)

    def named(sizes, rotation):
        used = int((sizes > 0).sum())
        fixed = max(1, used // 4)
        moved = fixed + (places - fixed + rotation * (used - fixed)) % max(1, count - fixed)
        return jnp.zeros((count,), jnp.int32).at[ranking[jnp.where(places < fixed, places, moved)]].set(jnp.asarray(sizes, jnp.int32))

    sizes = jnp.where(number % 4 == 0, named(packed, number // 4), named(ordinary, number - number // 4 - 1))
    mixed = jax.random.permutation(jax.random.fold_in(own, 3), count)
    giver, sink = mixed[0:count // 2 * 2:2], mixed[1:count // 2 * 2:2]
    margin = jnp.minimum(sizes[giver] - 1, reach - sizes[sink]) // 2
    margin = jnp.where((giver == ranking[0]) | (sink == ranking[0]) | (sizes[sink] == 0), 0, jnp.maximum(margin, 0))
    moved = jax.random.randint(jax.random.fold_in(own, 4), (count // 2,), 0, 1 << 20) % (margin + 1)
    sizes = sizes.at[giver].add(-moved).at[sink].add(moved)
    labels = jnp.searchsorted(jnp.cumsum(sizes), jnp.arange(rows * top), side="right").astype(jnp.int32)
    listing = labels.reshape(top, rows).T
    listing = listing[jax.random.permutation(jax.random.fold_in(own, 1), rows)]
    rotation = jax.random.randint(jax.random.fold_in(own, 2), (rows, 1), 0, top)
    return jnp.take_along_axis(listing, (jnp.arange(top)[None, :] + rotation) % top, axis=1)


def portions_of(amount, total, reach, slope, full):
    loads = [(1 << 20) // math.isqrt(standing ** slope) + 1 for standing in range(1, amount + 1)]
    largest = reach if full else min(reach, max(-(-total // amount), total * loads[0] // sum(loads)))
    least = 1 if total - largest >= amount - 1 else 0
    holding, surplus = [largest] + [least] * (amount - 1), total - largest - least * (amount - 1)
    while surplus > 0:
        movable = [i for i in range(1, amount) if holding[i] < largest] or [i for i in range(1, amount) if holding[i] < reach]
        pool, left = sum([loads[i] for i in movable]), surplus
        for i in movable:
            extra = min(reach - holding[i], max(1, left * loads[i] // pool), surplus)
            holding[i] = holding[i] + extra
            surplus = surplus - extra
    return np.array(holding)


def scatter_about(stream_key, extent, deviation, bound, cuts=(), kind=jnp.bfloat16):
    values = jax.random.normal(stream_key, extent, jnp.float32) * deviation
    if len(cuts) > 0:
        values = steps_of(stream_key, extent, cuts, -0.22, 0.18) * values
    return jnp.clip(values, min=-bound, max=bound).astype(kind)


def setup_inputs(seed: int = 0) -> dict:
    arg_keys = jax.random.split(jax.random.key(seed), 8)
    queries = draw_queries(jax.random.fold_in(arg_keys[7], 71), 0)
    cotangent = scatter_about(arg_keys[1], (TOKENS, D), 1.0, 6.0, ((0, 16), (1, 8)))
    database = draw_database(jax.random.fold_in(arg_keys[7], 71), 0)
    w_key = draw_w_key(jax.random.fold_in(arg_keys[7], 71), 0)
    w_value = scatter_about(arg_keys[4], (DE, D), DE ** -0.5, 0.1875, ((1, 8),))
    neighbour_owner_keys = jax.random.split(jax.random.fold_in(arg_keys[5], 1), NCH // CH_DEV)
    neighbour_owner_turns = jax.random.permutation(jax.random.fold_in(arg_keys[5], 3), NCH // CH_DEV)
    neighbour_owner = jax.vmap(lambda own, number: assign_block(jax.random.fold_in(arg_keys[5], 2), own, number, CH_DEV, N_DB, NBRS, CAP, 2))(neighbour_owner_keys, neighbour_owner_turns).reshape((NCH, NBRS))
    neighbour_slot = plant(jax.random.randint(arg_keys[6], (NCH, NBRS), 0, NDB_DEV), jax.random.fold_in(arg_keys[6], 1), 0, NDB_DEV - 1).astype(jnp.int32)
    return {"queries": queries, "cotangent": cotangent, "database": database, "w_key": w_key, "w_value": w_value, "neighbour_owner": neighbour_owner, "neighbour_slot": neighbour_slot}


def block_pass(query_block, grad_block, panels, w_key, w_value):
    span_count = panels.shape[0]
    key_count = NBRS * NBR_LEN
    flat_rows = panels.reshape(span_count * key_count, DE)
    key_rows = jnp.dot(flat_rows, w_key, preferred_element_type=jnp.float32).astype(jnp.bfloat16)
    value_rows = jnp.dot(flat_rows, w_value, preferred_element_type=jnp.float32).astype(jnp.bfloat16)
    key_heads = key_rows.reshape(span_count, key_count, H, HD).astype(jnp.float32)
    value_heads = value_rows.reshape(span_count, key_count, H, HD).astype(jnp.float32)
    query_heads = query_block.reshape(span_count, SPAN, H, HD).astype(jnp.float32)
    grad_heads = grad_block.reshape(span_count, SPAN, H, HD).astype(jnp.float32)
    score_scale = HD ** -0.5
    scores = jnp.einsum("cihd,cjhd->chij", query_heads, key_heads) * score_scale
    weights_full = jax.nn.softmax(scores, axis=-1)
    weights_half = lax.optimization_barrier(weights_full.astype(jnp.bfloat16)).astype(jnp.float32)
    attended = jnp.einsum("chij,cjhd->cihd", weights_half, value_heads).astype(jnp.bfloat16)
    attended = attended.reshape(span_count * SPAN, D)
    grad_prob = jnp.einsum("cihd,cjhd->chij", grad_heads, value_heads)
    grad_value = jnp.einsum("chij,cihd->cjhd", weights_half, grad_heads).astype(jnp.bfloat16)
    row_delta = jnp.sum(weights_full * grad_prob, axis=-1, keepdims=True)
    grad_score = (weights_full * (grad_prob - row_delta) * score_scale).astype(jnp.bfloat16)
    grad_score_f = lax.optimization_barrier(grad_score).astype(jnp.float32)
    grad_query = jnp.einsum("chij,cjhd->cihd", grad_score_f, key_heads).astype(jnp.bfloat16)
    grad_query = grad_query.reshape(span_count * SPAN, D)
    grad_key = jnp.einsum("chij,cihd->cjhd", grad_score_f, query_heads).astype(jnp.bfloat16)
    key_flat = grad_key.reshape(span_count * key_count, D)
    value_flat = grad_value.reshape(span_count * key_count, D)
    contract = (((0,), (0,)), ((), ()))
    term_key = lax.dot_general(flat_rows, key_flat, contract, preferred_element_type=jnp.float32)
    term_value = lax.dot_general(flat_rows, value_flat, contract, preferred_element_type=jnp.float32)
    use_grad = jnp.dot(key_flat, w_key.T, preferred_element_type=jnp.float32)
    use_grad = use_grad + jnp.dot(value_flat, w_value.T, preferred_element_type=jnp.float32)
    use_grad = use_grad.astype(jnp.bfloat16).reshape(span_count * NBRS, NBR_LEN, DE)
    return attended, grad_query, term_key, term_value, use_grad


def reference(queries, cotangent, database, w_key, w_value, neighbour_owner, neighbour_slot):
    global_rows = (neighbour_owner * NDB_DEV + neighbour_slot).astype(jnp.int32)

    def block_step(totals, block_id):
        sum_key, sum_value, sum_panel = totals
        first_token = (block_id * TOK_DEV).astype(jnp.int32)
        first_span = (block_id * CH_DEV).astype(jnp.int32)
        query_block = lax.dynamic_slice_in_dim(queries, first_token, TOK_DEV, 0)
        grad_block = lax.dynamic_slice_in_dim(cotangent, first_token, TOK_DEV, 0)
        row_block = lax.dynamic_slice_in_dim(global_rows, first_span, CH_DEV, 0).reshape(CH_DEV * NBRS)
        panels = jnp.take(database, row_block, axis=0).reshape(CH_DEV, NBRS * NBR_LEN, DE)
        attended, grad_query, term_key, term_value, use_grad = block_pass(query_block, grad_block, panels, w_key, w_value)
        sum_panel = sum_panel + jax.ops.segment_sum(use_grad.astype(jnp.float32), row_block, num_segments=NDB)
        return (sum_key + term_key, sum_value + term_value, sum_panel), (attended, grad_query)

    start = (jnp.zeros((DE, D), jnp.float32), jnp.zeros((DE, D), jnp.float32), jnp.zeros((NDB, NBR_LEN, DE), jnp.float32))
    totals, stacked = lax.scan(block_step, start, jnp.arange(N_DB, dtype=jnp.int32))
    attended = stacked[0].reshape(TOKENS, D)
    grad_queries = stacked[1].reshape(TOKENS, D)
    return attended, grad_queries, totals[0], totals[1], totals[2].astype(jnp.bfloat16)
```

```python
import functools

import jax
import jax.numpy as jnp
from jax import lax
from jax.experimental import pallas as pl
from jax.experimental.pallas import tpu as pltpu
from jax.sharding import PartitionSpec as P

HD = 128
SPAN = 64
CAP = 3
NT = (((1,), (1,)), ((), ()))
TN = (((0,), (0,)), ((), ()))
F32 = jnp.float32
BF16 = jnp.bfloat16


def dot(a, b):
    return jnp.dot(a, b, preferred_element_type=F32)


def block_kernel(spans, heads, panels, queries, cotangent, w_key, w_value, attended, grad_queries, part_key, part_value,
                 use_grad, flipped, rows_kv, grads_kv):
    step = pl.program_id(0)
    keys = panels.shape[0] // spans
    width = panels.shape[1]
    scale = HD ** -0.5

    @pl.when(step == 0)
    def _():
        for c in range(spans):
            flipped[:, c * keys:(c + 1) * keys] = panels[c * keys:(c + 1) * keys, :].T

    @pl.when(step < heads)
    def _():
        columns = pl.ds(pl.multiple_of(step * HD, HD), HD)
        weights = jnp.concatenate([w_key[:, columns], w_value[:, columns]], axis=1)
        half = spans // 2 * keys
        for part in range(2):
            rows_kv[part * half:(part + 1) * half, :] = dot(panels[part * half:(part + 1) * half, :], weights).astype(BF16)
        zero = jnp.zeros((SPAN, HD), BF16)
        for c in range(spans):
            tokens = slice(c * SPAN, (c + 1) * SPAN)
            own = slice(c * keys, (c + 1) * keys)
            query, grad = queries[tokens, :], cotangent[tokens, :]
            both = rows_kv[own, :]
            left = jnp.concatenate(
                [jnp.concatenate([query, zero], axis=1), jnp.concatenate([zero, grad], axis=1)], axis=0
            )
            pair = lax.dot_general(left, both, NT, preferred_element_type=F32)
            scores, grad_probs = pair[:SPAN] * scale, pair[SPAN:]
            raised = jnp.exp(scores - jnp.max(scores, axis=-1, keepdims=True))
            probs = raised / jnp.sum(raised, axis=-1, keepdims=True)
            delta = jnp.sum(probs * grad_probs, axis=-1, keepdims=True)
            grad_scores = (probs * (grad_probs - delta) * scale).astype(BF16)
            stacked = jnp.concatenate([probs.astype(BF16), grad_scores], axis=0)
            out = dot(stacked, both)
            attended[tokens, :] = out[:SPAN, HD:].astype(BF16)
            grad_queries[tokens, :] = out[SPAN:, :HD].astype(BF16)
            right = jnp.concatenate(
                [jnp.concatenate([zero, grad], axis=1), jnp.concatenate([query, zero], axis=1)], axis=0
            )
            grads_kv[step, own, :] = lax.dot_general(stacked, right, TN, preferred_element_type=F32).astype(BF16)
        total = dot(flipped[...], grads_kv[step]).astype(BF16)
        part_key[...] = total[:, :HD]
        part_value[...] = total[:, HD:]

    @pl.when(step >= heads)
    def _():
        c = step - heads
        own = pl.ds(pl.multiple_of(c * keys, keys), keys)
        total = jnp.zeros((keys, width), F32)
        for h in range(heads):
            columns = slice(h * HD, (h + 1) * HD)
            weights = jnp.concatenate([w_key[:, columns], w_value[:, columns]], axis=1)
            total = total + lax.dot_general(grads_kv[h, own, :], weights, NT, preferred_element_type=F32)
        total = total.astype(BF16)
        pieces, uses, rows = use_grad.shape[0], use_grad.shape[1], use_grad.shape[2]
        for n in range(uses):
            for r in range(pieces):
                first = (n * pieces + r) * rows
                use_grad[r, n, :, :] = total[first:first + rows, :]


def block_call(panels, queries, cotangent, w_key, w_value, racks):
    uses, panel_len, width = panels.shape
    spans = queries.shape[0] // SPAN
    features = w_key.shape[1]
    heads = features // HD
    per_span = uses // spans
    rows = panel_len // racks
    total = uses * panel_len
    once = dict(pipeline_mode=pl.Buffered(1))
    by_head = lambda size: pl.BlockSpec((size, HD), lambda i: (0, jnp.minimum(i, heads - 1)))
    whole = lambda a, b: pl.BlockSpec((a, b), lambda i: (0, 0), **once)

    return pl.pallas_call(
        functools.partial(block_kernel, spans, heads),
        grid=(heads + spans,),
        out_shape=(
            jax.ShapeDtypeStruct(queries.shape, BF16),
            jax.ShapeDtypeStruct(queries.shape, BF16),
            jax.ShapeDtypeStruct((width, features), BF16),
            jax.ShapeDtypeStruct((width, features), BF16),
            jax.ShapeDtypeStruct((racks, uses, rows, width), BF16),
        ),
        in_specs=[
            whole(total, width), by_head(queries.shape[0]), by_head(queries.shape[0]), whole(width, features), whole(width, features),
        ],
        out_specs=[
            by_head(queries.shape[0]), by_head(queries.shape[0]), by_head(width), by_head(width),
            pl.BlockSpec((racks, per_span, rows, width), lambda i: (0, jnp.maximum(i - heads, 0), 0, 0)),
        ],
        scratch_shapes=[
            pltpu.VMEM((width, total), BF16),
            pltpu.VMEM((total, 2 * HD), BF16),
            pltpu.VMEM((heads, total, 2 * HD), BF16),
        ],
        compiler_params=pltpu.CompilerParams(vmem_limit_bytes=56 * 1024 * 1024),
        cost_estimate=pl.CostEstimate(flops=6 * total * width * features * 2, bytes_accessed=24 << 20, transcendentals=1 << 20),
        name="block",
    )(panels.reshape(total, width), queries, cotangent, w_key, w_value)


def pick(selector, source):
    return jnp.einsum("ns,spw->npw", selector, source, preferred_element_type=F32).astype(BF16)


def local(queries, cotangent, database, w_key, w_value, neighbour_owner, neighbour_slot):
    peer_count = lax.axis_size("db")
    racks = lax.axis_size("rack")
    span_count, nbr_count = neighbour_owner.shape
    use_count = span_count * nbr_count
    local_rows, panel_len, width = database.shape
    rows = panel_len // racks
    owners = neighbour_owner.reshape(use_count)
    offsets = neighbour_slot.reshape(use_count)
    earlier = jnp.arange(use_count)[None, :] < jnp.arange(use_count)[:, None]
    ranked = jnp.sum(((owners[:, None] == owners[None, :]) & earlier).astype(jnp.int32), axis=1)
    target = owners * CAP + ranked
    named = (target[None, :] == jnp.arange(peer_count * CAP, dtype=jnp.int32)[:, None]).astype(jnp.int32)
    wanted = jnp.sum(named * (offsets - local_rows)[None, :], axis=1) + local_rows
    asked_rows = lax.all_to_all(wanted.reshape(peer_count, CAP), "db", split_axis=0, concat_axis=0, tiled=True)
    own = lax.dynamic_slice_in_dim(database, lax.axis_index("rack") * rows, rows, 1)
    selector = (
        asked_rows.reshape(peer_count * CAP)[:, None] == jnp.arange(local_rows, dtype=jnp.int32)[None, :]
    ).astype(BF16)
    answer = pick(selector, own).reshape(peer_count, CAP, rows, width)
    arrived = lax.all_to_all(answer, "db", split_axis=0, concat_axis=0, tiled=True)
    placed = (target[:, None] == jnp.arange(peer_count * CAP, dtype=jnp.int32)[None, :]).astype(BF16)
    mine = pick(placed, arrived.reshape(peer_count * CAP, rows, width))
    panels = lax.all_gather(mine, "rack", axis=1, tiled=True)
    attended, grad_query, part_key, part_value, use_grad = block_call(panels, queries, cotangent, w_key, w_value, racks)
    grad_w_key = lax.psum(part_key, "db").astype(F32)
    grad_w_value = lax.psum(part_value, "db").astype(F32)
    shares = lax.psum_scatter(use_grad, "rack", scatter_dimension=0, tiled=True)[0]
    outgoing = pick(placed.T, shares)
    returned = lax.all_to_all(outgoing.reshape(peer_count, CAP, rows, width), "db", split_axis=0, concat_axis=0, tiled=True)
    grad_database = pick(selector.T, returned.reshape(peer_count * CAP, rows, width))
    return attended, grad_query, grad_w_key, grad_w_value, grad_database


def solution(mesh):
    return jax.shard_map(
        local,
        mesh=mesh,
        in_specs=(
            P("db", "rack"), P("db", "rack"), P("db", None, None), P(None, "rack"), P(None, "rack"), P("db", None), P("db", None),
        ),
        out_specs=(P("db", "rack"), P("db", "rack"), P(None, "rack"), P(None, "rack"), P("db", "rack", None)),
        check_vma=False,
    )
```

```python
import functools

import jax
import jax.numpy as jnp
from jax import lax
from jax.experimental import pallas as pl
from jax.experimental.pallas import tpu as pltpu
from jax.sharding import PartitionSpec as P

HD = 128
SPAN = 64
CAP = 3
NT = (((1,), (1,)), ((), ()))
TN = (((0,), (0,)), ((), ()))
F32 = jnp.float32
BF16 = jnp.bfloat16


def dot(a, b):
    return jnp.dot(a, b, preferred_element_type=F32)


def block_kernel(spans, heads, panels, queries, cotangent, w_key, w_value, attended, grad_queries, part_key, part_value,
                 use_grad, flipped, rows_kv, grads_kv):
    step = pl.program_id(0)
    keys = panels.shape[0] // spans
    width = panels.shape[1]
    scale = HD ** -0.5

    @pl.when(step == 0)
    def _():
        for c in range(spans):
            flipped[:, c * keys:(c + 1) * keys] = panels[c * keys:(c + 1) * keys, :].T

    @pl.when(step < heads)
    def _():
        columns = pl.ds(pl.multiple_of(step * HD, HD), HD)
        weights = jnp.concatenate([w_key[:, columns], w_value[:, columns]], axis=1)
        half = spans // 2 * keys
        for part in range(2):
            rows_kv[part * half:(part + 1) * half, :] = dot(panels[part * half:(part + 1) * half, :], weights).astype(BF16)
        zero = jnp.zeros((SPAN, HD), BF16)
        for c in range(spans):
            tokens = slice(c * SPAN, (c + 1) * SPAN)
            own = slice(c * keys, (c + 1) * keys)
            query, grad = queries[tokens, :], cotangent[tokens, :]
            both = rows_kv[own, :]
            left = jnp.concatenate(
                [jnp.concatenate([query, zero], axis=1), jnp.concatenate([zero, grad], axis=1)], axis=0
            )
            pair = lax.dot_general(left, both, NT, preferred_element_type=F32)
            scores, grad_probs = pair[:SPAN] * scale, pair[SPAN:]
            raised = jnp.exp(scores - jnp.max(scores, axis=-1, keepdims=True))
            probs = raised / jnp.sum(raised, axis=-1, keepdims=True)
            delta = jnp.sum(probs * grad_probs, axis=-1, keepdims=True)
            grad_scores = (probs * (grad_probs - delta) * scale).astype(BF16)
            stacked = jnp.concatenate([probs.astype(BF16), grad_scores], axis=0)
            out = dot(stacked, both)
            attended[tokens, :] = out[:SPAN, HD:].astype(BF16)
            grad_queries[tokens, :] = out[SPAN:, :HD].astype(BF16)
            right = jnp.concatenate(
                [jnp.concatenate([zero, grad], axis=1), jnp.concatenate([query, zero], axis=1)], axis=0
            )
            grads_kv[step, own, :] = lax.dot_general(stacked, right, TN, preferred_element_type=F32).astype(BF16)
        total = dot(flipped[...], grads_kv[step]).astype(BF16)
        part_key[...] = total[:, :HD]
        part_value[...] = total[:, HD:]

    @pl.when(step >= heads)
    def _():
        c = step - heads
        own = pl.ds(pl.multiple_of(c * keys, keys), keys)
        total = jnp.zeros((keys, width), F32)
        for h in range(heads):
            columns = slice(h * HD, (h + 1) * HD)
            weights = jnp.concatenate([w_key[:, columns], w_value[:, columns]], axis=1)
            total = total + lax.dot_general(grads_kv[h, own, :], weights, NT, preferred_element_type=F32)
        total = total.astype(BF16)
        pieces, uses, rows = use_grad.shape[0], use_grad.shape[1], use_grad.shape[2]
        for n in range(uses):
            for r in range(pieces):
                first = (n * pieces + r) * rows
                use_grad[r, n, :, :] = total[first:first + rows, :]


def block_call(panels, queries, cotangent, w_key, w_value, racks):
    uses, panel_len, width = panels.shape
    spans = queries.shape[0] // SPAN
    features = w_key.shape[1]
    heads = features // HD
    per_span = uses // spans
    rows = panel_len // racks
    total = uses * panel_len
    once = dict(pipeline_mode=pl.Buffered(1))
    by_head = lambda size: pl.BlockSpec((size, HD), lambda i: (0, jnp.minimum(i, heads - 1)))
    whole = lambda a, b: pl.BlockSpec((a, b), lambda i: (0, 0), **once)

    return pl.pallas_call(
        functools.partial(block_kernel, spans, heads),
        grid=(heads + spans,),
        out_shape=(
            jax.ShapeDtypeStruct(queries.shape, BF16),
            jax.ShapeDtypeStruct(queries.shape, BF16),
            jax.ShapeDtypeStruct((width, features), BF16),
            jax.ShapeDtypeStruct((width, features), BF16),
            jax.ShapeDtypeStruct((racks, uses, rows, width), BF16),
        ),
        in_specs=[
            whole(total, width), by_head(queries.shape[0]), by_head(queries.shape[0]), whole(width, features), whole(width, features),
        ],
        out_specs=[
            by_head(queries.shape[0]), by_head(queries.shape[0]), by_head(width), by_head(width),
            pl.BlockSpec((racks, per_span, rows, width), lambda i: (0, jnp.maximum(i - heads, 0), 0, 0)),
        ],
        scratch_shapes=[
            pltpu.VMEM((width, total), BF16),
            pltpu.VMEM((total, 2 * HD), BF16),
            pltpu.VMEM((heads, total, 2 * HD), BF16),
        ],
        compiler_params=pltpu.CompilerParams(vmem_limit_bytes=56 * 1024 * 1024),
        cost_estimate=pl.CostEstimate(flops=6 * total * width * features * 2, bytes_accessed=24 << 20, transcendentals=1 << 20),
        name="block",
    )(panels.reshape(total, width), queries, cotangent, w_key, w_value)


MESH = pl.DeviceIdType.MESH


class Links:
    def __init__(self, side_z, side_y, side_x):
        db, rack = lax.axis_index("db"), lax.axis_index("rack")
        self.db, self.rack = db, rack
        self.z, self.y = db // side_y, db % side_y
        self.x, self.core = rack // 2, rack % 2
        self.side_x = side_x
        self.ids = {
            ("y", 1): (self.z * side_y + (self.y + 1) % side_y, rack),
            ("y", -1): (self.z * side_y + (self.y + side_y - 1) % side_y, rack),
            ("z", 1): ((self.z + 1) % side_z * side_y + self.y, rack),
            ("z", -1): ((self.z + side_z - 1) % side_z * side_y + self.y, rack),
            ("x", 1): (db, (self.x + 1) % side_x * 2 + self.core),
            ("x", -1): (db, (self.x + side_x - 1) % side_x * 2 + self.core),
            ("core", 1): (db, self.x * 2 + 1 - self.core),
        }

    def place(self, axis):
        return {"y": self.y, "z": self.z, "x": self.x}[axis]


class Mail:
    def __init__(self, send_sems, recv_sems, first=0):
        self.send_sems, self.recv_sems, self.next = send_sems, recv_sems, first
        self.open = {}
        self.sent = []

    def send(self, name, source, target, device):
        copy = pltpu.make_async_remote_copy(
            src_ref=source, dst_ref=target, send_sem=self.send_sems.at[self.next], recv_sem=self.recv_sems.at[self.next],
            device_id=device, device_id_type=MESH,
        )
        self.next += 1
        copy.start()
        self.open[name] = copy
        self.sent.append(copy)

    def arrive(self, *names):
        for name in names:
            self.open[name].wait_recv()

    def drain(self):
        for copy in self.sent:
            copy.wait_send()
        self.sent = []


def add(*terms):
    total = terms[0].astype(F32)
    for term in terms[1:]:
        total = total + term.astype(F32)
    return total.astype(BF16)


class Reduction:
    def __init__(self, tag, links, mail, part, full, first_column, columns, axes, near, far, middle):
        self.tag, self.links, self.mail = tag, links, mail
        self.part, self.full, self.first_column, self.columns = part, full, first_column, columns
        self.one, self.two = axes
        self.near, self.far, self.middle = near, far, middle
        self.rows = part.shape[0] // 4
        self.half = self.rows // 2
        self.narrow = columns // 4

    def name(self, what):
        return (self.tag, what)

    def spot(self, ref, one, side):
        first = one * self.rows + side * self.half
        return ref.at[pl.ds(pl.multiple_of(first, 16), self.half), pl.ds(self.first_column, self.columns)]

    def small(self, two, side):
        return self.middle.at[pl.ds(side * self.half, self.half), pl.ds(pl.multiple_of(two * self.narrow, 128), self.narrow)]

    def piece(self, one, two, first, size):
        return self.full.at[
            pl.ds(pl.multiple_of(one * self.rows + first, 16), size),
            pl.ds(pl.multiple_of(self.first_column + two * self.narrow, 128), self.narrow),
        ]

    def first(self, axis, at, buffer, level):
        links, mail, me = self.links, self.mail, self.links.place(axis)
        up, down = links.ids[(axis, 1)], links.ids[(axis, -1)]
        mail.send(self.name(level + "ra"), at((me + 2) % 4, 0), buffer.at[0], up)
        mail.send(self.name(level + "rb"), at((me + 2) % 4, 1), buffer.at[1], down)
        mail.send(self.name(level + "db"), at((me + 1) % 4, 1), buffer.at[3], up)
        mail.send(self.name(level + "da"), at((me + 3) % 4, 0), buffer.at[2], down)

    def second(self, axis, at, buffer, level):
        links, mail, me = self.links, self.mail, self.links.place(axis)
        up, down = links.ids[(axis, 1)], links.ids[(axis, -1)]
        mail.arrive(self.name(level + "ra"))
        buffer[0, :, :] = add(buffer[0], at((me + 1) % 4, 0)[...])
        mail.send(self.name(level + "sa"), buffer.at[0], buffer.at[4], up)
        mail.arrive(self.name(level + "rb"))
        buffer[1, :, :] = add(buffer[1], at((me + 3) % 4, 1)[...])
        mail.send(self.name(level + "sb"), buffer.at[1], buffer.at[5], down)

    def third(self, axis, at, buffer, level, side):
        mail, me = self.mail, self.links.place(axis)
        letter = "ab"[side]
        mail.arrive(self.name(level + "d" + letter), self.name(level + "s" + letter))
        return add(buffer[2 + side], buffer[4 + side], at(me, side)[...])

    def spread(self, axis, at, level):
        links, mail, me = self.links, self.mail, self.links.place(axis)
        mail.send(self.name(level + "up"), at(me, 0, self.rows), at(me, 0, self.rows), links.ids[(axis, 1)])
        mail.send(self.name(level + "down"), at(me, 0, self.rows), at(me, 0, self.rows), links.ids[(axis, -1)])

    def forward(self, axis, at, level):
        links, mail, me = self.links, self.mail, self.links.place(axis)
        mail.arrive(self.name(level + "up"))
        mail.send(
            self.name(level + "on"), at((me + 3) % 4, 0, self.half), at((me + 3) % 4, 0, self.half), links.ids[(axis, 1)]
        )
        mail.arrive(self.name(level + "down"))
        mail.send(
            self.name(level + "back"), at((me + 1) % 4, self.half, self.half), at((me + 1) % 4, self.half, self.half),
            links.ids[(axis, -1)],
        )

    def stage(self, number):
        wide = lambda one, side: self.spot(self.part, one, side)
        mine = self.links.place(self.one)
        column = lambda two, first, size: self.piece(mine, two, first, size)
        row = lambda one, first, size: self.full.at[
            pl.ds(pl.multiple_of(one * self.rows + first, 16), size), pl.ds(self.first_column, self.columns)
        ]
        if number == 0:
            self.first(self.one, wide, self.near, "n")
        elif number == 1:
            self.second(self.one, wide, self.near, "n")
        elif number == 2:
            for side in (0, 1):
                self.middle[side * self.half:(side + 1) * self.half, :] = self.third(self.one, wide, self.near, "n", side)
            self.first(self.two, self.small, self.far, "f")
        elif number == 3:
            self.second(self.two, self.small, self.far, "f")
        elif number == 4:
            for side in (0, 1):
                total = self.third(self.two, self.small, self.far, "f", side)
                column(self.links.place(self.two), side * self.half, self.half)[...] = total
            self.spread(self.two, column, "g")
        elif number == 5:
            self.forward(self.two, column, "g")
        elif number == 6:
            self.mail.arrive(self.name("gon"), self.name("gback"))
            self.spread(self.one, row, "h")
        elif number == 7:
            self.forward(self.one, row, "h")
        else:
            self.mail.arrive(self.name("hon"), self.name("hback"))


class Return:
    def __init__(self, links, mail, use_grad, user, returned, crossed, ring, mine, leaving, leave_sems, land_sems):
        self.links, self.mail, self.use_grad, self.user, self.returned = links, mail, use_grad, user, returned
        self.crossed, self.ring, self.mine, self.leaving = crossed, ring, mine, leaving
        self.leave_sems, self.land_sems = leave_sems, land_sems
        self.half = mine.shape[0] // 2

    def spot(self, far, side):
        return self.crossed.at[(self.links.x + far) % 4, pl.ds(side * self.half, self.half)]

    def stage(self, number):
        links, mail = self.links, self.mail
        up, down = links.ids[("x", 1)], links.ids[("x", -1)]
        half = self.half
        if number == 0:
            for far in (2, 1, 3, 0):
                x = (links.x + far) % 4
                mail.send(("c", far), self.use_grad.at[x * 2 + 1 - links.core], self.crossed.at[x], links.ids[("core", 1)])
        elif number == 1:
            def join(far):
                x = (links.x + far) % 4
                mail.arrive(("c", far))

                @pl.loop(0, half * 2)
                def _(n):
                    self.crossed[x, n] = add(self.crossed[x, n], self.use_grad[x * 2 + links.core, n])

            join(2)
            mail.send("xra", self.spot(2, 0), self.ring.at[0], up)
            mail.send("xrb", self.spot(2, 1), self.ring.at[1], down)
            join(1)
            mail.send("xdb", self.spot(1, 1), self.ring.at[3], up)
            join(3)
            mail.send("xda", self.spot(3, 0), self.ring.at[2], down)
            join(0)
        elif number == 2:
            for side, letter, far, device in ((0, "a", 1, up), (1, "b", 3, down)):
                mail.arrive("xr" + letter)
                own = self.spot(far, side)

                @pl.loop(0, half)
                def _(n):
                    self.ring[side, n] = add(self.ring[side, n], own[n])

                mail.send("xs" + letter, self.ring.at[side], self.ring.at[4 + side], device)
        elif number == 3:
            for side, letter in ((0, "a"), (1, "b")):
                mail.arrive("xd" + letter, "xs" + letter)
                own = self.spot(0, side)

                @pl.loop(0, half)
                def _(n):
                    self.mine[side * half + n] = add(self.ring[2 + side, n], self.ring[4 + side, n], own[n])

            self.mine[2 * half] = jnp.zeros(self.mine.shape[1:], BF16)
            peers = self.returned.shape[0]

            def fill(peer, target, at):
                for k in range(CAP):
                    target[at, k] = self.mine[self.user[peer * CAP + k]]

            fill(links.db, self.returned, links.db)

            @pl.loop(1, peers)
            def _(far):
                peer = (links.db + far) % peers
                fill(peer, self.leaving, peer)
                self.copy(far).start()
        else:
            @pl.loop(1, self.returned.shape[0])
            def _(far):
                self.copy(far).wait()

    def copy(self, far):
        links = self.links
        peer = (links.db + far) % self.returned.shape[0]
        return pltpu.make_async_remote_copy(
            src_ref=self.leaving.at[peer], dst_ref=self.returned.at[links.db], send_sem=self.leave_sems.at[far],
            recv_sem=self.land_sems.at[far], device_id=(peer, links.rack), device_id_type=MESH,
        )


def greet(links, peers):
    barrier = pltpu.get_barrier_semaphore()
    others = [links.ids[("core", 1)], links.ids[("x", 1)], links.ids[("x", -1)]]
    for device in others:
        pl.semaphore_signal(barrier, inc=1, device_id=device, device_id_type=MESH)

    @pl.loop(1, peers)
    def _(far):
        pl.semaphore_signal(barrier, inc=1, device_id=((links.db + far) % peers, links.rack), device_id_type=MESH)

    pl.semaphore_wait(barrier, len(others) + peers - 1)


GROUPS = 2
MESSAGES = 20 * 2 * GROUPS + 10


def return_kernel(user, part_key, part_value, use_grad, full_key, full_value, returned, near, far, middle, crossed, ring, mine,
                  leaving, send_sems, recv_sems, leave_sems, land_sems):
    links = Links(4, 4, 4)
    greet(links, returned.shape[0])
    mail = Mail(send_sems, recv_sems)
    columns = part_key.shape[1] // GROUPS
    items = []
    for g in range(GROUPS):
        for m, (part, full, axes) in enumerate(((part_key, full_key, "yz"), (part_value, full_value, "zy"))):
            n = g * 2 + m
            items.append(Reduction(n, links, mail, part, full, g * columns, columns, axes, near.at[n], far.at[n], middle.at[n]))
    back = Return(links, mail, use_grad, user, returned, crossed, ring, mine, leaving, leave_sems, land_sems)
    back.stage(0)
    for item in items:
        item.stage(0)
    back.stage(1)
    for item in items[:2]:
        item.stage(1)
    back.stage(2)
    for item in items[:2]:
        item.stage(2)
    for item in items[2:]:
        item.stage(1)
    back.stage(3)
    for item in items[:2]:
        item.stage(3)
    for item in items[2:]:
        item.stage(2)
    for number in (4, 5, 6, 7, 8):
        for item in items[:2]:
            item.stage(number)
        for item in items[2:]:
            item.stage(number - 1)
    for item in items[2:]:
        item.stage(8)
    back.stage(4)
    mail.drain()


def return_call(user, part_key, part_value, use_grad, peers):
    width, features = part_key.shape
    racks, uses, rows, _ = use_grad.shape
    columns = features // GROUPS
    vmem = pl.BlockSpec(memory_space=pltpu.VMEM)
    return pl.pallas_call(
        return_kernel,
        out_shape=(
            jax.ShapeDtypeStruct((width, features), BF16),
            jax.ShapeDtypeStruct((width, features), BF16),
            jax.ShapeDtypeStruct((peers, CAP, rows, width), BF16),
        ),
        in_specs=[pl.BlockSpec(memory_space=pltpu.SMEM), vmem, vmem, vmem],
        out_specs=(vmem, vmem, vmem),
        scratch_shapes=[
            pltpu.VMEM((2 * GROUPS, 6, width // 8, columns), BF16),
            pltpu.VMEM((2 * GROUPS, 6, width // 8, columns // 4), BF16),
            pltpu.VMEM((2 * GROUPS, width // 4, columns), BF16),
            pltpu.VMEM((4, uses, rows, width), BF16),
            pltpu.VMEM((6, uses // 2, rows, width), BF16),
            pltpu.VMEM((uses + 1, rows, width), BF16),
            pltpu.VMEM((peers, CAP, rows, width), BF16),
            pltpu.SemaphoreType.DMA((MESSAGES,)),
            pltpu.SemaphoreType.DMA((MESSAGES,)),
            pltpu.SemaphoreType.DMA((peers,)),
            pltpu.SemaphoreType.DMA((peers,)),
        ],
        compiler_params=pltpu.CompilerParams(
            collective_id=1, has_side_effects=True, vmem_limit_bytes=48 * 1024 * 1024
        ),
        name="send_back",
    )(user, part_key, part_value, use_grad)


def pick(selector, source):
    return jnp.einsum("ns,spw->npw", selector, source, preferred_element_type=F32).astype(BF16)


def local(queries, cotangent, database, w_key, w_value, neighbour_owner, neighbour_slot):
    peer_count = lax.axis_size("db")
    racks = lax.axis_size("rack")
    span_count, nbr_count = neighbour_owner.shape
    use_count = span_count * nbr_count
    local_rows, panel_len, width = database.shape
    rows = panel_len // racks
    owners = neighbour_owner.reshape(use_count)
    offsets = neighbour_slot.reshape(use_count)
    earlier = jnp.arange(use_count)[None, :] < jnp.arange(use_count)[:, None]
    ranked = jnp.sum(((owners[:, None] == owners[None, :]) & earlier).astype(jnp.int32), axis=1)
    target = owners * CAP + ranked
    named = (target[None, :] == jnp.arange(peer_count * CAP, dtype=jnp.int32)[:, None]).astype(jnp.int32)
    wanted = jnp.sum(named * (offsets - local_rows)[None, :], axis=1) + local_rows
    user = jnp.sum(named * (jnp.arange(use_count, dtype=jnp.int32) - use_count)[None, :], axis=1) + use_count
    asked_rows = lax.all_to_all(wanted.reshape(peer_count, CAP), "db", split_axis=0, concat_axis=0, tiled=True)
    own = lax.dynamic_slice_in_dim(database, lax.axis_index("rack") * rows, rows, 1)
    selector = (
        asked_rows.reshape(peer_count * CAP)[:, None] == jnp.arange(local_rows, dtype=jnp.int32)[None, :]
    ).astype(BF16)
    answer = pick(selector, own).reshape(peer_count, CAP, rows, width)
    arrived = lax.all_to_all(answer, "db", split_axis=0, concat_axis=0, tiled=True)
    placed = (target[:, None] == jnp.arange(peer_count * CAP, dtype=jnp.int32)[None, :]).astype(BF16)
    mine = pick(placed, arrived.reshape(peer_count * CAP, rows, width))
    panels = lax.all_gather(mine, "rack", axis=1, tiled=True)
    attended, grad_query, part_key, part_value, use_grad = block_call(panels, queries, cotangent, w_key, w_value, racks)
    full_key, full_value, returned = return_call(user, part_key, part_value, use_grad, peer_count)
    grad_w_key, grad_w_value = full_key.astype(F32), full_value.astype(F32)
    grad_database = pick(selector.T, returned.reshape(peer_count * CAP, rows, width))
    return attended, grad_query, grad_w_key, grad_w_value, grad_database


def solution(mesh):
    return jax.shard_map(
        local,
        mesh=mesh,
        in_specs=(
            P("db", "rack"), P("db", "rack"), P("db", None, None), P(None, "rack"), P(None, "rack"), P("db", None), P("db", None),
        ),
        out_specs=(P("db", "rack"), P("db", "rack"), P(None, "rack"), P(None, "rack"), P("db", "rack", None)),
        check_vma=False,
    )
```

```python
import functools

import jax
import jax.numpy as jnp
from jax import lax
from jax.experimental import pallas as pl
from jax.experimental.pallas import tpu as pltpu
from jax.sharding import PartitionSpec as P

HD = 128
SPAN = 64
CAP = 3
NT = (((1,), (1,)), ((), ()))
TN = (((0,), (0,)), ((), ()))
F32 = jnp.float32
BF16 = jnp.bfloat16


def dot(a, b):
    return jnp.dot(a, b, preferred_element_type=F32)


def block_kernel(spans, heads, panels, queries, cotangent, w_key, w_value, attended, grad_queries, part_key, part_value,
                 use_grad, flipped, rows_kv, grads_kv):
    step = pl.program_id(0)
    keys = panels.shape[0] // spans
    width = panels.shape[1]
    scale = HD ** -0.5

    @pl.when(step == 0)
    def _():
        for c in range(spans):
            flipped[:, c * keys:(c + 1) * keys] = panels[c * keys:(c + 1) * keys, :].T

    @pl.when(step < heads)
    def _():
        columns = pl.ds(pl.multiple_of(step * HD, HD), HD)
        weights = jnp.concatenate([w_key[:, columns], w_value[:, columns]], axis=1)
        half = spans // 2 * keys
        for part in range(2):
            rows_kv[part * half:(part + 1) * half, :] = dot(panels[part * half:(part + 1) * half, :], weights).astype(BF16)
        zero = jnp.zeros((SPAN, HD), BF16)
        for c in range(spans):
            tokens = slice(c * SPAN, (c + 1) * SPAN)
            own = slice(c * keys, (c + 1) * keys)
            query, grad = queries[tokens, :], cotangent[tokens, :]
            both = rows_kv[own, :]
            left = jnp.concatenate(
                [jnp.concatenate([query, zero], axis=1), jnp.concatenate([zero, grad], axis=1)], axis=0
            )
            pair = lax.dot_general(left, both, NT, preferred_element_type=F32)
            scores, grad_probs = pair[:SPAN] * scale, pair[SPAN:]
            raised = jnp.exp(scores - jnp.max(scores, axis=-1, keepdims=True))
            probs = raised / jnp.sum(raised, axis=-1, keepdims=True)
            delta = jnp.sum(probs * grad_probs, axis=-1, keepdims=True)
            grad_scores = (probs * (grad_probs - delta) * scale).astype(BF16)
            stacked = jnp.concatenate([probs.astype(BF16), grad_scores], axis=0)
            out = dot(stacked, both)
            attended[tokens, :] = out[:SPAN, HD:].astype(BF16)
            grad_queries[tokens, :] = out[SPAN:, :HD].astype(BF16)
            right = jnp.concatenate(
                [jnp.concatenate([zero, grad], axis=1), jnp.concatenate([query, zero], axis=1)], axis=0
            )
            grads_kv[step, own, :] = lax.dot_general(stacked, right, TN, preferred_element_type=F32).astype(BF16)
        total = dot(flipped[...], grads_kv[step]).astype(BF16)
        part_key[...] = total[:, :HD]
        part_value[...] = total[:, HD:]

    @pl.when(step >= heads)
    def _():
        c = step - heads
        own = pl.ds(pl.multiple_of(c * keys, keys), keys)
        total = jnp.zeros((keys, width), F32)
        for h in range(heads):
            columns = slice(h * HD, (h + 1) * HD)
            weights = jnp.concatenate([w_key[:, columns], w_value[:, columns]], axis=1)
            total = total + lax.dot_general(grads_kv[h, own, :], weights, NT, preferred_element_type=F32)
        total = total.astype(BF16)
        pieces, uses, rows = use_grad.shape[0], use_grad.shape[1], use_grad.shape[2]
        for n in range(uses):
            for r in range(pieces):
                first = (n * pieces + r) * rows
                use_grad[r, n, :, :] = total[first:first + rows, :]


def block_call(panels, queries, cotangent, w_key, w_value, racks):
    uses, panel_len, width = panels.shape
    spans = queries.shape[0] // SPAN
    features = w_key.shape[1]
    heads = features // HD
    per_span = uses // spans
    rows = panel_len // racks
    total = uses * panel_len
    once = dict(pipeline_mode=pl.Buffered(1))
    by_head = lambda size: pl.BlockSpec((size, HD), lambda i: (0, jnp.minimum(i, heads - 1)))
    whole = lambda a, b: pl.BlockSpec((a, b), lambda i: (0, 0), **once)

    return pl.pallas_call(
        functools.partial(block_kernel, spans, heads),
        grid=(heads + spans,),
        out_shape=(
            jax.ShapeDtypeStruct(queries.shape, BF16),
            jax.ShapeDtypeStruct(queries.shape, BF16),
            jax.ShapeDtypeStruct((width, features), BF16),
            jax.ShapeDtypeStruct((width, features), BF16),
            jax.ShapeDtypeStruct((racks, uses, rows, width), BF16),
        ),
        in_specs=[
            whole(total, width), by_head(queries.shape[0]), by_head(queries.shape[0]), whole(width, features), whole(width, features),
        ],
        out_specs=[
            by_head(queries.shape[0]), by_head(queries.shape[0]), by_head(width), by_head(width),
            pl.BlockSpec((racks, per_span, rows, width), lambda i: (0, jnp.maximum(i - heads, 0), 0, 0)),
        ],
        scratch_shapes=[
            pltpu.VMEM((width, total), BF16),
            pltpu.VMEM((total, 2 * HD), BF16),
            pltpu.VMEM((heads, total, 2 * HD), BF16),
        ],
        compiler_params=pltpu.CompilerParams(vmem_limit_bytes=56 * 1024 * 1024),
        cost_estimate=pl.CostEstimate(flops=6 * total * width * features * 2, bytes_accessed=24 << 20, transcendentals=1 << 20),
        name="block",
    )(panels.reshape(total, width), queries, cotangent, w_key, w_value)


MESH = pl.DeviceIdType.MESH


class Links:
    def __init__(self, side_z, side_y, side_x):
        db, rack = lax.axis_index("db"), lax.axis_index("rack")
        self.db, self.rack = db, rack
        self.z, self.y = db // side_y, db % side_y
        self.x, self.core = rack // 2, rack % 2
        self.side_x = side_x
        self.ids = {
            ("y", 1): (self.z * side_y + (self.y + 1) % side_y, rack),
            ("y", -1): (self.z * side_y + (self.y + side_y - 1) % side_y, rack),
            ("z", 1): ((self.z + 1) % side_z * side_y + self.y, rack),
            ("z", -1): ((self.z + side_z - 1) % side_z * side_y + self.y, rack),
            ("x", 1): (db, (self.x + 1) % side_x * 2 + self.core),
            ("x", -1): (db, (self.x + side_x - 1) % side_x * 2 + self.core),
            ("core", 1): (db, self.x * 2 + 1 - self.core),
        }

    def place(self, axis):
        return {"y": self.y, "z": self.z, "x": self.x}[axis]


class Mail:
    def __init__(self, send_sems, recv_sems, first=0):
        self.send_sems, self.recv_sems, self.next = send_sems, recv_sems, first
        self.open = {}
        self.sent = []

    def send(self, name, source, target, device):
        copy = pltpu.make_async_remote_copy(
            src_ref=source, dst_ref=target, send_sem=self.send_sems.at[self.next], recv_sem=self.recv_sems.at[self.next],
            device_id=device, device_id_type=MESH,
        )
        self.next += 1
        copy.start()
        self.open[name] = copy
        self.sent.append(copy)

    def arrive(self, *names):
        for name in names:
            self.open[name].wait_recv()

    def drain(self):
        for copy in self.sent:
            copy.wait_send()
        self.sent = []


def add(*terms):
    total = terms[0].astype(F32)
    for term in terms[1:]:
        total = total + term.astype(F32)
    return total.astype(BF16)


class Reduction:
    def __init__(self, tag, links, mail, part, full, first_column, columns, axes, near, far, middle):
        self.tag, self.links, self.mail = tag, links, mail
        self.part, self.full, self.first_column, self.columns = part, full, first_column, columns
        self.one, self.two = axes
        self.near, self.far, self.middle = near, far, middle
        self.rows = part.shape[0] // 4
        self.half = self.rows // 2
        self.narrow = columns // 4

    def name(self, what):
        return (self.tag, what)

    def spot(self, ref, one, side):
        first = one * self.rows + side * self.half
        return ref.at[pl.ds(pl.multiple_of(first, 16), self.half), pl.ds(self.first_column, self.columns)]

    def small(self, two, side):
        return self.middle.at[pl.ds(side * self.half, self.half), pl.ds(pl.multiple_of(two * self.narrow, 128), self.narrow)]

    def piece(self, one, two, first, size):
        return self.full.at[
            pl.ds(pl.multiple_of(one * self.rows + first, 16), size),
            pl.ds(pl.multiple_of(self.first_column + two * self.narrow, 128), self.narrow),
        ]

    def first(self, axis, at, buffer, level):
        links, mail, me = self.links, self.mail, self.links.place(axis)
        up, down = links.ids[(axis, 1)], links.ids[(axis, -1)]
        mail.send(self.name(level + "ra"), at((me + 2) % 4, 0), buffer.at[0], up)
        mail.send(self.name(level + "rb"), at((me + 2) % 4, 1), buffer.at[1], down)
        mail.send(self.name(level + "db"), at((me + 1) % 4, 1), buffer.at[3], up)
        mail.send(self.name(level + "da"), at((me + 3) % 4, 0), buffer.at[2], down)

    def second(self, axis, at, buffer, level):
        links, mail, me = self.links, self.mail, self.links.place(axis)
        up, down = links.ids[(axis, 1)], links.ids[(axis, -1)]
        mail.arrive(self.name(level + "ra"))
        buffer[0, :, :] = add(buffer[0], at((me + 1) % 4, 0)[...])
        mail.send(self.name(level + "sa"), buffer.at[0], buffer.at[4], up)
        mail.arrive(self.name(level + "rb"))
        buffer[1, :, :] = add(buffer[1], at((me + 3) % 4, 1)[...])
        mail.send(self.name(level + "sb"), buffer.at[1], buffer.at[5], down)

    def third(self, axis, at, buffer, level, side):
        mail, me = self.mail, self.links.place(axis)
        letter = "ab"[side]
        mail.arrive(self.name(level + "d" + letter), self.name(level + "s" + letter))
        return add(buffer[2 + side], buffer[4 + side], at(me, side)[...])

    def spread(self, axis, at, level):
        links, mail, me = self.links, self.mail, self.links.place(axis)
        mail.send(self.name(level + "up"), at(me, 0, self.rows), at(me, 0, self.rows), links.ids[(axis, 1)])
        mail.send(self.name(level + "down"), at(me, 0, self.rows), at(me, 0, self.rows), links.ids[(axis, -1)])

    def forward(self, axis, at, level):
        links, mail, me = self.links, self.mail, self.links.place(axis)
        mail.arrive(self.name(level + "up"))
        mail.send(
            self.name(level + "on"), at((me + 3) % 4, 0, self.half), at((me + 3) % 4, 0, self.half), links.ids[(axis, 1)]
        )
        mail.arrive(self.name(level + "down"))
        mail.send(
            self.name(level + "back"), at((me + 1) % 4, self.half, self.half), at((me + 1) % 4, self.half, self.half),
            links.ids[(axis, -1)],
        )

    def stage(self, number):
        wide = lambda one, side: self.spot(self.part, one, side)
        mine = self.links.place(self.one)
        column = lambda two, first, size: self.piece(mine, two, first, size)
        row = lambda one, first, size: self.full.at[
            pl.ds(pl.multiple_of(one * self.rows + first, 16), size), pl.ds(self.first_column, self.columns)
        ]
        if number == 0:
            self.first(self.one, wide, self.near, "n")
        elif number == 1:
            self.second(self.one, wide, self.near, "n")
        elif number == 2:
            for side in (0, 1):
                self.middle[side * self.half:(side + 1) * self.half, :] = self.third(self.one, wide, self.near, "n", side)
            self.first(self.two, self.small, self.far, "f")
        elif number == 3:
            self.second(self.two, self.small, self.far, "f")
        elif number == 4:
            for side in (0, 1):
                total = self.third(self.two, self.small, self.far, "f", side)
                column(self.links.place(self.two), side * self.half, self.half)[...] = total
            self.spread(self.two, column, "g")
        elif number == 5:
            self.forward(self.two, column, "g")
        elif number == 6:
            self.mail.arrive(self.name("gon"), self.name("gback"))
            self.spread(self.one, row, "h")
        elif number == 7:
            self.forward(self.one, row, "h")
        else:
            self.mail.arrive(self.name("hon"), self.name("hback"))


class Return:
    def __init__(self, links, mail, use_grad, user, returned, crossed, ring, mine, leaving, leave_sems, land_sems):
        self.links, self.mail, self.use_grad, self.user, self.returned = links, mail, use_grad, user, returned
        self.crossed, self.ring, self.mine, self.leaving = crossed, ring, mine, leaving
        self.leave_sems, self.land_sems = leave_sems, land_sems
        self.half = mine.shape[0] // 2

    def spot(self, far, side):
        return self.crossed.at[(self.links.x + far) % 4, pl.ds(side * self.half, self.half)]

    def stage(self, number):
        links, mail = self.links, self.mail
        up, down = links.ids[("x", 1)], links.ids[("x", -1)]
        half = self.half
        if number == 0:
            for far in (2, 1, 3, 0):
                x = (links.x + far) % 4
                mail.send(("c", far), self.use_grad.at[x * 2 + 1 - links.core], self.crossed.at[x], links.ids[("core", 1)])
        elif number == 1:
            def join(far):
                x = (links.x + far) % 4
                mail.arrive(("c", far))

                @pl.loop(0, half * 2)
                def _(n):
                    self.crossed[x, n] = add(self.crossed[x, n], self.use_grad[x * 2 + links.core, n])

            join(2)
            mail.send("xra", self.spot(2, 0), self.ring.at[0], up)
            mail.send("xrb", self.spot(2, 1), self.ring.at[1], down)
            join(1)
            mail.send("xdb", self.spot(1, 1), self.ring.at[3], up)
            join(3)
            mail.send("xda", self.spot(3, 0), self.ring.at[2], down)
            join(0)
        elif number == 2:
            for side, letter, far, device in ((0, "a", 1, up), (1, "b", 3, down)):
                mail.arrive("xr" + letter)
                own = self.spot(far, side)

                @pl.loop(0, half)
                def _(n):
                    self.ring[side, n] = add(self.ring[side, n], own[n])

                mail.send("xs" + letter, self.ring.at[side], self.ring.at[4 + side], device)
        elif number == 3:
            for side, letter in ((0, "a"), (1, "b")):
                mail.arrive("xd" + letter, "xs" + letter)
                own = self.spot(0, side)

                @pl.loop(0, half)
                def _(n):
                    self.mine[side * half + n] = add(self.ring[2 + side, n], self.ring[4 + side, n], own[n])

            self.mine[2 * half] = jnp.zeros(self.mine.shape[1:], BF16)
            peers = self.returned.shape[0]

            def fill(peer, target, at):
                for k in range(CAP):
                    target[at, k] = self.mine[self.user[peer, 0, k]]

            fill(links.db, self.returned, links.db)

            @pl.loop(1, peers)
            def _(far):
                peer = (links.db + far) % peers
                fill(peer, self.leaving, peer)
                self.copy(far).start()
        else:
            @pl.loop(1, self.returned.shape[0])
            def _(far):
                self.copy(far).wait()

    def copy(self, far):
        links = self.links
        peer = (links.db + far) % self.returned.shape[0]
        return pltpu.make_async_remote_copy(
            src_ref=self.leaving.at[peer], dst_ref=self.returned.at[links.db], send_sem=self.leave_sems.at[far],
            recv_sem=self.land_sems.at[far], device_id=(peer, links.rack), device_id_type=MESH,
        )


def greet(links, peers):
    barrier = pltpu.get_barrier_semaphore()
    others = [links.ids[("core", 1)], links.ids[("x", 1)], links.ids[("x", -1)]]
    for device in others:
        pl.semaphore_signal(barrier, inc=1, device_id=device, device_id_type=MESH)

    @pl.loop(1, peers)
    def _(far):
        pl.semaphore_signal(barrier, inc=1, device_id=((links.db + far) % peers, links.rack), device_id_type=MESH)

    pl.semaphore_wait(barrier, len(others) + peers - 1)


GROUPS = 2
MESSAGES = 20 * 2 * GROUPS + 10


def return_kernel(user, part_key, part_value, use_grad, full_key, full_value, returned, near, far, middle, crossed, ring, mine,
                  leaving, send_sems, recv_sems, leave_sems, land_sems):
    links = Links(4, 4, 4)
    greet(links, returned.shape[0])
    mail = Mail(send_sems, recv_sems)
    columns = part_key.shape[1] // GROUPS
    items = []
    for g in range(GROUPS):
        for m, (part, full, axes) in enumerate(((part_key, full_key, "yz"), (part_value, full_value, "zy"))):
            n = g * 2 + m
            items.append(Reduction(n, links, mail, part, full, g * columns, columns, axes, near.at[n], far.at[n], middle.at[n]))
    back = Return(links, mail, use_grad, user, returned, crossed, ring, mine, leaving, leave_sems, land_sems)
    back.stage(0)
    for item in items:
        item.stage(0)
    back.stage(1)
    for item in items[:2]:
        item.stage(1)
    back.stage(2)
    for item in items[:2]:
        item.stage(2)
    for item in items[2:]:
        item.stage(1)
    back.stage(3)
    for item in items[:2]:
        item.stage(3)
    for item in items[2:]:
        item.stage(2)
    for number in (4, 5, 6, 7, 8):
        for item in items[:2]:
            item.stage(number)
        for item in items[2:]:
            item.stage(number - 1)
    for item in items[2:]:
        item.stage(8)
    back.stage(4)
    mail.drain()


def return_call(user, part_key, part_value, use_grad, peers):
    width, features = part_key.shape
    racks, uses, rows, _ = use_grad.shape
    columns = features // GROUPS
    vmem = pl.BlockSpec(memory_space=pltpu.VMEM)
    return pl.pallas_call(
        return_kernel,
        out_shape=(
            jax.ShapeDtypeStruct((width, features), BF16),
            jax.ShapeDtypeStruct((width, features), BF16),
            jax.ShapeDtypeStruct((peers, CAP, rows, width), BF16),
        ),
        in_specs=[pl.BlockSpec(memory_space=pltpu.SMEM), vmem, vmem, vmem],
        out_specs=(vmem, vmem, vmem),
        scratch_shapes=[
            pltpu.VMEM((2 * GROUPS, 6, width // 8, columns), BF16),
            pltpu.VMEM((2 * GROUPS, 6, width // 8, columns // 4), BF16),
            pltpu.VMEM((2 * GROUPS, width // 4, columns), BF16),
            pltpu.VMEM((4, uses, rows, width), BF16),
            pltpu.VMEM((6, uses // 2, rows, width), BF16),
            pltpu.VMEM((uses + 1, rows, width), BF16),
            pltpu.VMEM((peers, CAP, rows, width), BF16),
            pltpu.SemaphoreType.DMA((MESSAGES,)),
            pltpu.SemaphoreType.DMA((MESSAGES,)),
            pltpu.SemaphoreType.DMA((peers,)),
            pltpu.SemaphoreType.DMA((peers,)),
        ],
        compiler_params=pltpu.CompilerParams(
            collective_id=1, has_side_effects=True, vmem_limit_bytes=48 * 1024 * 1024
        ),
        name="send_back",
    )(user, part_key, part_value, use_grad)


def fetch_kernel(cuts, owners, slots, database, panels, asked, user, stored, wanted, heard, leaving, landing, mine, load_sem, ask_send,
                 ask_recv, leave_sems, land_sems, own_sems, send_sems, recv_sems):
    links = Links(4, 4, 4)
    peers = asked.shape[0]
    local_rows, _, width = stored.shape
    uses, rows = mine.shape[0], mine.shape[1]
    nbrs = owners.shape[1]
    my_rows = lambda x, core: pl.ds(pl.multiple_of((x * 2 + core) * rows, rows), rows)
    load = pltpu.make_async_copy(database.at[:, my_rows(links.x, links.core), :], stored, load_sem.at[0])
    load.start()
    greet(links, peers)

    peer_of = lax.broadcasted_iota(jnp.int32, (peers, 1, 128), 0)
    lane = lax.broadcasted_iota(jnp.int32, (peers, 1, 128), 2)
    seen = jnp.zeros((peers, 1, 128), jnp.int32)
    rows_wanted = jnp.full((peers, 1, 128), local_rows, jnp.int32)
    users = jnp.full((peers, 1, 128), uses, jnp.int32)
    for u in range(uses):
        named = peer_of == owners[u // nbrs, u % nbrs]
        here = named & (lane == seen)
        rows_wanted = jnp.where(here, slots[u // nbrs, u % nbrs], rows_wanted)
        users = jnp.where(here, u, users)
        seen = seen + named.astype(jnp.int32)
    wanted[...] = rows_wanted
    user[...] = users

    def ask(far):
        peer = (links.db + far) % peers
        return pltpu.make_async_remote_copy(
            src_ref=wanted.at[peer], dst_ref=asked.at[links.db], send_sem=ask_send.at[far], recv_sem=ask_recv.at[far],
            device_id=(peer, links.rack), device_id_type=MESH,
        )

    pl.loop(1, peers)(lambda far: ask(far).start())
    asked[links.db] = wanted[links.db]
    load.wait()
    pl.loop(1, peers)(lambda far: ask(far).wait())
    tables = pltpu.make_async_copy(asked, heard, load_sem.at[1])
    tables.start()
    tables.wait()

    def answer(c, far):
        peer = (links.db + far) % peers
        return pltpu.make_async_remote_copy(
            src_ref=leaving[c].at[peer], dst_ref=landing[c].at[links.db], send_sem=leave_sems.at[c, far],
            recv_sem=land_sems.at[c, far], device_id=(peer, links.rack), device_id_type=MESH,
        )

    def fill(c, peer, target):
        for k in range(CAP):
            row = jnp.minimum(heard[peer, 0, k], local_rows - 1)
            target[peer, k] = stored[row, :, cuts[c]:cuts[c + 1]]

    for c in range(len(cuts) - 1):
        @pl.loop(1, peers)
        def _(far):
            fill(c, (links.db + far) % peers, leaving[c])
            answer(c, far).start()

        fill(c, links.db, landing[c])

    mail = Mail(send_sems, recv_sems)
    up, down, across = links.ids[("x", 1)], links.ids[("x", -1)], links.ids[("core", 1)]
    own_copies = []
    half = uses // 2

    def out(c, far, first, size):
        return panels.at[pl.ds(first, size), my_rows((links.x + far) % 4, links.core), pl.ds(cuts[c], cuts[c + 1] - cuts[c])]

    def pass_on(name, c, far, first, size, device):
        mail.send((name, c), out(c, far, first, size), out(c, far, first, size), device)

    def exchange(c):
        mail.arrive(("up", c))
        pass_on("on", c, 3, 0, half, up)
        pass_on("cross3", c, 3, 0, uses, across)
        mail.arrive(("down", c))
        pass_on("back", c, 1, half, half, down)
        pass_on("cross1", c, 1, 0, uses, across)

    def finish(c):
        mail.arrive(("on", c))
        pass_on("cross2a", c, 2, 0, half, across)
        mail.arrive(("back", c))
        pass_on("cross2b", c, 2, half, half, across)

    count = len(cuts) - 1
    for c in range(count):
        pl.loop(1, peers)(lambda far: answer(c, far).wait())
        for u in range(uses):
            owner = owners[u // nbrs, u % nbrs]
            rank = jnp.int32(0)
            for v in range(u):
                rank = rank + (owners[v // nbrs, v % nbrs] == owner).astype(jnp.int32)
            mine[u, :, cuts[c]:cuts[c + 1]] = landing[c][owner, jnp.minimum(rank, CAP - 1)]
        source = mine.at[:, :, pl.ds(cuts[c], cuts[c + 1] - cuts[c])]
        target = out(c, 0, 0, uses)
        mail.send(("up", c), source, target, up)
        mail.send(("down", c), source, target, down)
        mail.send(("cross0", c), source, target, across)
        copy = pltpu.make_async_copy(source, target, own_sems.at[c])
        copy.start()
        own_copies.append(copy)
        if c > 0:
            exchange(c - 1)
    exchange(count - 1)
    for c in range(count):
        finish(c)
    for c in range(count):
        mail.arrive(("cross0", c), ("cross1", c), ("cross3", c), ("cross2a", c), ("cross2b", c))
    for copy in own_copies:
        copy.wait()
    mail.drain()


CUTS = (0, 512, 896)


def fetch_call(owners, slots, database, peers, racks):
    uses = owners.shape[0] * owners.shape[1]
    local_rows, panel_len, width = database.shape
    rows = panel_len // racks
    parts = len(CUTS) - 1
    chunk = lambda c: pltpu.VMEM((peers, CAP, rows, CUTS[c + 1] - CUTS[c]), BF16)
    vmem = pl.BlockSpec(memory_space=pltpu.VMEM)
    smem = pl.BlockSpec(memory_space=pltpu.SMEM)
    anywhere = pl.BlockSpec(memory_space=pl.ANY)
    sems = pltpu.SemaphoreType.DMA
    return pl.pallas_call(
        functools.partial(fetch_kernel, CUTS),
        out_shape=(
            jax.ShapeDtypeStruct((uses, panel_len, width), BF16),
            jax.ShapeDtypeStruct((peers, 1, 128), jnp.int32),
            jax.ShapeDtypeStruct((peers, 1, 128), jnp.int32),
        ),
        in_specs=[smem, smem, anywhere],
        out_specs=(anywhere, vmem, vmem),
        scratch_shapes=[
            pltpu.VMEM((local_rows, rows, width), BF16),
            pltpu.VMEM((peers, 1, 128), jnp.int32),
            pltpu.SMEM((peers, 1, 128), jnp.int32),
            [chunk(c) for c in range(parts)],
            [chunk(c) for c in range(parts)],
            pltpu.VMEM((uses, rows, width), BF16),
            sems((2,)), sems((peers,)), sems((peers,)), sems((parts, peers)), sems((parts, peers)), sems((parts,)),
            sems((9 * parts,)), sems((9 * parts,)),
        ],
        compiler_params=pltpu.CompilerParams(
            collective_id=0, has_side_effects=True, vmem_limit_bytes=24 * 1024 * 1024
        ),
        name="fetch",
    )(owners, slots, database)


def pick(selector, source):
    return jnp.einsum("ns,spw->npw", selector, source, preferred_element_type=F32).astype(BF16)


def local(queries, cotangent, database, w_key, w_value, neighbour_owner, neighbour_slot):
    peer_count = lax.axis_size("db")
    racks = lax.axis_size("rack")
    local_rows, _, width = database.shape
    rows = database.shape[1] // racks
    panels, asked, user = fetch_call(neighbour_owner, neighbour_slot, database, peer_count, racks)
    asked_rows = asked[:, 0, :CAP].reshape(peer_count * CAP)
    selector = (asked_rows[:, None] == jnp.arange(local_rows, dtype=jnp.int32)[None, :]).astype(BF16)
    attended, grad_query, part_key, part_value, use_grad = block_call(panels, queries, cotangent, w_key, w_value, racks)
    full_key, full_value, returned = return_call(user, part_key, part_value, use_grad, peer_count)
    grad_w_key, grad_w_value = full_key.astype(F32), full_value.astype(F32)
    grad_database = pick(selector.T, returned.reshape(peer_count * CAP, rows, width))
    return attended, grad_query, grad_w_key, grad_w_value, grad_database


def solution(mesh):
    return jax.shard_map(
        local,
        mesh=mesh,
        in_specs=(
            P("db", "rack"), P("db", "rack"), P("db", None, None), P(None, "rack"), P(None, "rack"), P("db", None), P("db", None),
        ),
        out_specs=(P("db", "rack"), P("db", "rack"), P(None, "rack"), P(None, "rack"), P("db", "rack", None)),
        check_vma=False,
    )
```

```python
import functools

import jax
import jax.numpy as jnp
from jax import lax
from jax.experimental import pallas as pl
from jax.experimental.pallas import tpu as pltpu
from jax.sharding import PartitionSpec as P

HD = 128
SPAN = 64
CAP = 3
PARTS = 2
GPARTS = 2
NT = (((1,), (1,)), ((), ()))
TN = (((0,), (0,)), ((), ()))
F32 = jnp.float32
BF16 = jnp.bfloat16


def dot(a, b):
    return jnp.dot(a, b, preferred_element_type=F32)


MESH = pl.DeviceIdType.MESH


class Links:
    def __init__(self, side_z, side_y, side_x):
        db, rack = lax.axis_index("db"), lax.axis_index("rack")
        self.db, self.rack = db, rack
        self.z, self.y = db // side_y, db % side_y
        self.x, self.core = rack // 2, rack % 2
        self.side_x = side_x
        self.ids = {
            ("y", 1): (self.z * side_y + (self.y + 1) % side_y, rack),
            ("y", -1): (self.z * side_y + (self.y + side_y - 1) % side_y, rack),
            ("z", 1): ((self.z + 1) % side_z * side_y + self.y, rack),
            ("z", -1): ((self.z + side_z - 1) % side_z * side_y + self.y, rack),
            ("x", 1): (db, (self.x + 1) % side_x * 2 + self.core),
            ("x", -1): (db, (self.x + side_x - 1) % side_x * 2 + self.core),
            ("core", 1): (db, self.x * 2 + 1 - self.core),
        }

    def place(self, axis):
        return {"y": self.y, "z": self.z, "x": self.x}[axis]


class Mail:
    def __init__(self, send_sems, recv_sems):
        self.send_sems, self.recv_sems, self.book = send_sems, recv_sems, {}

    def plan(self, name, source, target, device):
        self.book[name] = (len(self.book), source, target, device)

    def copy(self, name):
        n, source, target, device = self.book[name]
        return pltpu.make_async_remote_copy(
            src_ref=source(), dst_ref=target(), send_sem=self.send_sems.at[n], recv_sem=self.recv_sems.at[n], device_id=device,
            device_id_type=MESH,
        )

    def start(self, *names):
        for name in names:
            self.copy(name).start()

    def arrive(self, *names):
        for name in names:
            self.copy(name).wait_recv()

    def settle(self):
        for name in self.book:
            self.copy(name).wait_send()


def greet(links, peers):
    barrier = pltpu.get_barrier_semaphore()
    others = [links.ids[("core", 1)], links.ids[("x", 1)], links.ids[("x", -1)]]
    for device in others:
        pl.semaphore_signal(barrier, inc=1, device_id=device, device_id_type=MESH)

    @pl.loop(1, peers)
    def _(far):
        pl.semaphore_signal(barrier, inc=1, device_id=((links.db + far) % peers, links.rack), device_id_type=MESH)

    return len(others) + peers - 1


def add(*terms):
    total = terms[0].astype(F32)
    for term in terms[1:]:
        total = total + term.astype(F32)
    return total.astype(BF16)


class Reduction:
    def __init__(self, tag, links, mail, part, full, first_column, columns, axes, near, far, middle):
        self.tag, self.links, self.mail = tag, links, mail
        self.part, self.full, self.first_column, self.columns = part, full, first_column, columns
        self.near, self.far, self.middle = near, far, middle
        self.rows = part.shape[0] // 4
        self.places = [links.place(axis) for axis in axes]
        self.across = columns // 128
        self.short = self.rows * self.across // 4
        self.sides = [(0, self.rows // 32 * 16), (self.rows // 32 * 16, self.rows - self.rows // 32 * 16)]
        whole = (self.short + 31) // 32 * 16
        self.bits = [(0, whole), (whole, self.short - whole)]
        up = [links.ids[(axis, 1)] for axis in axes]
        down = [links.ids[(axis, -1)] for axis in axes]
        one, two = self.places
        for level, at, buffer, sides, me, k in (("n", self.wide, near, self.sides, one, 0), ("f", self.small, far, self.bits, two, 1)):
            lot = lambda ref, slot, side, sides=sides: (lambda: ref.at[slot, pl.ds(0, sides[side][1])])
            spot = lambda far_off, side, at=at, me=me: (lambda: at((me + far_off) % 4, side))
            self.plan(level + "ra", spot(2, 0), lot(buffer, 0, 0), up[k])
            self.plan(level + "rb", spot(2, 1), lot(buffer, 1, 1), down[k])
            self.plan(level + "db", spot(1, 1), lot(buffer, 3, 1), up[k])
            self.plan(level + "da", spot(3, 0), lot(buffer, 2, 0), down[k])
            self.plan(level + "sa", lot(buffer, 0, 0), lot(buffer, 4, 0), up[k])
            self.plan(level + "sb", lot(buffer, 1, 1), lot(buffer, 5, 1), down[k])
        for level, at, sides, size, me, k in (("g", self.piece, self.bits, self.short, two, 1), ("h", self.band, self.sides, self.rows, one, 0)):
            spot = lambda far_off, first, size, at=at, me=me: (lambda: at((me + far_off) % 4, first, size))
            for name, far_off, (first, length), device in (
                ("up", 0, (0, size), up[k]), ("down", 0, (0, size), down[k]), ("on", 3, sides[0], up[k]), ("back", 1, sides[1], down[k]),
            ):
                self.plan(level + name, spot(far_off, first, length), spot(far_off, first, length), device)

    def plan(self, name, source, target, device):
        self.mail.plan((self.tag, name), source, target, device)

    def start(self, *names):
        self.mail.start(*[(self.tag, name) for name in names])

    def arrive(self, *names):
        self.mail.arrive(*[(self.tag, name) for name in names])

    def wide(self, one, side):
        first, size = self.sides[side]
        return self.part.at[pl.ds(pl.multiple_of(one * self.rows + first, 16), size), pl.ds(self.first_column, self.columns)]

    def small(self, two, side):
        first, size = self.bits[side]
        return self.middle.at[
            pl.ds(pl.multiple_of(two // self.across * self.short + first, 16), size),
            pl.ds(pl.multiple_of(two % self.across * 128, 128), 128),
        ]

    def piece(self, two, first, size):
        row = self.places[0] * self.rows + two // self.across * self.short + first
        column = self.first_column + two % self.across * 128
        return self.full.at[pl.ds(pl.multiple_of(row, 16), size), pl.ds(pl.multiple_of(column, 128), 128)]

    def band(self, one, first, size):
        return self.full.at[pl.ds(pl.multiple_of(one * self.rows + first, 16), size), pl.ds(self.first_column, self.columns)]

    def join(self, level, at, buffer, sides, me):
        for side, letter, far_off in ((0, "a", 1), (1, "b", 3)):
            size = sides[side][1]
            self.arrive(level + "r" + letter)
            buffer[side, :size] = add(buffer[side, :size], at((me + far_off) % 4, side)[...])
            self.start(level + "s" + letter)

    def total(self, level, at, buffer, sides, me, side):
        letter, size = "ab"[side], sides[side][1]
        self.arrive(level + "d" + letter, level + "s" + letter)
        return add(buffer[2 + side, :size], buffer[4 + side, :size], at(me, side)[...])

    def stage(self, number):
        one, two = self.places
        if number == 0:
            self.start("nra", "nrb", "ndb", "nda")
        elif number == 1:
            self.join("n", self.wide, self.near, self.sides, one)
        elif number == 2:
            for side, (first, size) in enumerate(self.sides):
                self.middle[first:first + size, :] = self.total("n", self.wide, self.near, self.sides, one, side)
            self.start("fra", "frb", "fdb", "fda")
        elif number == 3:
            self.join("f", self.small, self.far, self.bits, two)
        elif number == 4:
            for side, (first, size) in enumerate(self.bits):
                self.piece(two, first, size)[...] = self.total("f", self.small, self.far, self.bits, two, side)
            self.start("gup", "gdown")
        elif number == 6:
            self.arrive("gon", "gback")
            self.start("hup", "hdown")
        elif number == 8:
            self.arrive("hon", "hback")
        else:
            level = "g" if number == 5 else "h"
            self.arrive(level + "up")
            self.start(level + "on")
            self.arrive(level + "down")
            self.start(level + "back")


class Return:
    def __init__(self, links, mail, use_grad, user, returned, crossed, ring, mine, leaving, leave_sems, land_sems):
        self.links, self.mail, self.use_grad, self.user, self.returned = links, mail, use_grad, user, returned
        self.crossed, self.ring, self.mine, self.leaving = crossed, ring, mine, leaving
        self.leave_sems, self.land_sems = leave_sems, land_sems
        self.half = mine.shape[0] // 2
        up, down, across = links.ids[("x", 1)], links.ids[("x", -1)], links.ids[("core", 1)]
        for side in (0, 1):
            for far_off in (2, 1, 3, 0):
                mail.plan(("c", far_off, side), self.partner(far_off, side), self.spot(far_off, side), across)
        slot = lambda n: (lambda: ring.at[n])
        mail.plan("xra", self.spot(2, 0), slot(0), up)
        mail.plan("xda", self.spot(3, 0), slot(2), down)
        mail.plan("xrb", self.spot(2, 1), slot(1), down)
        mail.plan("xdb", self.spot(1, 1), slot(3), up)
        mail.plan("xsa", slot(0), slot(4), up)
        mail.plan("xsb", slot(1), slot(5), down)

    def uses(self, side):
        return pl.ds(side * self.half, self.half)

    def spot(self, far_off, side):
        return lambda: self.crossed.at[(self.links.x + far_off) % 4, self.uses(side)]

    def partner(self, far_off, side):
        return lambda: self.use_grad.at[(self.links.x + far_off) % 4 * 2 + 1 - self.links.core, self.uses(side)]

    def cross(self, side):
        self.mail.start(*[("c", far_off, side) for far_off in (2, 1, 3, 0)])

    def ring_out(self, side):
        links, mail, half = self.links, self.mail, self.half
        first, second = (("xra", 2), ("xda", 3)) if side == 0 else (("xrb", 2), ("xdb", 1))
        for name, far_off in (first, second, (None, 1 if side == 0 else 3), (None, 0)):
            x = (links.x + far_off) % 4
            mail.arrive(("c", far_off, side))

            @pl.loop(side * half, (side + 1) * half)
            def _(n):
                self.crossed[x, n] = add(self.crossed[x, n], self.use_grad[x * 2 + links.core, n])

            if name:
                mail.start(name)

    def ring_on(self, side):
        letter, far_off = ("a", 1) if side == 0 else ("b", 3)
        self.mail.arrive("xr" + letter)
        own = self.spot(far_off, side)()

        @pl.loop(0, self.half)
        def _(n):
            self.ring[side, n] = add(self.ring[side, n], own[n])

        self.mail.start("xs" + letter)

    def ring_end(self, side):
        letter = "ab"[side]
        self.mail.arrive("xd" + letter, "xs" + letter)
        own = self.spot(0, side)()

        @pl.loop(0, self.half)
        def _(n):
            self.mine[side * self.half + n] = add(self.ring[2 + side, n], self.ring[4 + side, n], own[n])

    def post(self):
        links, peers = self.links, self.returned.shape[0]
        self.mine[2 * self.half] = jnp.zeros(self.mine.shape[1:], BF16)

        def fill(peer, target):
            for k in range(CAP):
                target[peer, k] = self.mine[self.user[peer, 0, k]]

        @pl.loop(1, peers)
        def _(far_off):
            fill((links.db + far_off) % peers, self.leaving)
            self.copy(far_off).start()

        fill(links.db, self.returned)

    def received(self):
        pl.loop(1, self.returned.shape[0])(lambda far_off: self.copy(far_off).wait())

    def copy(self, far_off):
        links = self.links
        peer = (links.db + far_off) % self.returned.shape[0]
        return pltpu.make_async_remote_copy(
            src_ref=self.leaving.at[peer], dst_ref=self.returned.at[links.db], send_sem=self.leave_sems.at[far_off],
            recv_sem=self.land_sems.at[far_off], device_id=(peer, links.rack), device_id_type=MESH,
        )


def block_step(step, spans, heads, panels, queries, cotangent, w_key, w_value, attended, grad_queries, part_key, part_value,
               use_grad, flipped, rows_kv, grads_kv, left, right, pair, stacked, wide):
    keys = panels.shape[0] // spans
    width = panels.shape[1]
    scale = HD ** -0.5

    @pl.when(step == 0)
    def _():
        left[...] = jnp.zeros_like(left)
        right[...] = jnp.zeros_like(right)
        for c in range(spans):
            flipped[:, c * keys:(c + 1) * keys] = panels[c * keys:(c + 1) * keys, :].T

    @pl.when(step < heads)
    def _():
        columns = pl.ds(pl.multiple_of(step * HD, HD), HD)
        wide[:, :HD] = w_key[:, columns]
        wide[:, HD:] = w_value[:, columns]

        @pl.loop(0, PARTS)
        def _(n):
            size = panels.shape[0] // PARTS
            at = pl.ds(pl.multiple_of(n * size, size), size)
            rows_kv[at, :] = dot(panels[at, :], wide[...]).astype(BF16)

        for c in range(spans):
            tokens = slice(c * SPAN, (c + 1) * SPAN)
            query, grad = queries[tokens, :], cotangent[tokens, :]
            left[c, :SPAN, :HD] = query
            left[c, SPAN:, HD:] = grad
            right[c, :SPAN, HD:] = grad
            right[c, SPAN:, :HD] = query
        for c in range(spans):
            pair[c] = lax.dot_general(left[c], rows_kv[c * keys:(c + 1) * keys, :], NT, preferred_element_type=F32)
        for c in range(spans):
            scores = pair[c, :SPAN] * scale
            raised = jnp.exp(scores - jnp.max(scores, axis=-1, keepdims=True))
            probs = raised * (1.0 / jnp.sum(raised, axis=-1, keepdims=True))
            stacked[c, :SPAN] = probs.astype(BF16)
            grad_probs = pair[c, SPAN:]
            delta = jnp.sum(probs * grad_probs, axis=-1, keepdims=True)
            stacked[c, SPAN:] = (probs * (grad_probs - delta) * scale).astype(BF16)
        for c in range(spans):
            tokens = slice(c * SPAN, (c + 1) * SPAN)
            own = slice(c * keys, (c + 1) * keys)
            out = dot(stacked[c], rows_kv[own, :])
            attended[tokens, :] = out[:SPAN, HD:].astype(BF16)
            grad_queries[tokens, :] = out[SPAN:, :HD].astype(BF16)
        for c in range(spans):
            own = slice(c * keys, (c + 1) * keys)
            grads_kv[step, own, :] = lax.dot_general(stacked[c], right[c], TN, preferred_element_type=F32).astype(BF16)

        @pl.loop(0, GPARTS)
        def _(n):
            size = width // GPARTS
            at = pl.ds(pl.multiple_of(n * size, size), size)
            total = dot(flipped[at, :], grads_kv[step]).astype(BF16)
            part_key[at, columns] = total[:, :HD]
            part_value[at, columns] = total[:, HD:]

    @pl.when(step >= heads)
    def _():
        c = step - heads
        own = pl.ds(pl.multiple_of(c * keys, keys), keys)
        total = jnp.zeros((keys, width), F32)
        for h in range(heads):
            columns = slice(h * HD, (h + 1) * HD)
            weights = jnp.concatenate([w_key[:, columns], w_value[:, columns]], axis=1)
            total = total + lax.dot_general(grads_kv[h, own, :], weights, NT, preferred_element_type=F32)
        total = total.astype(BF16)
        pieces, uses, rows = use_grad.shape[0], use_grad.shape[1] // spans, use_grad.shape[2]
        for n in range(uses):
            for r in range(pieces):
                first = (n * pieces + r) * rows
                use_grad[r, c * uses + n, :, :] = total[first:first + rows, :]


GROUPS = 4


def block_kernel(spans, heads, user, panels, queries, cotangent, w_key, w_value, attended, grad_queries, out_key, out_value,
                 out_returned, full_key, full_value, returned, flipped, rows_kv, grads_kv, left, right, pair, stacked, wide, part_key, part_value, use_grad, near, far,
                 middle, crossed, ring, mine, leaving, send_sems, recv_sems, leave_sems, land_sems, out_sems):
    step = pl.program_id(0)
    links = Links(4, 4, 4)
    mail = Mail(send_sems, recv_sems)
    columns = part_key.shape[1] // GROUPS
    items = []
    for g in range(GROUPS):
        for m, (part, full, axes) in enumerate(((part_key, full_key, "yz"), (part_value, full_value, "zy"))):
            n = g * 2 + m
            items.append(Reduction(n, links, mail, part, full, g * columns, columns, axes, near.at[n], far.at[n], middle.at[n]))
    back = Return(links, mail, use_grad, user, returned, crossed, ring, mine, leaving, leave_sems, land_sems)

    def advance(*moves):
        for g, number in moves:
            items[2 * g].stage(number)
            items[2 * g + 1].stage(number)
            if number == 8:
                result(g, 0).start()
                result(g, 1).start()

    def result(g, m):
        source, target = ((full_key, out_key), (full_value, out_value))[m]
        at = (slice(None), pl.ds(g * columns, columns))
        return pltpu.make_async_copy(source.at[at], target.at[at], out_sems.at[2 * g + m])

    @pl.when(step == 0)
    def _():
        greet(links, returned.shape[0])

    block_step(step, spans, heads, panels, queries, cotangent, w_key, w_value, attended, grad_queries, part_key, part_value,
               use_grad, flipped, rows_kv, grads_kv, left, right, pair, stacked, wide)

    for after in range(1, heads):
        moves = [(g, after - 2 * g - 1) for g in reversed(range(GROUPS)) if 0 <= after - 2 * g - 1 <= 8]

        @pl.when(step == after)
        def _():
            if after == 1:
                pl.semaphore_wait(pltpu.get_barrier_semaphore(), 3 + returned.shape[0] - 1)
            advance(*moves)

    @pl.when(step == heads + spans // 2 - 1)
    def _():
        back.cross(0)
        advance((3, 1), (2, 3), (1, 5), (0, 7))

    @pl.when(step == heads + spans - 1)
    def _():
        back.cross(1)
        back.ring_out(0)
        advance((3, 2), (2, 4), (1, 6), (0, 8))
        back.ring_out(1)
        back.ring_on(0)
        back.ring_on(1)
        advance((3, 3), (2, 5), (1, 7))
        back.ring_end(0)
        back.ring_end(1)
        back.post()
        advance((3, 4), (2, 6), (1, 8), (3, 5), (2, 7), (3, 6), (2, 8), (3, 7), (3, 8))
        back.received()
        last = pltpu.make_async_copy(returned, out_returned, out_sems.at[2 * GROUPS])
        last.start()
        mail.settle()
        for g in range(GROUPS):
            result(g, 0).wait()
            result(g, 1).wait()
        last.wait()


def block_call(user, panels, queries, cotangent, w_key, w_value, racks, peers):
    uses, panel_len, width = panels.shape
    spans = queries.shape[0] // SPAN
    features = w_key.shape[1]
    heads = features // HD
    rows = panel_len // racks
    total = uses * panel_len
    columns = features // GROUPS
    messages = 2 * GROUPS * 20 + 14
    by_head = lambda size: pl.BlockSpec((size, HD), lambda i: (0, jnp.minimum(i, heads - 1)))
    whole = lambda a, b: pl.BlockSpec((a, b), lambda i: (0, 0), pipeline_mode=pl.Buffered(1))
    anywhere = pl.BlockSpec(memory_space=pl.ANY)
    return pl.pallas_call(
        functools.partial(block_kernel, spans, heads),
        grid=(heads + spans,),
        out_shape=(
            jax.ShapeDtypeStruct(queries.shape, BF16),
            jax.ShapeDtypeStruct(queries.shape, BF16),
            jax.ShapeDtypeStruct((width, features), BF16),
            jax.ShapeDtypeStruct((width, features), BF16),
            jax.ShapeDtypeStruct((peers, CAP, rows, width), BF16),
        ),
        in_specs=[
            pl.BlockSpec(memory_space=pltpu.SMEM), whole(total, width), by_head(queries.shape[0]), by_head(queries.shape[0]),
            whole(width, features), whole(width, features),
        ],
        out_specs=[by_head(queries.shape[0]), by_head(queries.shape[0]), anywhere, anywhere, anywhere],
        scratch_shapes=[
            pltpu.VMEM((width, features), BF16),
            pltpu.VMEM((width, features), BF16),
            pltpu.VMEM((peers, CAP, rows, width), BF16),
            pltpu.VMEM((width, total), BF16),
            pltpu.VMEM((total, 2 * HD), BF16),
            pltpu.VMEM((heads, total, 2 * HD), BF16),
            pltpu.VMEM((spans, 2 * SPAN, 2 * HD), BF16),
            pltpu.VMEM((spans, 2 * SPAN, 2 * HD), BF16),
            pltpu.VMEM((spans, 2 * SPAN, total // spans), F32),
            pltpu.VMEM((spans, 2 * SPAN, total // spans), BF16),
            pltpu.VMEM((width, 2 * HD), BF16),
            pltpu.VMEM((width, features), BF16),
            pltpu.VMEM((width, features), BF16),
            pltpu.VMEM((racks, uses, rows, width), BF16),
            pltpu.VMEM((2 * GROUPS, 6, width // 8, columns), BF16),
            pltpu.VMEM((2 * GROUPS, 6, 64, 128), BF16),
            pltpu.VMEM((2 * GROUPS, width // 4, columns), BF16),
            pltpu.VMEM((4, uses, rows, width), BF16),
            pltpu.VMEM((6, uses // 2, rows, width), BF16),
            pltpu.VMEM((uses + 1, rows, width), BF16),
            pltpu.VMEM((peers, CAP, rows, width), BF16),
            pltpu.SemaphoreType.DMA((messages,)),
            pltpu.SemaphoreType.DMA((messages,)),
            pltpu.SemaphoreType.DMA((peers,)),
            pltpu.SemaphoreType.DMA((peers,)),
            pltpu.SemaphoreType.DMA((2 * GROUPS + 1,)),
        ],
        compiler_params=pltpu.CompilerParams(
            collective_id=1, has_side_effects=True, vmem_limit_bytes=58 * 1024 * 1024
        ),
        name="block",
    )(user, panels.reshape(total, width), queries, cotangent, w_key, w_value)


def fetch_kernel(cuts, owners, slots, database, panels, asked, user, stored, wanted, heard, leaving, landing, mine, load_sem, ask_send,
                 ask_recv, leave_sems, land_sems, own_sems, send_sems, recv_sems):
    links = Links(4, 4, 4)
    peers = asked.shape[0]
    local_rows, _, width = stored.shape
    uses, rows = mine.shape[0], mine.shape[1]
    nbrs = owners.shape[1]
    my_rows = lambda x, core: pl.ds(pl.multiple_of((x * 2 + core) * rows, rows), rows)
    load = pltpu.make_async_copy(database.at[:, my_rows(links.x, links.core), :], stored, load_sem.at[0])
    load.start()
    signals = greet(links, peers)
    pl.semaphore_wait(pltpu.get_barrier_semaphore(), signals)

    peer_of = lax.broadcasted_iota(jnp.int32, (peers, 1, 128), 0)
    lane = lax.broadcasted_iota(jnp.int32, (peers, 1, 128), 2)
    seen = jnp.zeros((peers, 1, 128), jnp.int32)
    rows_wanted = jnp.full((peers, 1, 128), local_rows, jnp.int32)
    users = jnp.full((peers, 1, 128), uses, jnp.int32)
    for u in range(uses):
        named = peer_of == owners[u // nbrs, u % nbrs]
        here = named & (lane == seen)
        rows_wanted = jnp.where(here, slots[u // nbrs, u % nbrs], rows_wanted)
        users = jnp.where(here, u, users)
        seen = seen + named.astype(jnp.int32)
    wanted[...] = rows_wanted
    user[...] = users

    def ask(far):
        peer = (links.db + far) % peers
        return pltpu.make_async_remote_copy(
            src_ref=wanted.at[peer], dst_ref=asked.at[links.db], send_sem=ask_send.at[far], recv_sem=ask_recv.at[far],
            device_id=(peer, links.rack), device_id_type=MESH,
        )

    pl.loop(1, peers)(lambda far: ask(far).start())
    asked[links.db] = wanted[links.db]
    load.wait()
    pl.loop(1, peers)(lambda far: ask(far).wait())
    tables = pltpu.make_async_copy(asked, heard, load_sem.at[1])
    tables.start()
    tables.wait()

    def answer(c, far):
        peer = (links.db + far) % peers
        return pltpu.make_async_remote_copy(
            src_ref=leaving[c].at[peer], dst_ref=landing[c].at[links.db], send_sem=leave_sems.at[c, far],
            recv_sem=land_sems.at[c, far], device_id=(peer, links.rack), device_id_type=MESH,
        )

    def fill(c, peer, target):
        for k in range(CAP):
            row = jnp.minimum(heard[peer, 0, k], local_rows - 1)
            target[peer, k] = stored[row, :, cuts[c]:cuts[c + 1]]

    for c in range(len(cuts) - 1):
        @pl.loop(1, peers)
        def _(far):
            fill(c, (links.db + far) % peers, leaving[c])
            answer(c, far).start()

        fill(c, links.db, landing[c])

    mail = Mail(send_sems, recv_sems)
    up, down, across = links.ids[("x", 1)], links.ids[("x", -1)], links.ids[("core", 1)]
    own_copies = []
    half = uses // 2

    def out(c, far, first, size):
        return panels.at[pl.ds(first, size), my_rows((links.x + far) % 4, links.core), pl.ds(cuts[c], cuts[c + 1] - cuts[c])]

    def pass_on(name, c, far, first, size, device):
        spot = lambda: out(c, far, first, size)
        mail.plan((name, c), spot, spot, device)
        mail.start((name, c))

    def exchange(c):
        mail.arrive(("up", c))
        pass_on("on", c, 3, 0, half, up)
        pass_on("cross3", c, 3, 0, uses, across)
        mail.arrive(("down", c))
        pass_on("back", c, 1, half, half, down)
        pass_on("cross1", c, 1, 0, uses, across)

    def finish(c):
        mail.arrive(("on", c))
        pass_on("cross2a", c, 2, 0, half, across)
        mail.arrive(("back", c))
        pass_on("cross2b", c, 2, half, half, across)

    count = len(cuts) - 1
    for c in range(count):
        pl.loop(1, peers)(lambda far: answer(c, far).wait())
        for u in range(uses):
            owner = owners[u // nbrs, u % nbrs]
            rank = jnp.int32(0)
            for v in range(u):
                rank = rank + (owners[v // nbrs, v % nbrs] == owner).astype(jnp.int32)
            mine[u, :, cuts[c]:cuts[c + 1]] = landing[c][owner, jnp.minimum(rank, CAP - 1)]
        source = mine.at[:, :, pl.ds(cuts[c], cuts[c + 1] - cuts[c])]
        target = out(c, 0, 0, uses)
        for name, device in (("up", up), ("down", down), ("cross0", across)):
            mail.plan((name, c), lambda source=source: source, lambda target=target: target, device)
            mail.start((name, c))
        copy = pltpu.make_async_copy(source, target, own_sems.at[c])
        copy.start()
        own_copies.append(copy)
        if c > 0:
            exchange(c - 1)
    exchange(count - 1)
    for c in range(count):
        finish(c)
    for c in range(count):
        mail.arrive(("cross0", c), ("cross1", c), ("cross3", c), ("cross2a", c), ("cross2b", c))
    for copy in own_copies:
        copy.wait()
    mail.settle()


CUTS = (0, 512, 896)


def fetch_call(owners, slots, database, peers, racks):
    uses = owners.shape[0] * owners.shape[1]
    local_rows, panel_len, width = database.shape
    rows = panel_len // racks
    parts = len(CUTS) - 1
    chunk = lambda c: pltpu.VMEM((peers, CAP, rows, CUTS[c + 1] - CUTS[c]), BF16)
    vmem = pl.BlockSpec(memory_space=pltpu.VMEM)
    smem = pl.BlockSpec(memory_space=pltpu.SMEM)
    anywhere = pl.BlockSpec(memory_space=pl.ANY)
    sems = pltpu.SemaphoreType.DMA
    return pl.pallas_call(
        functools.partial(fetch_kernel, CUTS),
        out_shape=(
            jax.ShapeDtypeStruct((uses, panel_len, width), BF16),
            jax.ShapeDtypeStruct((peers, 1, 128), jnp.int32),
            jax.ShapeDtypeStruct((peers, 1, 128), jnp.int32),
        ),
        in_specs=[smem, smem, anywhere],
        out_specs=(anywhere, vmem, vmem),
        scratch_shapes=[
            pltpu.VMEM((local_rows, rows, width), BF16),
            pltpu.VMEM((peers, 1, 128), jnp.int32),
            pltpu.SMEM((peers, 1, 128), jnp.int32),
            [chunk(c) for c in range(parts)],
            [chunk(c) for c in range(parts)],
            pltpu.VMEM((uses, rows, width), BF16),
            sems((2,)), sems((peers,)), sems((peers,)), sems((parts, peers)), sems((parts, peers)), sems((parts,)),
            sems((9 * parts,)), sems((9 * parts,)),
        ],
        compiler_params=pltpu.CompilerParams(
            collective_id=0, has_side_effects=True, vmem_limit_bytes=24 * 1024 * 1024
        ),
        name="fetch",
    )(owners, slots, database)


def pick(selector, source):
    return jnp.einsum("ns,spw->npw", selector, source, preferred_element_type=F32).astype(BF16)


def local(queries, cotangent, database, w_key, w_value, neighbour_owner, neighbour_slot):
    peer_count = lax.axis_size("db")
    racks = lax.axis_size("rack")
    local_rows, _, width = database.shape
    rows = database.shape[1] // racks
    panels, asked, user = fetch_call(neighbour_owner, neighbour_slot, database, peer_count, racks)
    asked_rows = asked[:, 0, :CAP].reshape(peer_count * CAP)
    selector = (asked_rows[:, None] == jnp.arange(local_rows, dtype=jnp.int32)[None, :]).astype(BF16)
    attended, grad_query, full_key, full_value, returned = block_call(
        user, panels, queries, cotangent, w_key, w_value, racks, peer_count
    )
    grad_w_key, grad_w_value = full_key.astype(F32), full_value.astype(F32)
    grad_database = pick(selector.T, returned.reshape(peer_count * CAP, rows, width))
    return attended, grad_query, grad_w_key, grad_w_value, grad_database


def solution(mesh):
    return jax.shard_map(
        local,
        mesh=mesh,
        in_specs=(
            P("db", "rack"), P("db", "rack"), P("db", None, None), P(None, "rack"), P(None, "rack"), P("db", None), P("db", None),
        ),
        out_specs=(P("db", "rack"), P("db", "rack"), P(None, "rack"), P(None, "rack"), P("db", "rack", None)),
        check_vma=False,
    )
```

```python
import functools

import jax
import jax.numpy as jnp
from jax import lax
from jax.experimental import pallas as pl
from jax.experimental.pallas import tpu as pltpu
from jax.sharding import PartitionSpec as P

HD = 128
SPAN = 64
CAP = 3
PARTS = 2
GPARTS = 2
NT = (((1,), (1,)), ((), ()))
TN = (((0,), (0,)), ((), ()))
F32 = jnp.float32
BF16 = jnp.bfloat16


def dot(a, b):
    return jnp.dot(a, b, preferred_element_type=F32)


MESH = pl.DeviceIdType.MESH


class Links:
    def __init__(self, side_z, side_y, side_x):
        db, rack = lax.axis_index("db"), lax.axis_index("rack")
        self.db, self.rack = db, rack
        self.z, self.y = db // side_y, db % side_y
        self.x, self.core = rack // 2, rack % 2
        self.side_x = side_x
        self.ids = {
            ("y", 1): (self.z * side_y + (self.y + 1) % side_y, rack),
            ("y", -1): (self.z * side_y + (self.y + side_y - 1) % side_y, rack),
            ("z", 1): ((self.z + 1) % side_z * side_y + self.y, rack),
            ("z", -1): ((self.z + side_z - 1) % side_z * side_y + self.y, rack),
            ("x", 1): (db, (self.x + 1) % side_x * 2 + self.core),
            ("x", -1): (db, (self.x + side_x - 1) % side_x * 2 + self.core),
            ("core", 1): (db, self.x * 2 + 1 - self.core),
        }

    def place(self, axis):
        return {"y": self.y, "z": self.z, "x": self.x}[axis]


class Mail:
    def __init__(self, send_sems, recv_sems):
        self.send_sems, self.recv_sems, self.book = send_sems, recv_sems, {}

    def plan(self, name, source, target, device):
        self.book[name] = (len(self.book), source, target, device)

    def copy(self, name):
        n, source, target, device = self.book[name]
        return pltpu.make_async_remote_copy(
            src_ref=source(), dst_ref=target(), send_sem=self.send_sems.at[n], recv_sem=self.recv_sems.at[n], device_id=device,
            device_id_type=MESH,
        )

    def start(self, *names):
        for name in names:
            self.copy(name).start()

    def arrive(self, *names):
        for name in names:
            self.copy(name).wait_recv()

    def settle(self):
        for name in self.book:
            self.copy(name).wait_send()


def greet(links, peers):
    barrier = pltpu.get_barrier_semaphore()
    others = [links.ids[("core", 1)], links.ids[("x", 1)], links.ids[("x", -1)]]
    for device in others:
        pl.semaphore_signal(barrier, inc=1, device_id=device, device_id_type=MESH)

    @pl.loop(1, peers)
    def _(far):
        pl.semaphore_signal(barrier, inc=1, device_id=((links.db + far) % peers, links.rack), device_id_type=MESH)

    return len(others) + peers - 1


def add(*terms):
    total = terms[0].astype(F32)
    for term in terms[1:]:
        total = total + term.astype(F32)
    return total.astype(BF16)


class Reduction:
    def __init__(self, tag, links, mail, part, full, first_column, columns, axes, near, far, middle):
        self.tag, self.links, self.mail = tag, links, mail
        self.part, self.full, self.first_column, self.columns = part, full, first_column, columns
        self.near, self.far, self.middle = near, far, middle
        self.rows = part.shape[0] // 4
        self.places = [links.place(axis) for axis in axes]
        self.across = columns // 128
        self.short = self.rows * self.across // 4
        self.sides = [(0, self.rows // 32 * 16), (self.rows // 32 * 16, self.rows - self.rows // 32 * 16)]
        whole = (self.short + 31) // 32 * 16
        self.bits = [(0, whole), (whole, self.short - whole)]
        up = [links.ids[(axis, 1)] for axis in axes]
        down = [links.ids[(axis, -1)] for axis in axes]
        one, two = self.places
        for level, at, buffer, sides, me, k in (("n", self.wide, near, self.sides, one, 0), ("f", self.small, far, self.bits, two, 1)):
            lot = lambda ref, slot, side, sides=sides: (lambda: ref.at[slot, pl.ds(0, sides[side][1])])
            spot = lambda far_off, side, at=at, me=me: (lambda: at((me + far_off) % 4, side))
            self.plan(level + "ra", spot(2, 0), lot(buffer, 0, 0), up[k])
            self.plan(level + "rb", spot(2, 1), lot(buffer, 1, 1), down[k])
            self.plan(level + "db", spot(1, 1), lot(buffer, 3, 1), up[k])
            self.plan(level + "da", spot(3, 0), lot(buffer, 2, 0), down[k])
            self.plan(level + "sa", lot(buffer, 0, 0), lot(buffer, 4, 0), up[k])
            self.plan(level + "sb", lot(buffer, 1, 1), lot(buffer, 5, 1), down[k])
        for level, at, sides, size, me, k in (("g", self.piece, self.bits, self.short, two, 1), ("h", self.band, self.sides, self.rows, one, 0)):
            spot = lambda far_off, first, size, at=at, me=me: (lambda: at((me + far_off) % 4, first, size))
            for name, far_off, (first, length), device in (
                ("up", 0, (0, size), up[k]), ("down", 0, (0, size), down[k]), ("on", 3, sides[0], up[k]), ("back", 1, sides[1], down[k]),
            ):
                self.plan(level + name, spot(far_off, first, length), spot(far_off, first, length), device)

    def plan(self, name, source, target, device):
        self.mail.plan((self.tag, name), source, target, device)

    def start(self, *names):
        self.mail.start(*[(self.tag, name) for name in names])

    def arrive(self, *names):
        self.mail.arrive(*[(self.tag, name) for name in names])

    def wide(self, one, side):
        first, size = self.sides[side]
        return self.part.at[pl.ds(pl.multiple_of(one * self.rows + first, 16), size), pl.ds(self.first_column, self.columns)]

    def small(self, two, side):
        first, size = self.bits[side]
        return self.middle.at[
            pl.ds(pl.multiple_of(two // self.across * self.short + first, 16), size),
            pl.ds(pl.multiple_of(two % self.across * 128, 128), 128),
        ]

    def piece(self, two, first, size):
        row = self.places[0] * self.rows + two // self.across * self.short + first
        column = self.first_column + two % self.across * 128
        return self.full.at[pl.ds(pl.multiple_of(row, 16), size), pl.ds(pl.multiple_of(column, 128), 128)]

    def band(self, one, first, size):
        return self.full.at[pl.ds(pl.multiple_of(one * self.rows + first, 16), size), pl.ds(self.first_column, self.columns)]

    def join(self, level, at, buffer, sides, me):
        for side, letter, far_off in ((0, "a", 1), (1, "b", 3)):
            size = sides[side][1]
            self.arrive(level + "r" + letter)
            buffer[side, :size] = add(buffer[side, :size], at((me + far_off) % 4, side)[...])
            self.start(level + "s" + letter)

    def total(self, level, at, buffer, sides, me, side):
        letter, size = "ab"[side], sides[side][1]
        self.arrive(level + "d" + letter, level + "s" + letter)
        return add(buffer[2 + side, :size], buffer[4 + side, :size], at(me, side)[...])

    def stage(self, number):
        one, two = self.places
        if number == 0:
            self.start("nra", "nrb", "ndb", "nda")
        elif number == 1:
            self.join("n", self.wide, self.near, self.sides, one)
        elif number == 2:
            for side, (first, size) in enumerate(self.sides):
                self.middle[first:first + size, :] = self.total("n", self.wide, self.near, self.sides, one, side)
            self.start("fra", "frb", "fdb", "fda")
        elif number == 3:
            self.join("f", self.small, self.far, self.bits, two)
        elif number == 4:
            for side, (first, size) in enumerate(self.bits):
                self.piece(two, first, size)[...] = self.total("f", self.small, self.far, self.bits, two, side)
            self.start("gup", "gdown")
        elif number == 6:
            self.arrive("gon", "gback")
            self.start("hup", "hdown")
        elif number == 8:
            self.arrive("hon", "hback")
        else:
            level = "g" if number == 5 else "h"
            self.arrive(level + "up")
            self.start(level + "on")
            self.arrive(level + "down")
            self.start(level + "back")


class Return:
    def __init__(self, tag, links, mail, use_grad, user, returned, crossed, ring, mine, leaving, leave_sems, land_sems):
        self.tag = tag
        self.links, self.mail, self.use_grad, self.user, self.returned = links, mail, use_grad, user, returned
        self.crossed, self.ring, self.mine, self.leaving = crossed, ring, mine, leaving
        self.leave_sems, self.land_sems = leave_sems, land_sems
        self.half = mine.shape[0] // 2
        up, down, across = links.ids[("x", 1)], links.ids[("x", -1)], links.ids[("core", 1)]
        for side in (0, 1):
            for far_off in (2, 1, 3, 0):
                mail.plan((tag, "c", far_off, side), self.partner(far_off, side), self.spot(far_off, side), across)
        slot = lambda n: (lambda: ring.at[n])
        mail.plan((tag, "xra"), self.spot(2, 0), slot(0), up)
        mail.plan((tag, "xda"), self.spot(3, 0), slot(2), down)
        mail.plan((tag, "xrb"), self.spot(2, 1), slot(1), down)
        mail.plan((tag, "xdb"), self.spot(1, 1), slot(3), up)
        mail.plan((tag, "xsa"), slot(0), slot(4), up)
        mail.plan((tag, "xsb"), slot(1), slot(5), down)

    def uses(self, side):
        return pl.ds(side * self.half, self.half)

    def spot(self, far_off, side):
        return lambda: self.crossed.at[(self.links.x + far_off) % 4, self.uses(side)]

    def partner(self, far_off, side):
        return lambda: self.use_grad.at[(self.links.x + far_off) % 4 * 2 + 1 - self.links.core, self.uses(side)]

    def cross(self):
        self.mail.start(*[(self.tag, "c", far_off, side) for far_off in (2, 1, 3, 0) for side in (0, 1)])

    def ring_out(self):
        links, mail, half = self.links, self.mail, self.half
        for far_off, names in ((2, ("xra", "xrb")), (1, (None, "xdb")), (3, ("xda", None)), (0, (None, None))):
            x = (links.x + far_off) % 4
            for side, name in enumerate(names):
                mail.arrive((self.tag, "c", far_off, side))

                @pl.loop(side * half, (side + 1) * half)
                def _(n):
                    self.crossed[x, n] = add(self.crossed[x, n], self.use_grad[x * 2 + links.core, n])

                if name:
                    mail.start((self.tag, name))

    def ring_on(self):
        for side in (0, 1):
            self.pass_on(side)

    def ring_end(self):
        for side in (0, 1):
            self.finish(side)

    def pass_on(self, side):
        letter, far_off = ("a", 1) if side == 0 else ("b", 3)
        self.mail.arrive((self.tag, "xr" + letter))
        own = self.spot(far_off, side)()

        @pl.loop(0, self.half)
        def _(n):
            self.ring[side, n] = add(self.ring[side, n], own[n])

        self.mail.start((self.tag, "xs" + letter))

    def finish(self, side):
        letter = "ab"[side]
        self.mail.arrive((self.tag, "xd" + letter), (self.tag, "xs" + letter))
        own = self.spot(0, side)()

        @pl.loop(0, self.half)
        def _(n):
            self.mine[side * self.half + n] = add(self.ring[2 + side, n], self.ring[4 + side, n], own[n])

    def post(self):
        links, peers = self.links, self.returned.shape[0]
        self.mine[2 * self.half] = jnp.zeros(self.mine.shape[1:], BF16)

        def fill(peer, target):
            for k in range(CAP):
                target[peer, k] = self.mine[self.user[peer, 0, k]]

        @pl.loop(1, peers)
        def _(far_off):
            fill((links.db + far_off) % peers, self.leaving)
            self.copy(far_off).start()

        fill(links.db, self.returned)

    def received(self):
        pl.loop(1, self.returned.shape[0])(lambda far_off: self.copy(far_off).wait())

    def copy(self, far_off):
        links = self.links
        peer = (links.db + far_off) % self.returned.shape[0]
        return pltpu.make_async_remote_copy(
            src_ref=self.leaving.at[peer], dst_ref=self.returned.at[links.db], send_sem=self.leave_sems.at[far_off],
            recv_sem=self.land_sems.at[far_off], device_id=(peer, links.rack), device_id_type=MESH,
        )


def block_step(step, spans, heads, panels, queries, cotangent, w_key, w_value, attended, grad_queries, part_key, part_value,
               use_grad, flipped, rows_kv, grads_kv, left, right, pair, stacked, wide):
    keys = panels.shape[0] // spans
    width = panels.shape[1]
    scale = HD ** -0.5

    @pl.when(step == 0)
    def _():
        left[...] = jnp.zeros_like(left)
        right[...] = jnp.zeros_like(right)
        for c in range(spans):
            flipped[:, c * keys:(c + 1) * keys] = panels[c * keys:(c + 1) * keys, :].T

    @pl.when(step < heads)
    def _():
        columns = pl.ds(pl.multiple_of(step * HD, HD), HD)
        wide[:, :HD] = w_key[:, columns]
        wide[:, HD:] = w_value[:, columns]

        @pl.loop(0, PARTS)
        def _(n):
            size = panels.shape[0] // PARTS
            at = pl.ds(pl.multiple_of(n * size, size), size)
            rows_kv[at, :] = dot(panels[at, :], wide[...]).astype(BF16)

        for c in range(spans):
            tokens = slice(c * SPAN, (c + 1) * SPAN)
            query, grad = queries[tokens, :], cotangent[tokens, :]
            left[c, :SPAN, :HD] = query
            left[c, SPAN:, HD:] = grad
            right[c, :SPAN, HD:] = grad
            right[c, SPAN:, :HD] = query
        for c in range(spans):
            pair[c] = lax.dot_general(left[c], rows_kv[c * keys:(c + 1) * keys, :], NT, preferred_element_type=F32)
        for c in range(spans):
            scores = pair[c, :SPAN] * scale
            raised = jnp.exp(scores - jnp.max(scores, axis=-1, keepdims=True))
            probs = raised * (1.0 / jnp.sum(raised, axis=-1, keepdims=True))
            stacked[c, :SPAN] = probs.astype(BF16)
            grad_probs = pair[c, SPAN:]
            delta = jnp.sum(probs * grad_probs, axis=-1, keepdims=True)
            stacked[c, SPAN:] = (probs * (grad_probs - delta) * scale).astype(BF16)
        for c in range(spans):
            tokens = slice(c * SPAN, (c + 1) * SPAN)
            own = slice(c * keys, (c + 1) * keys)
            out = dot(stacked[c], rows_kv[own, :])
            attended[tokens, :] = out[:SPAN, HD:].astype(BF16)
            grad_queries[tokens, :] = out[SPAN:, :HD].astype(BF16)
        for c in range(spans):
            own = slice(c * keys, (c + 1) * keys)
            grads_kv[step, own, :] = lax.dot_general(stacked[c], right[c], TN, preferred_element_type=F32).astype(BF16)

        @pl.loop(0, GPARTS)
        def _(n):
            size = width // GPARTS
            at = pl.ds(pl.multiple_of(n * size, size), size)
            total = dot(flipped[at, :], grads_kv[step]).astype(BF16)
            part_key[at, columns] = total[:, :HD]
            part_value[at, columns] = total[:, HD:]

    for part in range(len(CUTS) - 1):
        first, last = CUTS[part], CUTS[part + 1]

        @pl.when((step >= heads + part * QUARTERS) & (step < heads + (part + 1) * QUARTERS))
        def _():
            pieces, uses, rows = use_grad[part].shape[0], use_grad[part].shape[1] // QUARTERS, use_grad[part].shape[2]
            c = step - heads - part * QUARTERS
            size = panels.shape[0] // QUARTERS
            own = pl.ds(pl.multiple_of(c * size, size), size)
            total = jnp.zeros((size, last - first), F32)
            for h in range(heads):
                columns = slice(h * HD, (h + 1) * HD)
                weights = jnp.concatenate([w_key[first:last, columns], w_value[first:last, columns]], axis=1)
                total = total + lax.dot_general(grads_kv[h, own, :], weights, NT, preferred_element_type=F32)
            total = total.astype(BF16)
            for n in range(uses):
                for r in range(pieces):
                    at = (n * pieces + r) * rows
                    use_grad[part][r, c * uses + n, :, :] = total[at:at + rows, :]


QUARTERS = 4
CUTS = (0, 512, 896)
GROUPS = 4


def block_kernel(spans, heads, user, panels, queries, cotangent, w_key, w_value, attended, grad_queries, out_key, out_value,
                 out_returned, full_key, full_value, returned, flipped, rows_kv, grads_kv, left, right, pair, stacked, wide, part_key, part_value, use_grad, near, far,
                 middle, crossed, ring, mine, leaving, send_sems, recv_sems, leave_sems, land_sems, out_sems):
    step = pl.program_id(0)
    links = Links(4, 4, 4)
    mail = Mail(send_sems, recv_sems)
    columns = part_key.shape[1] // GROUPS
    items = []
    for g in range(GROUPS):
        for m, (part, full, axes) in enumerate(((part_key, full_key, "yz"), (part_value, full_value, "zy"))):
            n = g * 2 + m
            items.append(Reduction(n, links, mail, part, full, g * columns, columns, axes, near.at[n], far.at[n], middle.at[n]))
    parts = range(len(CUTS) - 1)
    back = [
        Return("lr"[c], links, mail, use_grad[c], user, returned[c], crossed[c], ring[c], mine[c], leaving[c], leave_sems.at[c], land_sems.at[c])
        for c in parts
    ]

    def advance(*moves):
        for g, number in moves:
            items[2 * g].stage(number)
            items[2 * g + 1].stage(number)
            if number == 8:
                result(g, 0).start()
                result(g, 1).start()

    def result(g, m):
        source, target = ((full_key, out_key), (full_value, out_value))[m]
        at = (slice(None), pl.ds(g * columns, columns))
        return pltpu.make_async_copy(source.at[at], target.at[at], out_sems.at[2 * g + m])

    @pl.when(step == 0)
    def _():
        greet(links, user.shape[0])

    block_step(step, spans, heads, panels, queries, cotangent, w_key, w_value, attended, grad_queries, part_key, part_value,
               use_grad, flipped, rows_kv, grads_kv, left, right, pair, stacked, wide)

    for after in range(1, heads):
        moves = [(g, after - 2 * g - 1) for g in reversed(range(GROUPS)) if 0 <= after - 2 * g - 1 <= 8]

        @pl.when(step == after)
        def _():
            if after == 1:
                pl.semaphore_wait(pltpu.get_barrier_semaphore(), 3 + user.shape[0] - 1)
            advance(*moves)

    @pl.when(step == heads + QUARTERS - 1)
    def _():
        back[0].cross()
        advance((3, 1), (2, 3), (1, 5), (0, 7))

    @pl.when(step == heads + 2 * QUARTERS - 1)
    def _():
        back[1].cross()
        back[0].ring_out()
        advance((3, 2), (2, 4), (1, 6), (0, 8))
        back[0].ring_on()
        back[1].ring_out()
        advance((3, 3), (2, 5), (1, 7))
        back[0].ring_end()
        back[0].post()
        back[1].ring_on()
        advance((3, 4), (2, 6), (1, 8))
        back[1].ring_end()
        back[1].post()
        advance((3, 5), (2, 7), (3, 6), (2, 8), (3, 7), (3, 8))
        last = []
        for c in parts:
            back[c].received()
            target = out_returned.at[:, :, :, pl.ds(CUTS[c], CUTS[c + 1] - CUTS[c])]
            last.append(pltpu.make_async_copy(returned[c], target, out_sems.at[2 * GROUPS + c]))
            last[c].start()
        mail.settle()
        for g in range(GROUPS):
            result(g, 0).wait()
            result(g, 1).wait()
        for copy in last:
            copy.wait()


def block_call(user, panels, queries, cotangent, w_key, w_value, racks, peers):
    uses, panel_len, width = panels.shape
    spans = queries.shape[0] // SPAN
    features = w_key.shape[1]
    heads = features // HD
    rows = panel_len // racks
    total = uses * panel_len
    columns = features // GROUPS
    messages = 2 * GROUPS * 20 + 28
    cut = lambda *shape: [pltpu.VMEM(shape + (CUTS[c + 1] - CUTS[c],), BF16) for c in range(len(CUTS) - 1)]
    by_head = lambda size: pl.BlockSpec((size, HD), lambda i: (0, jnp.minimum(i, heads - 1)))
    whole = lambda a, b: pl.BlockSpec((a, b), lambda i: (0, 0), pipeline_mode=pl.Buffered(1))
    anywhere = pl.BlockSpec(memory_space=pl.ANY)
    return pl.pallas_call(
        functools.partial(block_kernel, spans, heads),
        grid=(heads + 2 * QUARTERS,),
        out_shape=(
            jax.ShapeDtypeStruct(queries.shape, BF16),
            jax.ShapeDtypeStruct(queries.shape, BF16),
            jax.ShapeDtypeStruct((width, features), BF16),
            jax.ShapeDtypeStruct((width, features), BF16),
            jax.ShapeDtypeStruct((peers, CAP, rows, width), BF16),
        ),
        in_specs=[
            pl.BlockSpec(memory_space=pltpu.SMEM), whole(total, width), by_head(queries.shape[0]), by_head(queries.shape[0]),
            whole(width, features), whole(width, features),
        ],
        out_specs=[by_head(queries.shape[0]), by_head(queries.shape[0]), anywhere, anywhere, anywhere],
        scratch_shapes=[
            pltpu.VMEM((width, features), BF16),
            pltpu.VMEM((width, features), BF16),
            cut(peers, CAP, rows),
            pltpu.VMEM((width, total), BF16),
            pltpu.VMEM((total, 2 * HD), BF16),
            pltpu.VMEM((heads, total, 2 * HD), BF16),
            pltpu.VMEM((spans, 2 * SPAN, 2 * HD), BF16),
            pltpu.VMEM((spans, 2 * SPAN, 2 * HD), BF16),
            pltpu.VMEM((spans, 2 * SPAN, total // spans), F32),
            pltpu.VMEM((spans, 2 * SPAN, total // spans), BF16),
            pltpu.VMEM((width, 2 * HD), BF16),
            pltpu.VMEM((width, features), BF16),
            pltpu.VMEM((width, features), BF16),
            cut(racks, uses, rows),
            pltpu.VMEM((2 * GROUPS, 6, width // 8, columns), BF16),
            pltpu.VMEM((2 * GROUPS, 6, 64, 128), BF16),
            pltpu.VMEM((2 * GROUPS, width // 4, columns), BF16),
            cut(4, uses, rows),
            cut(6, uses // 2, rows),
            cut(uses + 1, rows),
            cut(peers, CAP, rows),
            pltpu.SemaphoreType.DMA((messages,)),
            pltpu.SemaphoreType.DMA((messages,)),
            pltpu.SemaphoreType.DMA((len(CUTS) - 1, peers)),
            pltpu.SemaphoreType.DMA((len(CUTS) - 1, peers)),
            pltpu.SemaphoreType.DMA((2 * GROUPS + 2,)),
        ],
        compiler_params=pltpu.CompilerParams(
            collective_id=1, has_side_effects=True, vmem_limit_bytes=58 * 1024 * 1024
        ),
        name="block",
    )(user, panels.reshape(total, width), queries, cotangent, w_key, w_value)


def fetch_kernel(cuts, owners, slots, database, panels, asked, user, stored, wanted, heard, leaving, landing, mine, load_sem, ask_send,
                 ask_recv, leave_sems, land_sems, own_sems, send_sems, recv_sems):
    links = Links(4, 4, 4)
    peers = asked.shape[0]
    local_rows, _, width = stored.shape
    uses, rows = mine.shape[0], mine.shape[1]
    nbrs = owners.shape[1]
    my_rows = lambda x, core: pl.ds(pl.multiple_of((x * 2 + core) * rows, rows), rows)
    load = pltpu.make_async_copy(database.at[:, my_rows(links.x, links.core), :], stored, load_sem.at[0])
    load.start()
    signals = greet(links, peers)
    pl.semaphore_wait(pltpu.get_barrier_semaphore(), signals)

    peer_of = lax.broadcasted_iota(jnp.int32, (peers, 1, 128), 0)
    lane = lax.broadcasted_iota(jnp.int32, (peers, 1, 128), 2)
    seen = jnp.zeros((peers, 1, 128), jnp.int32)
    rows_wanted = jnp.full((peers, 1, 128), local_rows, jnp.int32)
    users = jnp.full((peers, 1, 128), uses, jnp.int32)
    for u in range(uses):
        named = peer_of == owners[u // nbrs, u % nbrs]
        here = named & (lane == seen)
        rows_wanted = jnp.where(here, slots[u // nbrs, u % nbrs], rows_wanted)
        users = jnp.where(here, u, users)
        seen = seen + named.astype(jnp.int32)
    wanted[...] = rows_wanted
    user[...] = users

    def ask(far):
        peer = (links.db + far) % peers
        return pltpu.make_async_remote_copy(
            src_ref=wanted.at[peer], dst_ref=asked.at[links.db], send_sem=ask_send.at[far], recv_sem=ask_recv.at[far],
            device_id=(peer, links.rack), device_id_type=MESH,
        )

    pl.loop(1, peers)(lambda far: ask(far).start())
    asked[links.db] = wanted[links.db]
    load.wait()
    pl.loop(1, peers)(lambda far: ask(far).wait())
    tables = pltpu.make_async_copy(asked, heard, load_sem.at[1])
    tables.start()
    tables.wait()

    def answer(c, far):
        peer = (links.db + far) % peers
        return pltpu.make_async_remote_copy(
            src_ref=leaving[c].at[peer], dst_ref=landing[c].at[links.db], send_sem=leave_sems.at[c, far],
            recv_sem=land_sems.at[c, far], device_id=(peer, links.rack), device_id_type=MESH,
        )

    def fill(c, peer, target):
        for k in range(CAP):
            row = jnp.minimum(heard[peer, 0, k], local_rows - 1)
            target[peer, k] = stored[row, :, cuts[c]:cuts[c + 1]]

    for c in range(len(cuts) - 1):
        @pl.loop(1, peers)
        def _(far):
            fill(c, (links.db + far) % peers, leaving[c])
            answer(c, far).start()

        fill(c, links.db, landing[c])

    mail = Mail(send_sems, recv_sems)
    up, down, across = links.ids[("x", 1)], links.ids[("x", -1)], links.ids[("core", 1)]
    own_copies = []
    half = uses // 2

    def out(c, far, first, size):
        return panels.at[pl.ds(first, size), my_rows((links.x + far) % 4, links.core), pl.ds(cuts[c], cuts[c + 1] - cuts[c])]

    def pass_on(name, c, far, first, size, device):
        spot = lambda: out(c, far, first, size)
        mail.plan((name, c), spot, spot, device)
        mail.start((name, c))

    def exchange(c):
        mail.arrive(("up", c))
        pass_on("on", c, 3, 0, half, up)
        pass_on("cross3", c, 3, 0, uses, across)
        mail.arrive(("down", c))
        pass_on("back", c, 1, half, half, down)
        pass_on("cross1", c, 1, 0, uses, across)

    def finish(c):
        mail.arrive(("on", c))
        pass_on("cross2a", c, 2, 0, half, across)
        mail.arrive(("back", c))
        pass_on("cross2b", c, 2, half, half, across)

    count = len(cuts) - 1
    for c in range(count):
        pl.loop(1, peers)(lambda far: answer(c, far).wait())
        for u in range(uses):
            owner = owners[u // nbrs, u % nbrs]
            rank = jnp.int32(0)
            for v in range(u):
                rank = rank + (owners[v // nbrs, v % nbrs] == owner).astype(jnp.int32)
            mine[u, :, cuts[c]:cuts[c + 1]] = landing[c][owner, jnp.minimum(rank, CAP - 1)]
        source = mine.at[:, :, pl.ds(cuts[c], cuts[c + 1] - cuts[c])]
        target = out(c, 0, 0, uses)
        for name, device in (("up", up), ("down", down), ("cross0", across)):
            mail.plan((name, c), lambda source=source: source, lambda target=target: target, device)
            mail.start((name, c))
        copy = pltpu.make_async_copy(source, target, own_sems.at[c])
        copy.start()
        own_copies.append(copy)
        if c > 0:
            exchange(c - 1)
    exchange(count - 1)
    for c in range(count):
        finish(c)
    for c in range(count):
        mail.arrive(("cross0", c), ("cross1", c), ("cross3", c), ("cross2a", c), ("cross2b", c))
    for copy in own_copies:
        copy.wait()
    mail.settle()


def fetch_call(owners, slots, database, peers, racks):
    uses = owners.shape[0] * owners.shape[1]
    local_rows, panel_len, width = database.shape
    rows = panel_len // racks
    parts = len(CUTS) - 1
    chunk = lambda c: pltpu.VMEM((peers, CAP, rows, CUTS[c + 1] - CUTS[c]), BF16)
    vmem = pl.BlockSpec(memory_space=pltpu.VMEM)
    smem = pl.BlockSpec(memory_space=pltpu.SMEM)
    anywhere = pl.BlockSpec(memory_space=pl.ANY)
    sems = pltpu.SemaphoreType.DMA
    return pl.pallas_call(
        functools.partial(fetch_kernel, CUTS),
        out_shape=(
            jax.ShapeDtypeStruct((uses, panel_len, width), BF16),
            jax.ShapeDtypeStruct((peers, 1, 128), jnp.int32),
            jax.ShapeDtypeStruct((peers, 1, 128), jnp.int32),
        ),
        in_specs=[smem, smem, pl.BlockSpec(memory_space=pltpu.HBM)],
        out_specs=(anywhere, vmem, vmem),
        scratch_shapes=[
            pltpu.VMEM((local_rows, rows, width), BF16),
            pltpu.VMEM((peers, 1, 128), jnp.int32),
            pltpu.SMEM((peers, 1, 128), jnp.int32),
            [chunk(c) for c in range(parts)],
            [chunk(c) for c in range(parts)],
            pltpu.VMEM((uses, rows, width), BF16),
            sems((2,)), sems((peers,)), sems((peers,)), sems((parts, peers)), sems((parts, peers)), sems((parts,)),
            sems((9 * parts,)), sems((9 * parts,)),
        ],
        compiler_params=pltpu.CompilerParams(
            collective_id=0, has_side_effects=True, vmem_limit_bytes=24 * 1024 * 1024
        ),
        name="fetch",
    )(owners, slots, database)


def pick(selector, source):
    return jnp.einsum("ns,spw->npw", selector, source, preferred_element_type=F32).astype(BF16)


def local(queries, cotangent, database, w_key, w_value, neighbour_owner, neighbour_slot):
    peer_count = lax.axis_size("db")
    racks = lax.axis_size("rack")
    local_rows, _, width = database.shape
    rows = database.shape[1] // racks
    panels, asked, user = fetch_call(neighbour_owner, neighbour_slot, database, peer_count, racks)
    asked_rows = asked[:, 0, :CAP].reshape(peer_count * CAP)
    selector = (asked_rows[:, None] == jnp.arange(local_rows, dtype=jnp.int32)[None, :]).astype(BF16)
    attended, grad_query, full_key, full_value, returned = block_call(
        user, panels, queries, cotangent, w_key, w_value, racks, peer_count
    )
    grad_w_key, grad_w_value = full_key.astype(F32), full_value.astype(F32)
    grad_database = pick(selector.T, returned.reshape(peer_count * CAP, rows, width))
    return attended, grad_query, grad_w_key, grad_w_value, grad_database


def solution(mesh):
    return jax.shard_map(
        local,
        mesh=mesh,
        in_specs=(
            P("db", "rack"), P("db", "rack"), P("db", None, None), P(None, "rack"), P(None, "rack"), P("db", None), P("db", None),
        ),
        out_specs=(P("db", "rack"), P("db", "rack"), P(None, "rack"), P(None, "rack"), P("db", "rack", None)),
        check_vma=False,
    )
```

```python
import functools

import jax
import jax.numpy as jnp
from jax import lax
from jax.experimental import pallas as pl
from jax.experimental.pallas import tpu as pltpu
from jax.sharding import PartitionSpec as P

HD = 128
SPAN = 64
CAP = 3
PARTS = 2
GPARTS = 1
NT = (((1,), (1,)), ((), ()))
TN = (((0,), (0,)), ((), ()))
F32 = jnp.float32
BF16 = jnp.bfloat16


def dot(a, b):
    return jnp.dot(a, b, preferred_element_type=F32)


MESH = pl.DeviceIdType.MESH


class Links:
    def __init__(self, side_z, side_y, side_x):
        db, rack = lax.axis_index("db"), lax.axis_index("rack")
        self.db, self.rack = db, rack
        self.z, self.y = db // side_y, db % side_y
        self.x, self.core = rack // 2, rack % 2
        self.side_x = side_x
        self.ids = {
            ("y", 1): (self.z * side_y + (self.y + 1) % side_y, rack),
            ("y", -1): (self.z * side_y + (self.y + side_y - 1) % side_y, rack),
            ("z", 1): ((self.z + 1) % side_z * side_y + self.y, rack),
            ("z", -1): ((self.z + side_z - 1) % side_z * side_y + self.y, rack),
            ("x", 1): (db, (self.x + 1) % side_x * 2 + self.core),
            ("x", -1): (db, (self.x + side_x - 1) % side_x * 2 + self.core),
            ("core", 1): (db, self.x * 2 + 1 - self.core),
        }

    def place(self, axis):
        return {"y": self.y, "z": self.z, "x": self.x}[axis]


class Mail:
    def __init__(self, send_sems, recv_sems):
        self.send_sems, self.recv_sems, self.book = send_sems, recv_sems, {}

    def plan(self, name, source, target, device):
        self.book[name] = (len(self.book), source, target, device)

    def copy(self, name):
        n, source, target, device = self.book[name]
        return pltpu.make_async_remote_copy(
            src_ref=source(), dst_ref=target(), send_sem=self.send_sems.at[n], recv_sem=self.recv_sems.at[n], device_id=device,
            device_id_type=MESH,
        )

    def start(self, *names):
        for name in names:
            self.copy(name).start()

    def arrive(self, *names):
        for name in names:
            self.copy(name).wait_recv()

    def settle(self):
        for name in self.book:
            self.copy(name).wait_send()


def greet(links, peers):
    barrier = pltpu.get_barrier_semaphore()
    others = [links.ids[("core", 1)], links.ids[("x", 1)], links.ids[("x", -1)]]
    for device in others:
        pl.semaphore_signal(barrier, inc=1, device_id=device, device_id_type=MESH)

    @pl.loop(1, peers)
    def _(far):
        pl.semaphore_signal(barrier, inc=1, device_id=((links.db + far) % peers, links.rack), device_id_type=MESH)

    return len(others) + peers - 1


def add(*terms):
    total = terms[0].astype(F32)
    for term in terms[1:]:
        total = total + term.astype(F32)
    return total.astype(BF16)


class Reduction:
    def __init__(self, tag, links, mail, part, full, first_column, columns, axes, near, far, middle):
        self.tag, self.links, self.mail = tag, links, mail
        self.part, self.full, self.first_column, self.columns = part, full, first_column, columns
        self.near, self.far, self.middle = near, far, middle
        self.rows = part.shape[0] // 4
        self.places = [links.place(axis) for axis in axes]
        self.across = columns // 128
        self.short = self.rows * self.across // 4
        self.sides = [(0, self.rows // 32 * 16), (self.rows // 32 * 16, self.rows - self.rows // 32 * 16)]
        whole = (self.short + 31) // 32 * 16
        self.bits = [(0, whole), (whole, self.short - whole)]
        up = [links.ids[(axis, 1)] for axis in axes]
        down = [links.ids[(axis, -1)] for axis in axes]
        one, two = self.places
        for level, at, buffer, sides, me, k in (("n", self.wide, near, self.sides, one, 0), ("f", self.small, far, self.bits, two, 1)):
            lot = lambda ref, slot, side, sides=sides: (lambda: ref.at[slot, pl.ds(0, sides[side][1])])
            spot = lambda far_off, side, at=at, me=me: (lambda: at((me + far_off) % 4, side))
            self.plan(level + "ra", spot(2, 0), lot(buffer, 0, 0), up[k])
            self.plan(level + "rb", spot(2, 1), lot(buffer, 1, 1), down[k])
            self.plan(level + "db", spot(1, 1), lot(buffer, 3, 1), up[k])
            self.plan(level + "da", spot(3, 0), lot(buffer, 2, 0), down[k])
            self.plan(level + "sa", lot(buffer, 0, 0), lot(buffer, 4, 0), up[k])
            self.plan(level + "sb", lot(buffer, 1, 1), lot(buffer, 5, 1), down[k])
        for level, at, sides, size, me, k in (("g", self.piece, self.bits, self.short, two, 1), ("h", self.band, self.sides, self.rows, one, 0)):
            spot = lambda far_off, first, size, at=at, me=me: (lambda: at((me + far_off) % 4, first, size))
            for name, far_off, (first, length), device in (
                ("up", 0, (0, size), up[k]), ("down", 0, (0, size), down[k]), ("on", 3, sides[0], up[k]), ("back", 1, sides[1], down[k]),
            ):
                self.plan(level + name, spot(far_off, first, length), spot(far_off, first, length), device)

    def plan(self, name, source, target, device):
        self.mail.plan((self.tag, name), source, target, device)

    def start(self, *names):
        self.mail.start(*[(self.tag, name) for name in names])

    def arrive(self, *names):
        self.mail.arrive(*[(self.tag, name) for name in names])

    def wide(self, one, side):
        first, size = self.sides[side]
        return self.part.at[pl.ds(pl.multiple_of(one * self.rows + first, 16), size), pl.ds(self.first_column, self.columns)]

    def small(self, two, side):
        first, size = self.bits[side]
        return self.middle.at[
            pl.ds(pl.multiple_of(two // self.across * self.short + first, 16), size),
            pl.ds(pl.multiple_of(two % self.across * 128, 128), 128),
        ]

    def piece(self, two, first, size):
        row = self.places[0] * self.rows + two // self.across * self.short + first
        column = self.first_column + two % self.across * 128
        return self.full.at[pl.ds(pl.multiple_of(row, 16), size), pl.ds(pl.multiple_of(column, 128), 128)]

    def band(self, one, first, size):
        return self.full.at[pl.ds(pl.multiple_of(one * self.rows + first, 16), size), pl.ds(self.first_column, self.columns)]

    def join(self, level, at, buffer, sides, me):
        for side, letter, far_off in ((0, "a", 1), (1, "b", 3)):
            size = sides[side][1]
            self.arrive(level + "r" + letter)
            buffer[side, :size] = add(buffer[side, :size], at((me + far_off) % 4, side)[...])
            self.start(level + "s" + letter)

    def total(self, level, at, buffer, sides, me, side):
        letter, size = "ab"[side], sides[side][1]
        self.arrive(level + "d" + letter, level + "s" + letter)
        return add(buffer[2 + side, :size], buffer[4 + side, :size], at(me, side)[...])

    def stage(self, number):
        one, two = self.places
        if number == 0:
            self.start("nra", "nrb", "ndb", "nda")
        elif number == 1:
            self.join("n", self.wide, self.near, self.sides, one)
        elif number == 2:
            for side, (first, size) in enumerate(self.sides):
                self.middle[first:first + size, :] = self.total("n", self.wide, self.near, self.sides, one, side)
            self.start("fra", "frb", "fdb", "fda")
        elif number == 3:
            self.join("f", self.small, self.far, self.bits, two)
        elif number == 4:
            for side, (first, size) in enumerate(self.bits):
                self.piece(two, first, size)[...] = self.total("f", self.small, self.far, self.bits, two, side)
            self.start("gup", "gdown")
        elif number == 6:
            self.arrive("gon", "gback")
            self.start("hup", "hdown")
        elif number == 8:
            self.arrive("hon", "hback")
        else:
            level = "g" if number == 5 else "h"
            self.arrive(level + "up")
            self.start(level + "on")
            self.arrive(level + "down")
            self.start(level + "back")


class Return:
    def __init__(self, tag, links, mail, use_grad, user, returned, crossed, ring, mine, leaving, leave_sems, land_sems):
        self.tag = tag
        self.links, self.mail, self.use_grad, self.user, self.returned = links, mail, use_grad, user, returned
        self.crossed, self.ring, self.mine, self.leaving = crossed, ring, mine, leaving
        self.leave_sems, self.land_sems = leave_sems, land_sems
        self.half = mine.shape[0] // 2
        up, down, across = links.ids[("x", 1)], links.ids[("x", -1)], links.ids[("core", 1)]
        for side in (0, 1):
            for far_off in (2, 1, 3, 0):
                mail.plan((tag, "c", far_off, side), self.partner(far_off, side), self.spot(far_off, side), across)
        slot = lambda n: (lambda: ring.at[n])
        mail.plan((tag, "xra"), self.spot(2, 0), slot(0), up)
        mail.plan((tag, "xda"), self.spot(3, 0), slot(2), down)
        mail.plan((tag, "xrb"), self.spot(2, 1), slot(1), down)
        mail.plan((tag, "xdb"), self.spot(1, 1), slot(3), up)
        mail.plan((tag, "xsa"), slot(0), slot(4), up)
        mail.plan((tag, "xsb"), slot(1), slot(5), down)

    def uses(self, side):
        return pl.ds(side * self.half, self.half)

    def spot(self, far_off, side):
        return lambda: self.crossed.at[(self.links.x + far_off) % 4, self.uses(side)]

    def partner(self, far_off, side):
        return lambda: self.use_grad.at[(self.links.x + far_off) % 4 * 2 + 1 - self.links.core, self.uses(side)]

    def cross(self):
        self.mail.start(*[(self.tag, "c", far_off, side) for far_off in (2, 1, 3, 0) for side in (0, 1)])

    def ring_out(self):
        links, mail, half = self.links, self.mail, self.half
        for far_off, names in ((2, ("xra", "xrb")), (1, (None, "xdb")), (3, ("xda", None)), (0, (None, None))):
            x = (links.x + far_off) % 4
            for side, name in enumerate(names):
                mail.arrive((self.tag, "c", far_off, side))

                @pl.loop(side * half, (side + 1) * half)
                def _(n):
                    self.crossed[x, n] = add(self.crossed[x, n], self.use_grad[x * 2 + links.core, n])

                if name:
                    mail.start((self.tag, name))

    def ring_on(self):
        for side in (0, 1):
            self.pass_on(side)

    def ring_end(self):
        for side in (0, 1):
            self.finish(side)

    def pass_on(self, side):
        letter, far_off = ("a", 1) if side == 0 else ("b", 3)
        self.mail.arrive((self.tag, "xr" + letter))
        own = self.spot(far_off, side)()

        @pl.loop(0, self.half)
        def _(n):
            self.ring[side, n] = add(self.ring[side, n], own[n])

        self.mail.start((self.tag, "xs" + letter))

    def finish(self, side):
        letter = "ab"[side]
        self.mail.arrive((self.tag, "xd" + letter), (self.tag, "xs" + letter))
        own = self.spot(0, side)()

        @pl.loop(0, self.half)
        def _(n):
            self.mine[side * self.half + n] = add(self.ring[2 + side, n], self.ring[4 + side, n], own[n])

    def post(self):
        links, peers = self.links, self.returned.shape[0]
        self.mine[2 * self.half] = jnp.zeros(self.mine.shape[1:], BF16)

        def fill(peer, target):
            for k in range(CAP):
                target[peer, k] = self.mine[self.user[peer, 0, k]]

        @pl.loop(1, peers)
        def _(far_off):
            fill((links.db + far_off) % peers, self.leaving)
            self.copy(far_off).start()

        fill(links.db, self.returned)

    def received(self):
        pl.loop(1, self.returned.shape[0])(lambda far_off: self.copy(far_off).wait())

    def copy(self, far_off):
        links = self.links
        peer = (links.db + far_off) % self.returned.shape[0]
        return pltpu.make_async_remote_copy(
            src_ref=self.leaving.at[peer], dst_ref=self.returned.at[links.db], send_sem=self.leave_sems.at[far_off],
            recv_sem=self.land_sems.at[far_off], device_id=(peer, links.rack), device_id_type=MESH,
        )


def block_step(step, spans, heads, panels, queries, cotangent, w_key, w_value, attended, grad_queries, part_key, part_value,
               use_grad, flipped, rows_kv, grads_kv, left, right, pair, stacked, wide):
    keys = panels.shape[0] // spans
    width = panels.shape[1]
    scale = HD ** -0.5

    @pl.when(step == 0)
    def _():
        left[...] = jnp.zeros_like(left)
        right[...] = jnp.zeros_like(right)
        for c in range(spans):
            flipped[:, c * keys:(c + 1) * keys] = panels[c * keys:(c + 1) * keys, :].T

    @pl.when(step < heads)
    def _():
        columns = pl.ds(pl.multiple_of(step * HD, HD), HD)
        wide[:, :HD] = w_key[:, columns]
        wide[:, HD:] = w_value[:, columns]

        @pl.loop(0, PARTS)
        def _(n):
            size = panels.shape[0] // PARTS
            at = pl.ds(pl.multiple_of(n * size, size), size)
            rows_kv[at, :] = dot(panels[at, :], wide[...]).astype(BF16)

        for c in range(spans):
            tokens = slice(c * SPAN, (c + 1) * SPAN)
            query, grad = queries[tokens, :], cotangent[tokens, :]
            left[c, :SPAN, :HD] = query
            left[c, SPAN:, HD:] = grad
            right[c, :SPAN, HD:] = grad
            right[c, SPAN:, :HD] = query
        for c in range(spans):
            pair[c] = lax.dot_general(left[c], rows_kv[c * keys:(c + 1) * keys, :], NT, preferred_element_type=F32)
        for c in range(spans):
            scores = pair[c, :SPAN] * scale
            raised = jnp.exp(scores - jnp.max(scores, axis=-1, keepdims=True))
            probs = raised * (1.0 / jnp.sum(raised, axis=-1, keepdims=True))
            stacked[c, :SPAN] = probs.astype(BF16)
            grad_probs = pair[c, SPAN:]
            delta = jnp.sum(probs * grad_probs, axis=-1, keepdims=True)
            stacked[c, SPAN:] = (probs * (grad_probs - delta) * scale).astype(BF16)
        for c in range(spans):
            tokens = slice(c * SPAN, (c + 1) * SPAN)
            own = slice(c * keys, (c + 1) * keys)
            out = dot(stacked[c], rows_kv[own, :])
            attended[tokens, :] = out[:SPAN, HD:].astype(BF16)
            grad_queries[tokens, :] = out[SPAN:, :HD].astype(BF16)
        for c in range(spans):
            own = slice(c * keys, (c + 1) * keys)
            grads_kv[step, own, :] = lax.dot_general(stacked[c], right[c], TN, preferred_element_type=F32).astype(BF16)

        @pl.loop(0, GPARTS)
        def _(n):
            size = width // GPARTS
            share = part_key.shape[2] // HD
            pair_of, column_of = step // share, pl.ds(pl.multiple_of(step % share * HD, HD), HD)
            at = pl.ds(pl.multiple_of(n * size, size), size)
            total = dot(flipped[at, :], grads_kv[step]).astype(BF16)
            part_key[pair_of, at, column_of] = total[:, :HD]
            part_value[pair_of, at, column_of] = total[:, HD:]

    for part in range(len(CUTS) - 1):
        first, last = CUTS[part], CUTS[part + 1]

        @pl.when((step >= heads + part * QUARTERS) & (step < heads + (part + 1) * QUARTERS))
        def _():
            pieces, uses, rows = use_grad[part].shape[0], use_grad[part].shape[1] // QUARTERS, use_grad[part].shape[2]
            c = step - heads - part * QUARTERS
            size = panels.shape[0] // QUARTERS
            own = pl.ds(pl.multiple_of(c * size, size), size)
            total = jnp.zeros((size, last - first), F32)
            for h in range(heads):
                columns = slice(h * HD, (h + 1) * HD)
                weights = jnp.concatenate([w_key[first:last, columns], w_value[first:last, columns]], axis=1)
                total = total + lax.dot_general(grads_kv[h, own, :], weights, NT, preferred_element_type=F32)
            total = total.astype(BF16)
            for n in range(uses):
                for r in range(pieces):
                    at = (n * pieces + r) * rows
                    use_grad[part][r, c * uses + n, :, :] = total[at:at + rows, :]


QUARTERS = 4
CUTS = (0, 512, 896)
GROUPS = 4


def block_kernel(spans, heads, user, panels, queries, cotangent, w_key, w_value, attended, grad_queries, out_key, out_value,
                 out_returned, full_key, full_value, returned, flipped, rows_kv, grads_kv, left, right, pair, stacked, wide, part_key, part_value, use_grad, near, far,
                 middle, crossed, ring, mine, leaving, send_sems, recv_sems, leave_sems, land_sems, out_sems):
    step = pl.program_id(0)
    links = Links(4, 4, 4)
    mail = Mail(send_sems, recv_sems)
    columns = part_key.shape[2]
    items = []
    for g in range(GROUPS):
        for m, (part, full, axes) in enumerate(((part_key, full_key, "yz"), (part_value, full_value, "zy"))):
            n = g * 2 + m
            items.append(Reduction(n, links, mail, part.at[g], full.at[g], 0, columns, axes, near.at[n], far.at[n], middle.at[n]))
    parts = range(len(CUTS) - 1)
    back = [
        Return("lr"[c], links, mail, use_grad[c], user, returned[c], crossed[c], ring[c], mine[c], leaving[c], leave_sems.at[c], land_sems.at[c])
        for c in parts
    ]

    def advance(*moves):
        for g, number in moves:
            items[2 * g].stage(number)
            items[2 * g + 1].stage(number)
            if number == 8:
                result(g, 0).start()
                result(g, 1).start()

    def result(g, m):
        source, target = ((full_key, out_key), (full_value, out_value))[m]
        return pltpu.make_async_copy(source.at[g], target.at[:, pl.ds(g * columns, columns)], out_sems.at[2 * g + m])

    @pl.when(step == 0)
    def _():
        greet(links, user.shape[0])

    block_step(step, spans, heads, panels, queries, cotangent, w_key, w_value, attended, grad_queries, part_key, part_value,
               use_grad, flipped, rows_kv, grads_kv, left, right, pair, stacked, wide)

    for after in range(1, heads):
        moves = [(g, after - 2 * g - 1) for g in reversed(range(GROUPS)) if 0 <= after - 2 * g - 1 <= 8]

        @pl.when(step == after)
        def _():
            if after == 1:
                pl.semaphore_wait(pltpu.get_barrier_semaphore(), 3 + user.shape[0] - 1)
            advance(*moves)

    @pl.when(step == heads + 3)
    def _():
        back[0].cross()
        advance((3, 1), (2, 3), (1, 5), (0, 7))

    @pl.when(step == heads + 2 * QUARTERS - 1)
    def _():
        back[1].cross()
        back[0].ring_out()
        advance((3, 2), (2, 4), (1, 6), (0, 8))
        advance((3, 3), (2, 5), (1, 7))
        back[0].ring_on()
        back[1].ring_out()
        advance((3, 4), (2, 6), (1, 8))
        advance((3, 5), (2, 7))
        back[0].ring_end()
        advance((3, 6), (2, 8))
        back[0].post()
        back[1].ring_on()
        advance((3, 7))
        back[1].ring_end()
        back[1].post()
        advance((3, 8))
        last = []
        for c in parts:
            back[c].received()
            target = out_returned.at[:, :, :, pl.ds(CUTS[c], CUTS[c + 1] - CUTS[c])]
            last.append(pltpu.make_async_copy(returned[c], target, out_sems.at[2 * GROUPS + c]))
            last[c].start()
        mail.settle()
        for g in range(GROUPS):
            result(g, 0).wait()
            result(g, 1).wait()
        for copy in last:
            copy.wait()


def block_call(user, panels, queries, cotangent, w_key, w_value, racks, peers):
    uses, panel_len, width = panels.shape
    spans = queries.shape[0] // SPAN
    features = w_key.shape[1]
    heads = features // HD
    rows = panel_len // racks
    total = uses * panel_len
    columns = features // GROUPS
    messages = 2 * GROUPS * 20 + 28
    cut = lambda *shape: [pltpu.VMEM(shape + (CUTS[c + 1] - CUTS[c],), BF16) for c in range(len(CUTS) - 1)]
    by_head = lambda size: pl.BlockSpec((size, HD), lambda i: (0, jnp.minimum(i, heads - 1)))
    whole = lambda a, b: pl.BlockSpec((a, b), lambda i: (0, 0), pipeline_mode=pl.Buffered(1))
    anywhere = pl.BlockSpec(memory_space=pl.ANY)
    return pl.pallas_call(
        functools.partial(block_kernel, spans, heads),
        grid=(heads + 2 * QUARTERS,),
        out_shape=(
            jax.ShapeDtypeStruct(queries.shape, BF16),
            jax.ShapeDtypeStruct(queries.shape, BF16),
            jax.ShapeDtypeStruct((width, features), BF16),
            jax.ShapeDtypeStruct((width, features), BF16),
            jax.ShapeDtypeStruct((peers, CAP, rows, width), BF16),
        ),
        in_specs=[
            pl.BlockSpec(memory_space=pltpu.SMEM), whole(total, width), by_head(queries.shape[0]), by_head(queries.shape[0]),
            whole(width, features), whole(width, features),
        ],
        out_specs=[by_head(queries.shape[0]), by_head(queries.shape[0]), anywhere, anywhere, anywhere],
        scratch_shapes=[
            pltpu.VMEM((GROUPS, width, columns), BF16),
            pltpu.VMEM((GROUPS, width, columns), BF16),
            cut(peers, CAP, rows),
            pltpu.VMEM((width, total), BF16),
            pltpu.VMEM((total, 2 * HD), BF16),
            pltpu.VMEM((heads, total, 2 * HD), BF16),
            pltpu.VMEM((spans, 2 * SPAN, 2 * HD), BF16),
            pltpu.VMEM((spans, 2 * SPAN, 2 * HD), BF16),
            pltpu.VMEM((spans, 2 * SPAN, total // spans), F32),
            pltpu.VMEM((spans, 2 * SPAN, total // spans), BF16),
            pltpu.VMEM((width, 2 * HD), BF16),
            pltpu.VMEM((GROUPS, width, columns), BF16),
            pltpu.VMEM((GROUPS, width, columns), BF16),
            cut(racks, uses, rows),
            pltpu.VMEM((2 * GROUPS, 6, width // 8, columns), BF16),
            pltpu.VMEM((2 * GROUPS, 6, 64, 128), BF16),
            pltpu.VMEM((2 * GROUPS, width // 4, columns), BF16),
            cut(4, uses, rows),
            cut(6, uses // 2, rows),
            cut(uses + 1, rows),
            cut(peers, CAP, rows),
            pltpu.SemaphoreType.DMA((messages,)),
            pltpu.SemaphoreType.DMA((messages,)),
            pltpu.SemaphoreType.DMA((len(CUTS) - 1, peers)),
            pltpu.SemaphoreType.DMA((len(CUTS) - 1, peers)),
            pltpu.SemaphoreType.DMA((2 * GROUPS + 2,)),
        ],
        compiler_params=pltpu.CompilerParams(
            collective_id=1, has_side_effects=True, vmem_limit_bytes=58 * 1024 * 1024
        ),
        name="block",
    )(user, panels.reshape(total, width), queries, cotangent, w_key, w_value)


def fetch_kernel(cuts, owners, slots, database, panels, asked, user, stored, wanted, heard, leaving, landing, mine, load_sem, ask_send,
                 ask_recv, leave_sems, land_sems, own_sems, send_sems, recv_sems):
    links = Links(4, 4, 4)
    peers = asked.shape[0]
    local_rows, _, width = stored.shape
    uses, rows = mine.shape[0], mine.shape[1]
    nbrs = owners.shape[1]
    my_rows = lambda x, core: pl.ds(pl.multiple_of((x * 2 + core) * rows, rows), rows)
    load = pltpu.make_async_copy(database.at[:, my_rows(links.x, links.core), :], stored, load_sem.at[0])
    load.start()
    signals = greet(links, peers)
    pl.semaphore_wait(pltpu.get_barrier_semaphore(), signals)

    peer_of = lax.broadcasted_iota(jnp.int32, (peers, 1, 128), 0)
    lane = lax.broadcasted_iota(jnp.int32, (peers, 1, 128), 2)
    seen = jnp.zeros((peers, 1, 128), jnp.int32)
    rows_wanted = jnp.full((peers, 1, 128), local_rows, jnp.int32)
    users = jnp.full((peers, 1, 128), uses, jnp.int32)
    for u in range(uses):
        named = peer_of == owners[u // nbrs, u % nbrs]
        here = named & (lane == seen)
        rows_wanted = jnp.where(here, slots[u // nbrs, u % nbrs], rows_wanted)
        users = jnp.where(here, u, users)
        seen = seen + named.astype(jnp.int32)
    wanted[...] = rows_wanted
    user[...] = users

    def ask(far):
        peer = (links.db + far) % peers
        return pltpu.make_async_remote_copy(
            src_ref=wanted.at[peer], dst_ref=asked.at[links.db], send_sem=ask_send.at[far], recv_sem=ask_recv.at[far],
            device_id=(peer, links.rack), device_id_type=MESH,
        )

    pl.loop(1, peers)(lambda far: ask(far).start())
    asked[links.db] = wanted[links.db]
    load.wait()
    pl.loop(1, peers)(lambda far: ask(far).wait())
    tables = pltpu.make_async_copy(asked, heard, load_sem.at[1])
    tables.start()
    tables.wait()

    def answer(c, far):
        peer = (links.db + far) % peers
        return pltpu.make_async_remote_copy(
            src_ref=leaving[c].at[peer], dst_ref=landing[c].at[links.db], send_sem=leave_sems.at[c, far],
            recv_sem=land_sems.at[c, far], device_id=(peer, links.rack), device_id_type=MESH,
        )

    def fill(c, peer, target):
        for k in range(CAP):
            row = jnp.minimum(heard[peer, 0, k], local_rows - 1)
            target[peer, k] = stored[row, :, cuts[c]:cuts[c + 1]]

    for c in range(len(cuts) - 1):
        @pl.loop(1, peers)
        def _(far):
            fill(c, (links.db + far) % peers, leaving[c])
            answer(c, far).start()

        fill(c, links.db, landing[c])

    mail = Mail(send_sems, recv_sems)
    up, down, across = links.ids[("x", 1)], links.ids[("x", -1)], links.ids[("core", 1)]
    own_copies = []
    half = uses // 2

    def out(c, far, first, size):
        return panels.at[pl.ds(first, size), my_rows((links.x + far) % 4, links.core), pl.ds(cuts[c], cuts[c + 1] - cuts[c])]

    def pass_on(name, c, far, first, size, device):
        spot = lambda: out(c, far, first, size)
        mail.plan((name, c), spot, spot, device)
        mail.start((name, c))

    def exchange(c):
        mail.arrive(("up", c))
        pass_on("on", c, 3, 0, half, up)
        pass_on("cross3", c, 3, 0, uses, across)
        mail.arrive(("down", c))
        pass_on("back", c, 1, half, half, down)
        pass_on("cross1", c, 1, 0, uses, across)

    def finish(c):
        mail.arrive(("on", c))
        pass_on("cross2a", c, 2, 0, half, across)
        mail.arrive(("back", c))
        pass_on("cross2b", c, 2, half, half, across)

    count = len(cuts) - 1
    for c in range(count):
        pl.loop(1, peers)(lambda far: answer(c, far).wait())
        for u in range(uses):
            owner = owners[u // nbrs, u % nbrs]
            rank = jnp.int32(0)
            for v in range(u):
                rank = rank + (owners[v // nbrs, v % nbrs] == owner).astype(jnp.int32)
            mine[u, :, cuts[c]:cuts[c + 1]] = landing[c][owner, jnp.minimum(rank, CAP - 1)]
        source = mine.at[:, :, pl.ds(cuts[c], cuts[c + 1] - cuts[c])]
        target = out(c, 0, 0, uses)
        for name, device in (("up", up), ("down", down), ("cross0", across)):
            mail.plan((name, c), lambda source=source: source, lambda target=target: target, device)
            mail.start((name, c))
        copy = pltpu.make_async_copy(source, target, own_sems.at[c])
        copy.start()
        own_copies.append(copy)
        if c > 0:
            exchange(c - 1)
    exchange(count - 1)
    for c in range(count):
        finish(c)
    for c in range(count):
        mail.arrive(("cross0", c), ("cross1", c), ("cross3", c), ("cross2a", c), ("cross2b", c))
    for copy in own_copies:
        copy.wait()
    mail.settle()


def fetch_call(owners, slots, database, peers, racks):
    uses = owners.shape[0] * owners.shape[1]
    local_rows, panel_len, width = database.shape
    rows = panel_len // racks
    parts = len(CUTS) - 1
    chunk = lambda c: pltpu.VMEM((peers, CAP, rows, CUTS[c + 1] - CUTS[c]), BF16)
    vmem = pl.BlockSpec(memory_space=pltpu.VMEM)
    smem = pl.BlockSpec(memory_space=pltpu.SMEM)
    anywhere = pl.BlockSpec(memory_space=pl.ANY)
    sems = pltpu.SemaphoreType.DMA
    return pl.pallas_call(
        functools.partial(fetch_kernel, CUTS),
        out_shape=(
            jax.ShapeDtypeStruct((uses, panel_len, width), BF16),
            jax.ShapeDtypeStruct((peers, 1, 128), jnp.int32),
            jax.ShapeDtypeStruct((peers, 1, 128), jnp.int32),
        ),
        in_specs=[smem, smem, pl.BlockSpec(memory_space=pltpu.HBM)],
        out_specs=(anywhere, vmem, vmem),
        scratch_shapes=[
            pltpu.VMEM((local_rows, rows, width), BF16),
            pltpu.VMEM((peers, 1, 128), jnp.int32),
            pltpu.SMEM((peers, 1, 128), jnp.int32),
            [chunk(c) for c in range(parts)],
            [chunk(c) for c in range(parts)],
            pltpu.VMEM((uses, rows, width), BF16),
            sems((2,)), sems((peers,)), sems((peers,)), sems((parts, peers)), sems((parts, peers)), sems((parts,)),
            sems((9 * parts,)), sems((9 * parts,)),
        ],
        compiler_params=pltpu.CompilerParams(
            collective_id=0, has_side_effects=True, vmem_limit_bytes=58 * 1024 * 1024
        ),
        name="fetch",
    )(owners, slots, database)


def pick(selector, source):
    return jnp.einsum("ns,spw->npw", selector, source, preferred_element_type=F32).astype(BF16)


def local(queries, cotangent, database, w_key, w_value, neighbour_owner, neighbour_slot):
    peer_count = lax.axis_size("db")
    racks = lax.axis_size("rack")
    local_rows, _, width = database.shape
    rows = database.shape[1] // racks
    panels, asked, user = fetch_call(neighbour_owner, neighbour_slot, database, peer_count, racks)
    asked_rows = asked[:, 0, :CAP].reshape(peer_count * CAP)
    selector = (asked_rows[:, None] == jnp.arange(local_rows, dtype=jnp.int32)[None, :]).astype(BF16)
    attended, grad_query, full_key, full_value, returned = block_call(
        user, panels, queries, cotangent, w_key, w_value, racks, peer_count
    )
    grad_w_key, grad_w_value = full_key.astype(F32), full_value.astype(F32)
    grad_database = pick(selector.T, returned.reshape(peer_count * CAP, rows, width))
    return attended, grad_query, grad_w_key, grad_w_value, grad_database


def solution(mesh):
    return jax.shard_map(
        local,
        mesh=mesh,
        in_specs=(
            P("db", "rack"), P("db", "rack"), P("db", None, None), P(None, "rack"), P(None, "rack"), P("db", None), P("db", None),
        ),
        out_specs=(P("db", "rack"), P("db", "rack"), P(None, "rack"), P(None, "rack"), P("db", "rack", None)),
        check_vma=False,
    )
```

```python
import functools

import jax
import jax.numpy as jnp
from jax import lax
from jax.experimental import pallas as pl
from jax.experimental.pallas import tpu as pltpu
from jax.sharding import PartitionSpec as P

HD = 128
SPAN = 64
CAP = 3
PARTS = 2
GPARTS = 1
NT = (((1,), (1,)), ((), ()))
TN = (((0,), (0,)), ((), ()))
F32 = jnp.float32
BF16 = jnp.bfloat16


def dot(a, b):
    return jnp.dot(a, b, preferred_element_type=F32)


MESH = pl.DeviceIdType.MESH


class Links:
    def __init__(self, side_z, side_y, side_x):
        db, rack = lax.axis_index("db"), lax.axis_index("rack")
        self.db, self.rack = db, rack
        self.z, self.y = db // side_y, db % side_y
        self.x, self.core = rack // 2, rack % 2
        self.side_x = side_x
        self.ids = {
            ("y", 1): (self.z * side_y + (self.y + 1) % side_y, rack),
            ("y", -1): (self.z * side_y + (self.y + side_y - 1) % side_y, rack),
            ("z", 1): ((self.z + 1) % side_z * side_y + self.y, rack),
            ("z", -1): ((self.z + side_z - 1) % side_z * side_y + self.y, rack),
            ("x", 1): (db, (self.x + 1) % side_x * 2 + self.core),
            ("x", -1): (db, (self.x + side_x - 1) % side_x * 2 + self.core),
            ("core", 1): (db, self.x * 2 + 1 - self.core),
        }

    def place(self, axis):
        return {"y": self.y, "z": self.z, "x": self.x}[axis]


class Mail:
    def __init__(self, send_sems, recv_sems):
        self.send_sems, self.recv_sems, self.book = send_sems, recv_sems, {}

    def plan(self, name, source, target, device):
        self.book[name] = (len(self.book), source, target, device)

    def copy(self, name):
        n, source, target, device = self.book[name]
        return pltpu.make_async_remote_copy(
            src_ref=source(), dst_ref=target(), send_sem=self.send_sems.at[n], recv_sem=self.recv_sems.at[n], device_id=device,
            device_id_type=MESH,
        )

    def start(self, *names):
        for name in names:
            self.copy(name).start()

    def arrive(self, *names):
        for name in names:
            self.copy(name).wait_recv()

    def settle(self):
        for name in self.book:
            self.copy(name).wait_send()


def greet(links, peers):
    barrier = pltpu.get_barrier_semaphore()
    others = [links.ids[("core", 1)], links.ids[("x", 1)], links.ids[("x", -1)]]
    for device in others:
        pl.semaphore_signal(barrier, inc=1, device_id=device, device_id_type=MESH)

    @pl.loop(1, peers)
    def _(far):
        pl.semaphore_signal(barrier, inc=1, device_id=((links.db + far) % peers, links.rack), device_id_type=MESH)

    return len(others) + peers - 1


def add(*terms):
    total = terms[0].astype(F32)
    for term in terms[1:]:
        total = total + term.astype(F32)
    return total.astype(BF16)


class Reduction:
    def __init__(self, tag, links, mail, part, full, first_column, columns, axes, near, far, middle):
        self.tag, self.links, self.mail = tag, links, mail
        self.part, self.full, self.first_column, self.columns = part, full, first_column, columns
        self.near, self.far, self.middle = near, far, middle
        self.rows = part.shape[0] // 4
        self.places = [links.place(axis) for axis in axes]
        self.across = columns // 128
        self.short = self.rows * self.across // 4
        self.sides = [(0, self.rows // 32 * 16), (self.rows // 32 * 16, self.rows - self.rows // 32 * 16)]
        whole = (self.short + 31) // 32 * 16
        self.bits = [(0, whole), (whole, self.short - whole)]
        up = [links.ids[(axis, 1)] for axis in axes]
        down = [links.ids[(axis, -1)] for axis in axes]
        one, two = self.places
        for level, at, buffer, sides, me, k in (("n", self.wide, near, self.sides, one, 0), ("f", self.small, far, self.bits, two, 1)):
            lot = lambda ref, slot, side, sides=sides: (lambda: ref.at[slot, pl.ds(0, sides[side][1])])
            spot = lambda far_off, side, at=at, me=me: (lambda: at((me + far_off) % 4, side))
            self.plan(level + "ra", spot(2, 0), lot(buffer, 0, 0), up[k])
            self.plan(level + "rb", spot(2, 1), lot(buffer, 1, 1), down[k])
            self.plan(level + "db", spot(1, 1), lot(buffer, 3, 1), up[k])
            self.plan(level + "da", spot(3, 0), lot(buffer, 2, 0), down[k])
            self.plan(level + "sa", lot(buffer, 0, 0), lot(buffer, 4, 0), up[k])
            self.plan(level + "sb", lot(buffer, 1, 1), lot(buffer, 5, 1), down[k])
        for level, at, sides, size, me, k in (("g", self.piece, self.bits, self.short, two, 1), ("h", self.band, self.sides, self.rows, one, 0)):
            spot = lambda far_off, first, size, at=at, me=me: (lambda: at((me + far_off) % 4, first, size))
            for name, far_off, (first, length), device in (
                ("up", 0, (0, size), up[k]), ("down", 0, (0, size), down[k]), ("on", 3, sides[0], up[k]), ("back", 1, sides[1], down[k]),
            ):
                self.plan(level + name, spot(far_off, first, length), spot(far_off, first, length), device)

    def plan(self, name, source, target, device):
        self.mail.plan((self.tag, name), source, target, device)

    def start(self, *names):
        self.mail.start(*[(self.tag, name) for name in names])

    def arrive(self, *names):
        self.mail.arrive(*[(self.tag, name) for name in names])

    def wide(self, one, side):
        first, size = self.sides[side]
        return self.part.at[pl.ds(pl.multiple_of(one * self.rows + first, 16), size), pl.ds(self.first_column, self.columns)]

    def small(self, two, side):
        first, size = self.bits[side]
        return self.middle.at[
            pl.ds(pl.multiple_of(two // self.across * self.short + first, 16), size),
            pl.ds(pl.multiple_of(two % self.across * 128, 128), 128),
        ]

    def piece(self, two, first, size):
        row = self.places[0] * self.rows + two // self.across * self.short + first
        column = self.first_column + two % self.across * 128
        return self.full.at[pl.ds(pl.multiple_of(row, 16), size), pl.ds(pl.multiple_of(column, 128), 128)]

    def band(self, one, first, size):
        return self.full.at[pl.ds(pl.multiple_of(one * self.rows + first, 16), size), pl.ds(self.first_column, self.columns)]

    def join(self, level, at, buffer, sides, me):
        for side, letter, far_off in ((0, "a", 1), (1, "b", 3)):
            size = sides[side][1]
            self.arrive(level + "r" + letter)
            buffer[side, :size] = add(buffer[side, :size], at((me + far_off) % 4, side)[...])
            self.start(level + "s" + letter)

    def total(self, level, at, buffer, sides, me, side):
        letter, size = "ab"[side], sides[side][1]
        self.arrive(level + "d" + letter, level + "s" + letter)
        return add(buffer[2 + side, :size], buffer[4 + side, :size], at(me, side)[...])

    def stage(self, number):
        one, two = self.places
        if number == 0:
            self.start("nra", "nrb", "ndb", "nda")
        elif number == 1:
            self.join("n", self.wide, self.near, self.sides, one)
        elif number == 2:
            for side, (first, size) in enumerate(self.sides):
                self.middle[first:first + size, :] = self.total("n", self.wide, self.near, self.sides, one, side)
            self.start("fra", "frb", "fdb", "fda")
        elif number == 3:
            self.join("f", self.small, self.far, self.bits, two)
        elif number == 4:
            for side, (first, size) in enumerate(self.bits):
                self.piece(two, first, size)[...] = self.total("f", self.small, self.far, self.bits, two, side)
            self.start("gup", "gdown")
        elif number == 6:
            self.arrive("gon", "gback")
            self.start("hup", "hdown")
        elif number == 8:
            self.arrive("hon", "hback")
        else:
            level = "g" if number == 5 else "h"
            self.arrive(level + "up")
            self.start(level + "on")
            self.arrive(level + "down")
            self.start(level + "back")


class Return:
    def __init__(self, tag, links, mail, use_grad, user, returned, crossed, ring, mine, leaving, leave_sems, land_sems):
        self.tag = tag
        self.links, self.mail, self.use_grad, self.user, self.returned = links, mail, use_grad, user, returned
        self.crossed, self.ring, self.mine, self.leaving = crossed, ring, mine, leaving
        self.leave_sems, self.land_sems = leave_sems, land_sems
        self.half = mine.shape[0] // 2
        up, down, across = links.ids[("x", 1)], links.ids[("x", -1)], links.ids[("core", 1)]
        for side in (0, 1):
            for far_off in (2, 1, 3, 0):
                mail.plan((tag, "c", far_off, side), self.partner(far_off, side), self.spot(far_off, side), across)
        slot = lambda n: (lambda: ring.at[n])
        mail.plan((tag, "xra"), self.spot(2, 0), slot(0), up)
        mail.plan((tag, "xda"), self.spot(3, 0), slot(2), down)
        mail.plan((tag, "xrb"), self.spot(2, 1), slot(1), down)
        mail.plan((tag, "xdb"), self.spot(1, 1), slot(3), up)
        mail.plan((tag, "xsa"), slot(0), slot(4), up)
        mail.plan((tag, "xsb"), slot(1), slot(5), down)

    def uses(self, side):
        return pl.ds(side * self.half, self.half)

    def spot(self, far_off, side):
        return lambda: self.crossed.at[(self.links.x + far_off) % 4, self.uses(side)]

    def partner(self, far_off, side):
        return lambda: self.use_grad.at[(self.links.x + far_off) % 4 * 2 + 1 - self.links.core, self.uses(side)]

    def cross(self):
        self.mail.start(*[(self.tag, "c", far_off, side) for far_off in (2, 1, 3, 0) for side in (0, 1)])

    def ring_out(self):
        links, mail, half = self.links, self.mail, self.half
        for far_off, names in ((2, ("xra", "xrb")), (1, (None, "xdb")), (3, ("xda", None)), (0, (None, None))):
            x = (links.x + far_off) % 4
            for side, name in enumerate(names):
                mail.arrive((self.tag, "c", far_off, side))

                @pl.loop(side * half, (side + 1) * half)
                def _(n):
                    self.crossed[x, n] = add(self.crossed[x, n], self.use_grad[x * 2 + links.core, n])

                if name:
                    mail.start((self.tag, name))

    def ring_on(self):
        for side in (0, 1):
            self.pass_on(side)

    def ring_end(self):
        for side in (0, 1):
            self.finish(side)

    def pass_on(self, side):
        letter, far_off = ("a", 1) if side == 0 else ("b", 3)
        self.mail.arrive((self.tag, "xr" + letter))
        own = self.spot(far_off, side)()

        @pl.loop(0, self.half)
        def _(n):
            self.ring[side, n] = add(self.ring[side, n], own[n])

        self.mail.start((self.tag, "xs" + letter))

    def finish(self, side):
        letter = "ab"[side]
        self.mail.arrive((self.tag, "xd" + letter), (self.tag, "xs" + letter))
        own = self.spot(0, side)()

        @pl.loop(0, self.half)
        def _(n):
            self.mine[side * self.half + n] = add(self.ring[2 + side, n], self.ring[4 + side, n], own[n])

    def post(self):
        links, peers = self.links, self.returned.shape[0]
        self.mine[2 * self.half] = jnp.zeros(self.mine.shape[1:], BF16)

        def fill(peer, target):
            for k in range(CAP):
                target[peer, k] = self.mine[self.user[peer, 0, k]]

        @pl.loop(1, peers)
        def _(far_off):
            fill((links.db + far_off) % peers, self.leaving)
            self.copy(far_off).start()

        fill(links.db, self.returned)

    def received(self):
        pl.loop(1, self.returned.shape[0])(lambda far_off: self.copy(far_off).wait())

    def copy(self, far_off):
        links = self.links
        peer = (links.db + far_off) % self.returned.shape[0]
        return pltpu.make_async_remote_copy(
            src_ref=self.leaving.at[peer], dst_ref=self.returned.at[links.db], send_sem=self.leave_sems.at[far_off],
            recv_sem=self.land_sems.at[far_off], device_id=(peer, links.rack), device_id_type=MESH,
        )


def block_step(step, spans, heads, panels, queries, cotangent, head_key, head_value, w_key, w_value, attended, grad_queries, part_key, part_value,
               use_grad, flipped, rows_kv, grads_kv, left, right, pair, stacked, wide):
    keys = panels.shape[0] // spans
    width = panels.shape[1]
    scale = HD ** -0.5

    @pl.when(step == 0)
    def _():
        left[...] = jnp.zeros_like(left)
        right[...] = jnp.zeros_like(right)
        for c in range(spans):
            flipped[:, c * keys:(c + 1) * keys] = panels[c * keys:(c + 1) * keys, :].T

    @pl.when(step < heads)
    def _():
        wide[:, :HD] = head_key[...]
        wide[:, HD:] = head_value[...]

        @pl.loop(0, PARTS)
        def _(n):
            size = panels.shape[0] // PARTS
            at = pl.ds(pl.multiple_of(n * size, size), size)
            rows_kv[at, :] = dot(panels[at, :], wide[...]).astype(BF16)

        for c in range(spans):
            tokens = slice(c * SPAN, (c + 1) * SPAN)
            query, grad = queries[tokens, :], cotangent[tokens, :]
            left[c, :SPAN, :HD] = query
            left[c, SPAN:, HD:] = grad
            right[c, :SPAN, HD:] = grad
            right[c, SPAN:, :HD] = query
        for c in range(spans):
            pair[c] = lax.dot_general(left[c], rows_kv[c * keys:(c + 1) * keys, :], NT, preferred_element_type=F32)
        for c in range(spans):
            scores = pair[c, :SPAN] * scale
            raised = jnp.exp(scores - jnp.max(scores, axis=-1, keepdims=True))
            probs = raised * (1.0 / jnp.sum(raised, axis=-1, keepdims=True))
            stacked[c, :SPAN] = probs.astype(BF16)
            grad_probs = pair[c, SPAN:]
            delta = jnp.sum(probs * grad_probs, axis=-1, keepdims=True)
            stacked[c, SPAN:] = (probs * (grad_probs - delta) * scale).astype(BF16)
        for c in range(spans):
            tokens = slice(c * SPAN, (c + 1) * SPAN)
            own = slice(c * keys, (c + 1) * keys)
            out = dot(stacked[c], rows_kv[own, :])
            attended[tokens, :] = out[:SPAN, HD:].astype(BF16)
            grad_queries[tokens, :] = out[SPAN:, :HD].astype(BF16)
        for c in range(spans):
            own = slice(c * keys, (c + 1) * keys)
            grads_kv[step, own, :] = lax.dot_general(stacked[c], right[c], TN, preferred_element_type=F32).astype(BF16)

        @pl.loop(0, GPARTS)
        def _(n):
            size = width // GPARTS
            share = part_key.shape[2] // HD
            pair_of, column_of = step // share, pl.ds(pl.multiple_of(step % share * HD, HD), HD)
            at = pl.ds(pl.multiple_of(n * size, size), size)
            total = dot(flipped[at, :], grads_kv[step]).astype(BF16)
            part_key[pair_of, at, column_of] = total[:, :HD]
            part_value[pair_of, at, column_of] = total[:, HD:]

    for part in range(len(CUTS) - 1):
        first, last = CUTS[part], CUTS[part + 1]

        @pl.when((step >= heads + part * QUARTERS) & (step < heads + (part + 1) * QUARTERS))
        def _():
            pieces, uses, rows = use_grad[part].shape[0], use_grad[part].shape[1] // QUARTERS, use_grad[part].shape[2]
            c = step - heads - part * QUARTERS
            size = panels.shape[0] // QUARTERS
            own = pl.ds(pl.multiple_of(c * size, size), size)
            total = jnp.zeros((size, last - first), F32)
            for h in range(heads):
                columns = slice(h * HD, (h + 1) * HD)
                weights = jnp.concatenate([w_key[first:last, columns], w_value[first:last, columns]], axis=1)
                total = total + lax.dot_general(grads_kv[h, own, :], weights, NT, preferred_element_type=F32)
            total = total.astype(BF16)
            for n in range(uses):
                for r in range(pieces):
                    at = (n * pieces + r) * rows
                    use_grad[part][r, c * uses + n, :, :] = total[at:at + rows, :]


QUARTERS = 4
CUTS = (0, 512, 896)
GROUPS = 4


def block_kernel(spans, heads, user, panels, queries, cotangent, head_key, head_value, all_key, all_value, attended, grad_queries,
                 out_key, out_value, out_returned, w_key, w_value, full_key, full_value, returned, flipped, rows_kv, grads_kv, left, right, pair, stacked, wide, part_key, part_value, use_grad, near, far,
                 middle, crossed, ring, mine, leaving, send_sems, recv_sems, leave_sems, land_sems, out_sems, weight_sems):
    step = pl.program_id(0)
    weights = [
        pltpu.make_async_copy(all_key, w_key, weight_sems.at[0]), pltpu.make_async_copy(all_value, w_value, weight_sems.at[1])
    ]
    links = Links(4, 4, 4)
    mail = Mail(send_sems, recv_sems)
    columns = part_key.shape[2]
    items = []
    for g in range(GROUPS):
        for m, (part, full, axes) in enumerate(((part_key, full_key, "yz"), (part_value, full_value, "zy"))):
            n = g * 2 + m
            items.append(Reduction(n, links, mail, part.at[g], full.at[g], 0, columns, axes, near.at[n], far.at[n], middle.at[n]))
    parts = range(len(CUTS) - 1)
    back = [
        Return("lr"[c], links, mail, use_grad[c], user, returned[c], crossed[c], ring[c], mine[c], leaving[c], leave_sems.at[c], land_sems.at[c])
        for c in parts
    ]

    def advance(*moves):
        for g, number in moves:
            items[2 * g].stage(number)
            items[2 * g + 1].stage(number)
            if number == 8:
                result(g, 0).start()
                result(g, 1).start()

    def result(g, m):
        source, target = ((full_key, out_key), (full_value, out_value))[m]
        return pltpu.make_async_copy(source.at[g], target.at[:, pl.ds(g * columns, columns)], out_sems.at[2 * g + m])

    @pl.when(step == 0)
    def _():
        greet(links, user.shape[0])

    @pl.when(step == 0)
    def _():
        for copy in weights:
            copy.start()

    @pl.when(step == heads)
    def _():
        for copy in weights:
            copy.wait()

    block_step(step, spans, heads, panels, queries, cotangent, head_key, head_value, w_key, w_value, attended, grad_queries, part_key, part_value,
               use_grad, flipped, rows_kv, grads_kv, left, right, pair, stacked, wide)

    for after in range(1, heads):
        moves = [(g, after - 2 * g - 1) for g in reversed(range(GROUPS)) if 0 <= after - 2 * g - 1 <= 8]

        @pl.when(step == after)
        def _():
            if after == 1:
                pl.semaphore_wait(pltpu.get_barrier_semaphore(), 3 + user.shape[0] - 1)
            advance(*moves)

    @pl.when(step == heads + 3)
    def _():
        back[0].cross()
        advance((3, 1), (2, 3), (1, 5), (0, 7))

    @pl.when(step == heads + 2 * QUARTERS - 1)
    def _():
        back[1].cross()
        back[0].ring_out()
        advance((3, 2), (2, 4), (1, 6), (0, 8))
        advance((3, 3), (2, 5), (1, 7))
        back[0].ring_on()
        back[1].ring_out()
        advance((3, 4), (2, 6), (1, 8))
        advance((3, 5), (2, 7))
        back[0].ring_end()
        advance((3, 6), (2, 8))
        back[0].post()
        back[1].ring_on()
        advance((3, 7))
        back[1].ring_end()
        back[1].post()
        advance((3, 8))
        last = []
        for c in parts:
            back[c].received()
            target = out_returned.at[:, :, :, pl.ds(CUTS[c], CUTS[c + 1] - CUTS[c])]
            last.append(pltpu.make_async_copy(returned[c], target, out_sems.at[2 * GROUPS + c]))
            last[c].start()
        mail.settle()
        for g in range(GROUPS):
            result(g, 0).wait()
            result(g, 1).wait()
        for copy in last:
            copy.wait()


def block_call(user, panels, queries, cotangent, w_key, w_value, racks, peers):
    uses, panel_len, width = panels.shape
    spans = queries.shape[0] // SPAN
    features = w_key.shape[1]
    heads = features // HD
    rows = panel_len // racks
    total = uses * panel_len
    columns = features // GROUPS
    messages = 2 * GROUPS * 20 + 28
    cut = lambda *shape: [pltpu.VMEM(shape + (CUTS[c + 1] - CUTS[c],), BF16) for c in range(len(CUTS) - 1)]
    by_head = lambda size: pl.BlockSpec((size, HD), lambda i: (0, jnp.minimum(i, heads - 1)))
    whole = lambda a, b: pl.BlockSpec((a, b), lambda i: (0, 0), pipeline_mode=pl.Buffered(1))
    anywhere = pl.BlockSpec(memory_space=pl.ANY)
    return pl.pallas_call(
        functools.partial(block_kernel, spans, heads),
        grid=(heads + 2 * QUARTERS,),
        out_shape=(
            jax.ShapeDtypeStruct(queries.shape, BF16),
            jax.ShapeDtypeStruct(queries.shape, BF16),
            jax.ShapeDtypeStruct((width, features), BF16),
            jax.ShapeDtypeStruct((width, features), BF16),
            jax.ShapeDtypeStruct((peers, CAP, rows, width), BF16),
        ),
        in_specs=[
            pl.BlockSpec(memory_space=pltpu.SMEM), whole(total, width), by_head(queries.shape[0]), by_head(queries.shape[0]),
            by_head(width), by_head(width), anywhere, anywhere,
        ],
        out_specs=[by_head(queries.shape[0]), by_head(queries.shape[0]), anywhere, anywhere, anywhere],
        scratch_shapes=[
            pltpu.VMEM((width, features), BF16),
            pltpu.VMEM((width, features), BF16),
            pltpu.VMEM((GROUPS, width, columns), BF16),
            pltpu.VMEM((GROUPS, width, columns), BF16),
            cut(peers, CAP, rows),
            pltpu.VMEM((width, total), BF16),
            pltpu.VMEM((total, 2 * HD), BF16),
            pltpu.VMEM((heads, total, 2 * HD), BF16),
            pltpu.VMEM((spans, 2 * SPAN, 2 * HD), BF16),
            pltpu.VMEM((spans, 2 * SPAN, 2 * HD), BF16),
            pltpu.VMEM((spans, 2 * SPAN, total // spans), F32),
            pltpu.VMEM((spans, 2 * SPAN, total // spans), BF16),
            pltpu.VMEM((width, 2 * HD), BF16),
            pltpu.VMEM((GROUPS, width, columns), BF16),
            pltpu.VMEM((GROUPS, width, columns), BF16),
            cut(racks, uses, rows),
            pltpu.VMEM((2 * GROUPS, 6, width // 8, columns), BF16),
            pltpu.VMEM((2 * GROUPS, 6, 64, 128), BF16),
            pltpu.VMEM((2 * GROUPS, width // 4, columns), BF16),
            cut(4, uses, rows),
            cut(6, uses // 2, rows),
            cut(uses + 1, rows),
            cut(peers, CAP, rows),
            pltpu.SemaphoreType.DMA((messages,)),
            pltpu.SemaphoreType.DMA((messages,)),
            pltpu.SemaphoreType.DMA((len(CUTS) - 1, peers)),
            pltpu.SemaphoreType.DMA((len(CUTS) - 1, peers)),
            pltpu.SemaphoreType.DMA((2 * GROUPS + 2,)),
            pltpu.SemaphoreType.DMA((2,)),
        ],
        compiler_params=pltpu.CompilerParams(
            collective_id=1, has_side_effects=True, vmem_limit_bytes=58 * 1024 * 1024
        ),
        name="block",
    )(user, panels.reshape(total, width), queries, cotangent, w_key, w_value, w_key, w_value)


def fetch_kernel(cuts, named_rows, database, panels, asked, user, stored, wanted, heard, leaving, landing, mine, load_sem, ask_send,
                 ask_recv, leave_sems, land_sems, own_sems, send_sems, recv_sems):
    links = Links(4, 4, 4)
    peers = asked.shape[0]
    local_rows, _, width = stored.shape
    uses, rows = mine.shape[0], mine.shape[1]
    nbrs = named_rows.shape[1] // 2
    my_rows = lambda x, core: pl.ds(pl.multiple_of((x * 2 + core) * rows, rows), rows)
    load = pltpu.make_async_copy(database.at[:, my_rows(links.x, links.core), :], stored, load_sem.at[0])
    load.start()
    signals = greet(links, peers)
    pl.semaphore_wait(pltpu.get_barrier_semaphore(), signals)

    peer_of = lax.broadcasted_iota(jnp.int32, (peers, 1, 128), 0)
    lane = lax.broadcasted_iota(jnp.int32, (peers, 1, 128), 2)
    seen = jnp.zeros((peers, 1, 128), jnp.int32)
    rows_wanted = jnp.full((peers, 1, 128), local_rows, jnp.int32)
    users = jnp.full((peers, 1, 128), uses, jnp.int32)
    for u in range(uses):
        named = peer_of == named_rows[u // nbrs, u % nbrs]
        here = named & (lane == seen)
        rows_wanted = jnp.where(here, named_rows[u // nbrs, nbrs + u % nbrs], rows_wanted)
        users = jnp.where(here, u, users)
        seen = seen + named.astype(jnp.int32)
    wanted[...] = rows_wanted
    user[...] = users

    def ask(far):
        peer = (links.db + far) % peers
        return pltpu.make_async_remote_copy(
            src_ref=wanted.at[peer], dst_ref=asked.at[links.db], send_sem=ask_send.at[far], recv_sem=ask_recv.at[far],
            device_id=(peer, links.rack), device_id_type=MESH,
        )

    pl.loop(1, peers)(lambda far: ask(far).start())
    asked[links.db] = wanted[links.db]
    load.wait()
    pl.loop(1, peers)(lambda far: ask(far).wait())
    tables = pltpu.make_async_copy(asked, heard, load_sem.at[1])
    tables.start()
    tables.wait()

    def answer(c, far):
        peer = (links.db + far) % peers
        return pltpu.make_async_remote_copy(
            src_ref=leaving[c].at[peer], dst_ref=landing[c].at[links.db], send_sem=leave_sems.at[c, far],
            recv_sem=land_sems.at[c, far], device_id=(peer, links.rack), device_id_type=MESH,
        )

    def fill(c, peer, target):
        for k in range(CAP):
            row = jnp.minimum(heard[peer, 0, k], local_rows - 1)
            target[peer, k] = stored[row, :, cuts[c]:cuts[c + 1]]

    for c in range(len(cuts) - 1):
        @pl.loop(1, peers)
        def _(far):
            fill(c, (links.db + far) % peers, leaving[c])
            answer(c, far).start()

        fill(c, links.db, landing[c])

    mail = Mail(send_sems, recv_sems)
    up, down, across = links.ids[("x", 1)], links.ids[("x", -1)], links.ids[("core", 1)]
    own_copies = []
    half = uses // 2

    def out(c, far, first, size):
        return panels.at[pl.ds(first, size), my_rows((links.x + far) % 4, links.core), pl.ds(cuts[c], cuts[c + 1] - cuts[c])]

    def pass_on(name, c, far, first, size, device):
        spot = lambda: out(c, far, first, size)
        mail.plan((name, c), spot, spot, device)
        mail.start((name, c))

    def exchange(c):
        mail.arrive(("up", c))
        pass_on("on", c, 3, 0, half, up)
        pass_on("cross3", c, 3, 0, uses, across)
        mail.arrive(("down", c))
        pass_on("back", c, 1, half, half, down)
        pass_on("cross1", c, 1, 0, uses, across)

    def finish(c):
        mail.arrive(("on", c))
        pass_on("cross2a", c, 2, 0, half, across)
        mail.arrive(("back", c))
        pass_on("cross2b", c, 2, half, half, across)

    count = len(cuts) - 1
    for c in range(count):
        pl.loop(1, peers)(lambda far: answer(c, far).wait())
        for u in range(uses):
            owner = named_rows[u // nbrs, u % nbrs]
            rank = jnp.int32(0)
            for v in range(u):
                rank = rank + (named_rows[v // nbrs, v % nbrs] == owner).astype(jnp.int32)
            mine[u, :, cuts[c]:cuts[c + 1]] = landing[c][owner, jnp.minimum(rank, CAP - 1)]
        source = mine.at[:, :, pl.ds(cuts[c], cuts[c + 1] - cuts[c])]
        target = out(c, 0, 0, uses)
        for name, device in (("up", up), ("down", down), ("cross0", across)):
            mail.plan((name, c), lambda source=source: source, lambda target=target: target, device)
            mail.start((name, c))
        copy = pltpu.make_async_copy(source, target, own_sems.at[c])
        copy.start()
        own_copies.append(copy)
        if c > 0:
            exchange(c - 1)
    exchange(count - 1)
    for c in range(count):
        finish(c)
    for c in range(count):
        mail.arrive(("cross0", c), ("cross1", c), ("cross3", c), ("cross2a", c), ("cross2b", c))
    for copy in own_copies:
        copy.wait()
    mail.settle()


def fetch_call(owners, slots, database, peers, racks):
    uses = owners.shape[0] * owners.shape[1]
    local_rows, panel_len, width = database.shape
    rows = panel_len // racks
    parts = len(CUTS) - 1
    chunk = lambda c: pltpu.VMEM((peers, CAP, rows, CUTS[c + 1] - CUTS[c]), BF16)
    vmem = pl.BlockSpec(memory_space=pltpu.VMEM)
    smem = pl.BlockSpec(memory_space=pltpu.SMEM)
    anywhere = pl.BlockSpec(memory_space=pl.ANY)
    sems = pltpu.SemaphoreType.DMA
    return pl.pallas_call(
        functools.partial(fetch_kernel, CUTS),
        out_shape=(
            jax.ShapeDtypeStruct((uses, panel_len, width), BF16),
            jax.ShapeDtypeStruct((peers, 1, 128), jnp.int32),
            jax.ShapeDtypeStruct((peers, 1, 128), jnp.int32),
        ),
        in_specs=[smem, pl.BlockSpec(memory_space=pltpu.HBM)],
        out_specs=(anywhere, vmem, vmem),
        scratch_shapes=[
            pltpu.VMEM((local_rows, rows, width), BF16),
            pltpu.VMEM((peers, 1, 128), jnp.int32),
            pltpu.SMEM((peers, 1, 128), jnp.int32),
            [chunk(c) for c in range(parts)],
            [chunk(c) for c in range(parts)],
            pltpu.VMEM((uses, rows, width), BF16),
            sems((2,)), sems((peers,)), sems((peers,)), sems((parts, peers)), sems((parts, peers)), sems((parts,)),
            sems((9 * parts,)), sems((9 * parts,)),
        ],
        compiler_params=pltpu.CompilerParams(
            collective_id=0, has_side_effects=True, vmem_limit_bytes=58 * 1024 * 1024
        ),
        name="fetch",
    )(jnp.concatenate([owners, slots], axis=1), database)


def pick(selector, source):
    return jnp.einsum("ns,spw->npw", selector, source, preferred_element_type=F32).astype(BF16)


def local(queries, cotangent, database, w_key, w_value, neighbour_owner, neighbour_slot):
    peer_count = lax.axis_size("db")
    racks = lax.axis_size("rack")
    local_rows, _, width = database.shape
    rows = database.shape[1] // racks
    panels, asked, user = fetch_call(neighbour_owner, neighbour_slot, database, peer_count, racks)
    asked_rows = asked[:, 0, :CAP].reshape(peer_count * CAP)
    selector = (asked_rows[:, None] == jnp.arange(local_rows, dtype=jnp.int32)[None, :]).astype(BF16)
    attended, grad_query, full_key, full_value, returned = block_call(
        user, panels, queries, cotangent, w_key, w_value, racks, peer_count
    )
    grad_w_key, grad_w_value = full_key.astype(F32), full_value.astype(F32)
    grad_database = pick(selector.T, returned.reshape(peer_count * CAP, rows, width))
    return attended, grad_query, grad_w_key, grad_w_value, grad_database


def solution(mesh):
    return jax.shard_map(
        local,
        mesh=mesh,
        in_specs=(
            P("db", "rack"), P("db", "rack"), P("db", None, None), P(None, "rack"), P(None, "rack"), P("db", None), P("db", None),
        ),
        out_specs=(P("db", "rack"), P("db", "rack"), P(None, "rack"), P(None, "rack"), P("db", "rack", None)),
        check_vma=False,
    )
```

```python
import functools

import jax
import jax.numpy as jnp
from jax import lax
from jax.experimental import pallas as pl
from jax.experimental.pallas import tpu as pltpu
from jax.sharding import PartitionSpec as P

HD = 128
SPAN = 64
CAP = 3
PARTS = 2
GPARTS = 1
NT = (((1,), (1,)), ((), ()))
TN = (((0,), (0,)), ((), ()))
F32 = jnp.float32
BF16 = jnp.bfloat16


def dot(a, b):
    return jnp.dot(a, b, preferred_element_type=F32)


MESH = pl.DeviceIdType.MESH


class Links:
    def __init__(self, side_z, side_y, side_x):
        db, rack = lax.axis_index("db"), lax.axis_index("rack")
        self.db, self.rack = db, rack
        self.z, self.y = db // side_y, db % side_y
        self.x, self.core = rack // 2, rack % 2
        self.side_x = side_x
        self.ids = {
            ("y", 1): (self.z * side_y + (self.y + 1) % side_y, rack),
            ("y", -1): (self.z * side_y + (self.y + side_y - 1) % side_y, rack),
            ("z", 1): ((self.z + 1) % side_z * side_y + self.y, rack),
            ("z", -1): ((self.z + side_z - 1) % side_z * side_y + self.y, rack),
            ("x", 1): (db, (self.x + 1) % side_x * 2 + self.core),
            ("x", -1): (db, (self.x + side_x - 1) % side_x * 2 + self.core),
            ("core", 1): (db, self.x * 2 + 1 - self.core),
        }

    def place(self, axis):
        return {"y": self.y, "z": self.z, "x": self.x}[axis]


class Mail:
    def __init__(self, send_sems, recv_sems):
        self.send_sems, self.recv_sems, self.book = send_sems, recv_sems, {}

    def plan(self, name, source, target, device):
        self.book[name] = (len(self.book), source, target, device)

    def copy(self, name):
        n, source, target, device = self.book[name]
        return pltpu.make_async_remote_copy(
            src_ref=source(), dst_ref=target(), send_sem=self.send_sems.at[n], recv_sem=self.recv_sems.at[n], device_id=device,
            device_id_type=MESH,
        )

    def start(self, *names):
        for name in names:
            self.copy(name).start()

    def arrive(self, *names):
        for name in names:
            self.copy(name).wait_recv()

    def settle(self):
        for name in self.book:
            self.copy(name).wait_send()


def greet(links, peers):
    barrier = pltpu.get_barrier_semaphore()
    others = [links.ids[("core", 1)], links.ids[("x", 1)], links.ids[("x", -1)]]
    for device in others:
        pl.semaphore_signal(barrier, inc=1, device_id=device, device_id_type=MESH)

    @pl.loop(1, peers)
    def _(far):
        pl.semaphore_signal(barrier, inc=1, device_id=((links.db + far) % peers, links.rack), device_id_type=MESH)

    return len(others) + peers - 1


def add(*terms):
    total = terms[0].astype(F32)
    for term in terms[1:]:
        total = total + term.astype(F32)
    return total.astype(BF16)


class Reduction:
    def __init__(self, tag, links, mail, part, full, first_column, columns, axes, near, far, middle):
        self.tag, self.links, self.mail = tag, links, mail
        self.part, self.full, self.first_column, self.columns = part, full, first_column, columns
        self.near, self.far, self.middle = near, far, middle
        self.rows = part.shape[0] // 4
        self.places = [links.place(axis) for axis in axes]
        self.across = columns // 128
        self.short = self.rows * self.across // 4
        self.sides = [(0, self.rows // 32 * 16), (self.rows // 32 * 16, self.rows - self.rows // 32 * 16)]
        whole = (self.short + 31) // 32 * 16
        self.bits = [(0, whole), (whole, self.short - whole)]
        up = [links.ids[(axis, 1)] for axis in axes]
        down = [links.ids[(axis, -1)] for axis in axes]
        one, two = self.places
        for level, at, buffer, sides, me, k in (("n", self.wide, near, self.sides, one, 0), ("f", self.small, far, self.bits, two, 1)):
            lot = lambda ref, slot, side, sides=sides: (lambda: ref.at[slot, pl.ds(0, sides[side][1])])
            spot = lambda far_off, side, at=at, me=me: (lambda: at((me + far_off) % 4, side))
            self.plan(level + "ra", spot(2, 0), lot(buffer, 0, 0), up[k])
            self.plan(level + "rb", spot(2, 1), lot(buffer, 1, 1), down[k])
            self.plan(level + "db", spot(1, 1), lot(buffer, 3, 1), up[k])
            self.plan(level + "da", spot(3, 0), lot(buffer, 2, 0), down[k])
            self.plan(level + "sa", lot(buffer, 0, 0), lot(buffer, 4, 0), up[k])
            self.plan(level + "sb", lot(buffer, 1, 1), lot(buffer, 5, 1), down[k])
        for level, at, sides, size, me, k in (("g", self.piece, self.bits, self.short, two, 1), ("h", self.band, self.sides, self.rows, one, 0)):
            spot = lambda far_off, first, size, at=at, me=me: (lambda: at((me + far_off) % 4, first, size))
            for name, far_off, (first, length), device in (
                ("up", 0, (0, size), up[k]), ("down", 0, (0, size), down[k]), ("on", 3, sides[0], up[k]), ("back", 1, sides[1], down[k]),
            ):
                self.plan(level + name, spot(far_off, first, length), spot(far_off, first, length), device)

    def plan(self, name, source, target, device):
        self.mail.plan((self.tag, name), source, target, device)

    def start(self, *names):
        self.mail.start(*[(self.tag, name) for name in names])

    def arrive(self, *names):
        self.mail.arrive(*[(self.tag, name) for name in names])

    def wide(self, one, side):
        first, size = self.sides[side]
        return self.part.at[pl.ds(pl.multiple_of(one * self.rows + first, 16), size), pl.ds(self.first_column, self.columns)]

    def small(self, two, side):
        first, size = self.bits[side]
        return self.middle.at[
            pl.ds(pl.multiple_of(two // self.across * self.short + first, 16), size),
            pl.ds(pl.multiple_of(two % self.across * 128, 128), 128),
        ]

    def piece(self, two, first, size):
        row = self.places[0] * self.rows + two // self.across * self.short + first
        column = self.first_column + two % self.across * 128
        return self.full.at[pl.ds(pl.multiple_of(row, 16), size), pl.ds(pl.multiple_of(column, 128), 128)]

    def band(self, one, first, size):
        return self.full.at[pl.ds(pl.multiple_of(one * self.rows + first, 16), size), pl.ds(self.first_column, self.columns)]

    def join(self, level, at, buffer, sides, me):
        for side, letter, far_off in ((0, "a", 1), (1, "b", 3)):
            size = sides[side][1]
            self.arrive(level + "r" + letter)
            buffer[side, :size] = add(buffer[side, :size], at((me + far_off) % 4, side)[...])
            self.start(level + "s" + letter)

    def total(self, level, at, buffer, sides, me, side):
        letter, size = "ab"[side], sides[side][1]
        self.arrive(level + "d" + letter, level + "s" + letter)
        return add(buffer[2 + side, :size], buffer[4 + side, :size], at(me, side)[...])

    def stage(self, number):
        one, two = self.places
        if number == 0:
            self.start("nra", "nrb", "ndb", "nda")
        elif number == 1:
            self.join("n", self.wide, self.near, self.sides, one)
        elif number == 2:
            for side, (first, size) in enumerate(self.sides):
                self.middle[first:first + size, :] = self.total("n", self.wide, self.near, self.sides, one, side)
            self.start("fra", "frb", "fdb", "fda")
        elif number == 3:
            self.join("f", self.small, self.far, self.bits, two)
        elif number == 4:
            for side, (first, size) in enumerate(self.bits):
                self.piece(two, first, size)[...] = self.total("f", self.small, self.far, self.bits, two, side)
            self.start("gup", "gdown")
        elif number == 6:
            self.arrive("gon", "gback")
            self.start("hup", "hdown")
        elif number == 8:
            self.arrive("hon", "hback")
        else:
            level = "g" if number == 5 else "h"
            self.arrive(level + "up")
            self.start(level + "on")
            self.arrive(level + "down")
            self.start(level + "back")


class Return:
    def __init__(self, tag, links, mail, use_grad, user, returned, crossed, ring, mine, leaving, leave_sems, land_sems):
        self.tag = tag
        self.links, self.mail, self.use_grad, self.user, self.returned = links, mail, use_grad, user, returned
        self.crossed, self.ring, self.mine, self.leaving = crossed, ring, mine, leaving
        self.leave_sems, self.land_sems = leave_sems, land_sems
        self.half = mine.shape[0] // 2
        up, down, across = links.ids[("x", 1)], links.ids[("x", -1)], links.ids[("core", 1)]
        for side in (0, 1):
            for far_off in (2, 1, 3, 0):
                mail.plan((tag, "c", far_off, side), self.partner(far_off, side), self.spot(far_off, side), across)
        slot = lambda n: (lambda: ring.at[n])
        mail.plan((tag, "xra"), self.spot(2, 0), slot(0), up)
        mail.plan((tag, "xda"), self.spot(3, 0), slot(2), down)
        mail.plan((tag, "xrb"), self.spot(2, 1), slot(1), down)
        mail.plan((tag, "xdb"), self.spot(1, 1), slot(3), up)
        mail.plan((tag, "xsa"), slot(0), slot(4), up)
        mail.plan((tag, "xsb"), slot(1), slot(5), down)

    def uses(self, side):
        return pl.ds(side * self.half, self.half)

    def spot(self, far_off, side):
        return lambda: self.crossed.at[(self.links.x + far_off) % 4, self.uses(side)]

    def partner(self, far_off, side):
        return lambda: self.use_grad.at[(self.links.x + far_off) % 4 * 2 + 1 - self.links.core, self.uses(side)]

    def cross(self):
        self.mail.start(*[(self.tag, "c", far_off, side) for far_off in (2, 1, 3, 0) for side in (0, 1)])

    def ring_out(self):
        links, mail, half = self.links, self.mail, self.half
        for far_off, names in ((2, ("xra", "xrb")), (1, (None, "xdb")), (3, ("xda", None)), (0, (None, None))):
            x = (links.x + far_off) % 4
            for side, name in enumerate(names):
                mail.arrive((self.tag, "c", far_off, side))

                @pl.loop(side * half, (side + 1) * half)
                def _(n):
                    self.crossed[x, n] = add(self.crossed[x, n], self.use_grad[x * 2 + links.core, n])

                if name:
                    mail.start((self.tag, name))

    def ring_on(self):
        for side in (0, 1):
            self.pass_on(side)

    def ring_end(self):
        for side in (0, 1):
            self.finish(side)

    def pass_on(self, side):
        letter, far_off = ("a", 1) if side == 0 else ("b", 3)
        self.mail.arrive((self.tag, "xr" + letter))
        own = self.spot(far_off, side)()

        @pl.loop(0, self.half)
        def _(n):
            self.ring[side, n] = add(self.ring[side, n], own[n])

        self.mail.start((self.tag, "xs" + letter))

    def finish(self, side):
        letter = "ab"[side]
        self.mail.arrive((self.tag, "xd" + letter), (self.tag, "xs" + letter))
        own = self.spot(0, side)()

        @pl.loop(0, self.half)
        def _(n):
            self.mine[side * self.half + n] = add(self.ring[2 + side, n], self.ring[4 + side, n], own[n])

    def post(self):
        links, peers = self.links, self.returned.shape[0]
        self.mine[2 * self.half] = jnp.zeros(self.mine.shape[1:], BF16)

        def fill(peer, target):
            for k in range(CAP):
                target[peer, k] = self.mine[self.user[peer, 0, k]]

        @pl.loop(1, peers)
        def _(far_off):
            fill((links.db + far_off) % peers, self.leaving)
            self.copy(far_off).start()

        fill(links.db, self.returned)

    def received(self):
        pl.loop(1, self.returned.shape[0])(lambda far_off: self.copy(far_off).wait())

    def copy(self, far_off):
        links = self.links
        peer = (links.db + far_off) % self.returned.shape[0]
        return pltpu.make_async_remote_copy(
            src_ref=self.leaving.at[peer], dst_ref=self.returned.at[links.db], send_sem=self.leave_sems.at[far_off],
            recv_sem=self.land_sems.at[far_off], device_id=(peer, links.rack), device_id_type=MESH,
        )


def block_step(step, spans, heads, panels, queries, cotangent, head_key, head_value, w_key, w_value, attended, grad_queries, part_key, part_value,
               use_grad, flipped, rows_kv, grads_kv, left, right, pair, stacked, wide):
    keys = panels.shape[0] // spans
    width = panels.shape[1]
    scale = HD ** -0.5

    @pl.when(step == 0)
    def _():
        left[...] = jnp.zeros_like(left)
        right[...] = jnp.zeros_like(right)
        for c in range(spans):
            flipped[:, c * keys:(c + 1) * keys] = panels[c * keys:(c + 1) * keys, :].T

    @pl.when(step < heads)
    def _():
        wide[:, :HD] = head_key[...]
        wide[:, HD:] = head_value[...]

        @pl.loop(0, PARTS)
        def _(n):
            size = panels.shape[0] // PARTS
            at = pl.ds(pl.multiple_of(n * size, size), size)
            rows_kv[at, :] = dot(panels[at, :], wide[...]).astype(BF16)

        for c in range(spans):
            tokens = slice(c * SPAN, (c + 1) * SPAN)
            query, grad = queries[tokens, :], cotangent[tokens, :]
            left[c, :SPAN, :HD] = query
            left[c, SPAN:, HD:] = grad
            right[c, :SPAN, HD:] = grad
            right[c, SPAN:, :HD] = query
        for c in range(spans):
            pair[c] = lax.dot_general(left[c], rows_kv[c * keys:(c + 1) * keys, :], NT, preferred_element_type=F32)
        for c in range(spans):
            scores = pair[c, :SPAN] * scale
            raised = jnp.exp(scores - jnp.max(scores, axis=-1, keepdims=True))
            probs = raised * (1.0 / jnp.sum(raised, axis=-1, keepdims=True))
            stacked[c, :SPAN] = probs.astype(BF16)
            grad_probs = pair[c, SPAN:]
            delta = jnp.sum(probs * grad_probs, axis=-1, keepdims=True)
            stacked[c, SPAN:] = (probs * (grad_probs - delta) * scale).astype(BF16)
        for c in range(spans):
            tokens = slice(c * SPAN, (c + 1) * SPAN)
            own = slice(c * keys, (c + 1) * keys)
            out = dot(stacked[c], rows_kv[own, :])
            attended[tokens, :] = out[:SPAN, HD:].astype(BF16)
            grad_queries[tokens, :] = out[SPAN:, :HD].astype(BF16)
        for c in range(spans):
            own = slice(c * keys, (c + 1) * keys)
            grads_kv[step, own, :] = lax.dot_general(stacked[c], right[c], TN, preferred_element_type=F32).astype(BF16)

        @pl.loop(0, GPARTS)
        def _(n):
            size = width // GPARTS
            share = part_key.shape[2] // HD
            pair_of, column_of = step // share, pl.ds(pl.multiple_of(step % share * HD, HD), HD)
            at = pl.ds(pl.multiple_of(n * size, size), size)
            total = dot(flipped[at, :], grads_kv[step]).astype(BF16)
            part_key[pair_of, at, column_of] = total[:, :HD]
            part_value[pair_of, at, column_of] = total[:, HD:]

    for part in range(len(CUTS) - 1):
        first, last = CUTS[part], CUTS[part + 1]

        @pl.when((step >= heads + part * QUARTERS) & (step < heads + (part + 1) * QUARTERS))
        def _():
            pieces, uses, rows = use_grad[part].shape[0], use_grad[part].shape[1] // QUARTERS, use_grad[part].shape[2]
            c = step - heads - part * QUARTERS
            size = panels.shape[0] // QUARTERS
            own = pl.ds(pl.multiple_of(c * size, size), size)
            total = jnp.zeros((size, last - first), F32)
            for h in range(heads):
                columns = slice(h * HD, (h + 1) * HD)
                weights = jnp.concatenate([w_key[first:last, columns], w_value[first:last, columns]], axis=1)
                total = total + lax.dot_general(grads_kv[h, own, :], weights, NT, preferred_element_type=F32)
            total = total.astype(BF16)
            for n in range(uses):
                for r in range(pieces):
                    at = (n * pieces + r) * rows
                    use_grad[part][r, c * uses + n, :, :] = total[at:at + rows, :]


QUARTERS = 2
CUTS = (0, 512, 896)
GROUPS = 4


def block_kernel(spans, heads, user, panels, queries, cotangent, head_key, head_value, all_key, all_value, attended, grad_queries,
                 out_key, out_value, out_returned, w_key, w_value, full_key, full_value, returned, flipped, rows_kv, grads_kv, left, right, pair, stacked, wide, part_key, part_value, use_grad, near, far,
                 middle, crossed, ring, mine, leaving, send_sems, recv_sems, leave_sems, land_sems, out_sems, weight_sems):
    step = pl.program_id(0)
    weights = [
        pltpu.make_async_copy(all_key, w_key, weight_sems.at[0]), pltpu.make_async_copy(all_value, w_value, weight_sems.at[1])
    ]
    links = Links(4, 4, 4)
    mail = Mail(send_sems, recv_sems)
    columns = part_key.shape[2]
    items = []
    for g in range(GROUPS):
        for m, (part, full, axes) in enumerate(((part_key, full_key, "yz"), (part_value, full_value, "zy"))):
            n = g * 2 + m
            items.append(Reduction(n, links, mail, part.at[g], full.at[g], 0, columns, axes, near.at[n], far.at[n], middle.at[n]))
    parts = range(len(CUTS) - 1)
    back = [
        Return("lr"[c], links, mail, use_grad[c], user, returned[c], crossed[c], ring[c], mine[c], leaving[c], leave_sems.at[c], land_sems.at[c])
        for c in parts
    ]

    def advance(*moves):
        for g, number in moves:
            items[2 * g].stage(number)
            items[2 * g + 1].stage(number)
            if number == 8:
                result(g, 0).start()
                result(g, 1).start()

    def result(g, m):
        source, target = ((full_key, out_key), (full_value, out_value))[m]
        return pltpu.make_async_copy(source.at[g], target.at[:, pl.ds(g * columns, columns)], out_sems.at[2 * g + m])

    @pl.when(step == 0)
    def _():
        greet(links, user.shape[0])

    @pl.when(step == 0)
    def _():
        for copy in weights:
            copy.start()

    @pl.when(step == heads)
    def _():
        for copy in weights:
            copy.wait()

    block_step(step, spans, heads, panels, queries, cotangent, head_key, head_value, w_key, w_value, attended, grad_queries, part_key, part_value,
               use_grad, flipped, rows_kv, grads_kv, left, right, pair, stacked, wide)

    for after in range(1, heads):
        moves = [(g, after - 2 * g - 1) for g in reversed(range(GROUPS)) if 0 <= after - 2 * g - 1 <= 8]

        @pl.when(step == after)
        def _():
            if after == 1:
                pl.semaphore_wait(pltpu.get_barrier_semaphore(), 3 + user.shape[0] - 1)
            advance(*moves)

    @pl.when(step == heads + QUARTERS - 1)
    def _():
        back[0].cross()
        advance((3, 1), (2, 3), (1, 5), (0, 7))

    @pl.when(step == heads + 2 * QUARTERS - 1)
    def _():
        back[1].cross()
        back[0].ring_out()
        advance((3, 2), (2, 4), (1, 6), (0, 8))
        advance((3, 3), (2, 5), (1, 7))
        back[0].ring_on()
        back[1].ring_out()
        advance((3, 4), (2, 6), (1, 8))
        advance((3, 5), (2, 7))
        back[0].ring_end()
        advance((3, 6), (2, 8))
        back[0].post()
        back[1].ring_on()
        advance((3, 7))
        back[1].ring_end()
        back[1].post()
        advance((3, 8))
        last = []
        for c in parts:
            back[c].received()
            target = out_returned.at[:, :, :, pl.ds(CUTS[c], CUTS[c + 1] - CUTS[c])]
            last.append(pltpu.make_async_copy(returned[c], target, out_sems.at[2 * GROUPS + c]))
            last[c].start()
        mail.settle()
        for g in range(GROUPS):
            result(g, 0).wait()
            result(g, 1).wait()
        for copy in last:
            copy.wait()


def block_call(user, panels, queries, cotangent, w_key, w_value, racks, peers):
    uses, panel_len, width = panels.shape
    spans = queries.shape[0] // SPAN
    features = w_key.shape[1]
    heads = features // HD
    rows = panel_len // racks
    total = uses * panel_len
    columns = features // GROUPS
    messages = 2 * GROUPS * 20 + 28
    cut = lambda *shape: [pltpu.VMEM(shape + (CUTS[c + 1] - CUTS[c],), BF16) for c in range(len(CUTS) - 1)]
    by_head = lambda size: pl.BlockSpec((size, HD), lambda i: (0, jnp.minimum(i, heads - 1)))
    whole = lambda a, b: pl.BlockSpec((a, b), lambda i: (0, 0), pipeline_mode=pl.Buffered(1))
    anywhere = pl.BlockSpec(memory_space=pl.ANY)
    return pl.pallas_call(
        functools.partial(block_kernel, spans, heads),
        grid=(heads + 2 * QUARTERS,),
        out_shape=(
            jax.ShapeDtypeStruct(queries.shape, BF16),
            jax.ShapeDtypeStruct(queries.shape, BF16),
            jax.ShapeDtypeStruct((width, features), BF16),
            jax.ShapeDtypeStruct((width, features), BF16),
            jax.ShapeDtypeStruct((peers, CAP, rows, width), BF16),
        ),
        in_specs=[
            pl.BlockSpec(memory_space=pltpu.SMEM), whole(total, width), by_head(queries.shape[0]), by_head(queries.shape[0]),
            by_head(width), by_head(width), anywhere, anywhere,
        ],
        out_specs=[by_head(queries.shape[0]), by_head(queries.shape[0]), anywhere, anywhere, anywhere],
        scratch_shapes=[
            pltpu.VMEM((width, features), BF16),
            pltpu.VMEM((width, features), BF16),
            pltpu.VMEM((GROUPS, width, columns), BF16),
            pltpu.VMEM((GROUPS, width, columns), BF16),
            cut(peers, CAP, rows),
            pltpu.VMEM((width, total), BF16),
            pltpu.VMEM((total, 2 * HD), BF16),
            pltpu.VMEM((heads, total, 2 * HD), BF16),
            pltpu.VMEM((spans, 2 * SPAN, 2 * HD), BF16),
            pltpu.VMEM((spans, 2 * SPAN, 2 * HD), BF16),
            pltpu.VMEM((spans, 2 * SPAN, total // spans), F32),
            pltpu.VMEM((spans, 2 * SPAN, total // spans), BF16),
            pltpu.VMEM((width, 2 * HD), BF16),
            pltpu.VMEM((GROUPS, width, columns), BF16),
            pltpu.VMEM((GROUPS, width, columns), BF16),
            cut(racks, uses, rows),
            pltpu.VMEM((2 * GROUPS, 6, width // 8, columns), BF16),
            pltpu.VMEM((2 * GROUPS, 6, 64, 128), BF16),
            pltpu.VMEM((2 * GROUPS, width // 4, columns), BF16),
            cut(4, uses, rows),
            cut(6, uses // 2, rows),
            cut(uses + 1, rows),
            cut(peers, CAP, rows),
            pltpu.SemaphoreType.DMA((messages,)),
            pltpu.SemaphoreType.DMA((messages,)),
            pltpu.SemaphoreType.DMA((len(CUTS) - 1, peers)),
            pltpu.SemaphoreType.DMA((len(CUTS) - 1, peers)),
            pltpu.SemaphoreType.DMA((2 * GROUPS + 2,)),
            pltpu.SemaphoreType.DMA((2,)),
        ],
        compiler_params=pltpu.CompilerParams(
            collective_id=1, has_side_effects=True, vmem_limit_bytes=58 * 1024 * 1024
        ),
        name="block",
    )(user, panels.reshape(total, width), queries, cotangent, w_key, w_value, w_key, w_value)


def fetch_kernel(cuts, named_rows, database, panels, asked, user, stored, wanted, heard, leaving, landing, mine, load_sem, ask_send,
                 ask_recv, leave_sems, land_sems, own_sems, send_sems, recv_sems):
    links = Links(4, 4, 4)
    peers = asked.shape[0]
    local_rows, _, width = stored.shape
    uses, rows = mine.shape[0], mine.shape[1]
    nbrs = named_rows.shape[1] // 2
    my_rows = lambda x, core: pl.ds(pl.multiple_of((x * 2 + core) * rows, rows), rows)
    load = pltpu.make_async_copy(database.at[:, my_rows(links.x, links.core), :], stored, load_sem.at[0])
    load.start()
    signals = greet(links, peers)
    pl.semaphore_wait(pltpu.get_barrier_semaphore(), signals)

    peer_of = lax.broadcasted_iota(jnp.int32, (peers, 1, 128), 0)
    lane = lax.broadcasted_iota(jnp.int32, (peers, 1, 128), 2)
    seen = jnp.zeros((peers, 1, 128), jnp.int32)
    rows_wanted = jnp.full((peers, 1, 128), local_rows, jnp.int32)
    users = jnp.full((peers, 1, 128), uses, jnp.int32)
    for u in range(uses):
        named = peer_of == named_rows[u // nbrs, u % nbrs]
        here = named & (lane == seen)
        rows_wanted = jnp.where(here, named_rows[u // nbrs, nbrs + u % nbrs], rows_wanted)
        users = jnp.where(here, u, users)
        seen = seen + named.astype(jnp.int32)
    wanted[...] = rows_wanted
    user[...] = users

    def ask(far):
        peer = (links.db + far) % peers
        return pltpu.make_async_remote_copy(
            src_ref=wanted.at[peer], dst_ref=asked.at[links.db], send_sem=ask_send.at[far], recv_sem=ask_recv.at[far],
            device_id=(peer, links.rack), device_id_type=MESH,
        )

    pl.loop(1, peers)(lambda far: ask(far).start())
    asked[links.db] = wanted[links.db]
    load.wait()
    pl.loop(1, peers)(lambda far: ask(far).wait())
    tables = pltpu.make_async_copy(asked, heard, load_sem.at[1])
    tables.start()
    tables.wait()

    def answer(c, far):
        peer = (links.db + far) % peers
        return pltpu.make_async_remote_copy(
            src_ref=leaving[c].at[peer], dst_ref=landing[c].at[links.db], send_sem=leave_sems.at[c, far],
            recv_sem=land_sems.at[c, far], device_id=(peer, links.rack), device_id_type=MESH,
        )

    def fill(c, peer, target):
        for k in range(CAP):
            row = jnp.minimum(heard[peer, 0, k], local_rows - 1)
            target[peer, k] = stored[row, :, cuts[c]:cuts[c + 1]]

    for c in range(len(cuts) - 1):
        @pl.loop(1, peers)
        def _(far):
            fill(c, (links.db + far) % peers, leaving[c])
            answer(c, far).start()

        fill(c, links.db, landing[c])

    mail = Mail(send_sems, recv_sems)
    up, down, across = links.ids[("x", 1)], links.ids[("x", -1)], links.ids[("core", 1)]
    own_copies = []
    half = uses // 2

    def out(c, far, first, size):
        return panels.at[pl.ds(first, size), my_rows((links.x + far) % 4, links.core), pl.ds(cuts[c], cuts[c + 1] - cuts[c])]

    def pass_on(name, c, far, first, size, device):
        spot = lambda: out(c, far, first, size)
        mail.plan((name, c), spot, spot, device)
        mail.start((name, c))

    def exchange(c):
        mail.arrive(("up", c))
        pass_on("on", c, 3, 0, half, up)
        pass_on("cross3", c, 3, 0, uses, across)
        mail.arrive(("down", c))
        pass_on("back", c, 1, half, half, down)
        pass_on("cross1", c, 1, 0, uses, across)

    def finish(c):
        mail.arrive(("on", c))
        pass_on("cross2a", c, 2, 0, half, across)
        mail.arrive(("back", c))
        pass_on("cross2b", c, 2, half, half, across)

    count = len(cuts) - 1
    for c in range(count):
        pl.loop(1, peers)(lambda far: answer(c, far).wait())
        for u in range(uses):
            owner = named_rows[u // nbrs, u % nbrs]
            rank = jnp.int32(0)
            for v in range(u):
                rank = rank + (named_rows[v // nbrs, v % nbrs] == owner).astype(jnp.int32)
            mine[u, :, cuts[c]:cuts[c + 1]] = landing[c][owner, jnp.minimum(rank, CAP - 1)]
        source = mine.at[:, :, pl.ds(cuts[c], cuts[c + 1] - cuts[c])]
        target = out(c, 0, 0, uses)
        for name, device in (("up", up), ("down", down), ("cross0", across)):
            mail.plan((name, c), lambda source=source: source, lambda target=target: target, device)
            mail.start((name, c))
        copy = pltpu.make_async_copy(source, target, own_sems.at[c])
        copy.start()
        own_copies.append(copy)
        if c > 0:
            exchange(c - 1)
    exchange(count - 1)
    for c in range(count):
        finish(c)
    for c in range(count):
        mail.arrive(("cross0", c), ("cross1", c), ("cross3", c), ("cross2a", c), ("cross2b", c))
    for copy in own_copies:
        copy.wait()
    mail.settle()


def fetch_call(owners, slots, database, peers, racks):
    uses = owners.shape[0] * owners.shape[1]
    local_rows, panel_len, width = database.shape
    rows = panel_len // racks
    parts = len(CUTS) - 1
    chunk = lambda c: pltpu.VMEM((peers, CAP, rows, CUTS[c + 1] - CUTS[c]), BF16)
    vmem = pl.BlockSpec(memory_space=pltpu.VMEM)
    smem = pl.BlockSpec(memory_space=pltpu.SMEM)
    anywhere = pl.BlockSpec(memory_space=pl.ANY)
    sems = pltpu.SemaphoreType.DMA
    return pl.pallas_call(
        functools.partial(fetch_kernel, CUTS),
        out_shape=(
            jax.ShapeDtypeStruct((uses, panel_len, width), BF16),
            jax.ShapeDtypeStruct((peers, 1, 128), jnp.int32),
            jax.ShapeDtypeStruct((peers, 1, 128), jnp.int32),
        ),
        in_specs=[smem, pl.BlockSpec(memory_space=pltpu.HBM)],
        out_specs=(anywhere, vmem, vmem),
        scratch_shapes=[
            pltpu.VMEM((local_rows, rows, width), BF16),
            pltpu.VMEM((peers, 1, 128), jnp.int32),
            pltpu.SMEM((peers, 1, 128), jnp.int32),
            [chunk(c) for c in range(parts)],
            [chunk(c) for c in range(parts)],
            pltpu.VMEM((uses, rows, width), BF16),
            sems((2,)), sems((peers,)), sems((peers,)), sems((parts, peers)), sems((parts, peers)), sems((parts,)),
            sems((9 * parts,)), sems((9 * parts,)),
        ],
        compiler_params=pltpu.CompilerParams(
            collective_id=0, has_side_effects=True, vmem_limit_bytes=58 * 1024 * 1024
        ),
        name="fetch",
    )(jnp.concatenate([owners, slots], axis=1), database)


def pick(selector, source):
    return jnp.einsum("ns,spw->npw", selector, source, preferred_element_type=F32).astype(BF16)


def local(queries, cotangent, database, w_key, w_value, neighbour_owner, neighbour_slot):
    peer_count = lax.axis_size("db")
    racks = lax.axis_size("rack")
    local_rows, _, width = database.shape
    rows = database.shape[1] // racks
    panels, asked, user = fetch_call(neighbour_owner, neighbour_slot, database, peer_count, racks)
    asked_rows = asked[:, 0, :CAP].reshape(peer_count * CAP)
    selector = (asked_rows[:, None] == jnp.arange(local_rows, dtype=jnp.int32)[None, :]).astype(BF16)
    attended, grad_query, full_key, full_value, returned = block_call(
        user, panels, queries, cotangent, w_key, w_value, racks, peer_count
    )
    grad_w_key, grad_w_value = full_key.astype(F32), full_value.astype(F32)
    grad_database = pick(selector.T, returned.reshape(peer_count * CAP, rows, width))
    return attended, grad_query, grad_w_key, grad_w_value, grad_database


def solution(mesh):
    return jax.shard_map(
        local,
        mesh=mesh,
        in_specs=(
            P("db", "rack"), P("db", "rack"), P("db", None, None), P(None, "rack"), P(None, "rack"), P("db", None), P("db", None),
        ),
        out_specs=(P("db", "rack"), P("db", "rack"), P(None, "rack"), P(None, "rack"), P("db", "rack", None)),
        check_vma=False,
    )
```
